768 devices in a mesh: seq: 96 (over z, y), head: 8 (over x, core).
Axes of the slice: x: 4, y: 8, z: 12, core: 2. Of those that a mesh axis runs over, the one named last changes fastest.
Arguments:
- queries: bfloat16 [12288, 8192], P('seq', 'head'), may hold values from -6 to 6
- key_rows: bfloat16 [12288, 8192], P('seq', 'head'), may hold values from -6 to 6
- value_rows: bfloat16 [12288, 8192], P('seq', 'head'), may hold values from -64 to 64
- out_grad: bfloat16 [12288, 8192], P('seq', 'head'), may hold values from -6 to 6
- norm_gain: float32 [8192], P('head'), may hold values from 0.1 to 1.9
- dial_start: int32 [12288], P('seq'), may hold values from 0 to 12287, as said below
- dial_end: int32 [12288], P('seq'), may hold values from 1 to 12288
Outputs:
- normed: bfloat16 [12288, 8192], P('seq', 'head')
- query_grad: bfloat16 [12288, 8192], P('seq', 'head')
- key_grad: bfloat16 [12288, 8192], P('seq', 'head')
- value_grad: bfloat16 [12288, 8192], P('seq', 'head')
The draws below stay inside these ranges and needn't reach their ends.
Inputs may be any that keep to these rules, and one draw needn't show every extreme that they name: Tokens of one dialogue are consecutive: dial_start gives the first token of a token's dialogue and dial_end one past its last; every dialogue holds 1 to 512 tokens and one holds exactly 512; the last token forms a dialogue of its own.
All inputs are finite; a program needn't handle non-finite values.
Results may differ from the reference program's by a relative error of at most 0.007.
Values sent between devices are 32-bit elements; how exact they have to be, the bound alone decides.
A program may use at most 128 MiB of HBM per device.

```python
import jax
import jax.numpy as jnp
from jax import lax

HEADS = 64
HD = 128
TOK_DEV = 128
MAXLEN = 512
TOKENS = 12288
N_SEQ = 96


def dialogue_bounds(key):
    inner_key = jax.random.fold_in(key, 11)
    key_len, key_pos = jax.random.split(inner_key, 2)
    longest = MAXLEN
    drawn_len = jax.random.randint(key_len, (TOKENS,), 1, longest + 1, dtype=jnp.int32)
    forced = jax.random.randint(key_pos, (), 0, 2, dtype=jnp.int32)
    lengths = jnp.where(jnp.arange(TOKENS, dtype=jnp.int32) == forced, longest, drawn_len).astype(jnp.int32)
    finishes = jnp.cumsum(lengths).astype(jnp.int32)
    beginnings = (finishes - lengths).astype(jnp.int32)
    position = jnp.arange(TOKENS, dtype=jnp.int32)
    owner = jnp.searchsorted(finishes, position, side='right').astype(jnp.int32)
    start_of = beginnings[owner].astype(jnp.int32)
    finish_of = jnp.minimum(finishes[owner], TOKENS - 1).astype(jnp.int32)
    is_last = position == TOKENS - 1
    start_of = jnp.where(is_last, TOKENS - 1, start_of).astype(jnp.int32)
    finish_of = jnp.where(is_last, TOKENS, finish_of).astype(jnp.int32)
    return (start_of, finish_of)


def draw_dial_start(key, part):
    return dialogue_bounds(key)[0]


def draw_dial_end(key, part):
    return dialogue_bounds(key)[1]


def draw_value_rows(key, part):
    head_pos = jnp.arange(HEADS, dtype=jnp.float32) / max(HEADS - 1, 1)
    key_a, key_b = jax.random.split(key, 2)
    jitter = jax.random.uniform(key_b, (HEADS,), jnp.float32, -0.1, 0.1)
    spread = 10.0 ** (head_pos + jitter)
    entries = jax.random.normal(key_a, (TOKENS, HEADS, HD), jnp.float32)
    result = entries * spread[None, :, None]
    return jnp.clip(result, -64.0, 64.0).reshape(TOKENS, HEADS * HD).astype(jnp.bfloat16)


def shard_levels(stream_key, extent, cuts, least, top_value):
    def one(dim, blocks):
        steps = jax.random.uniform(jax.random.fold_in(jax.random.fold_in(stream_key, 6), dim), (blocks,), jnp.float32, least / len(cuts), top_value / len(cuts))
        return jnp.repeat(jnp.exp(steps), extent[dim] // blocks).reshape((-1,) + (1,) * (len(extent) - dim - 1))

    factor_of = one(*cuts[0])
    for cut in cuts[1:]:
        factor_of = factor_of * one(*cut)
    return factor_of


def noise(rng, shape, deviation, reach, cuts=(), kind=jnp.bfloat16):
    values = deviation * jax.random.normal(rng, shape, jnp.float32)
    if cuts:
        values = values * shard_levels(rng, shape, cuts, -0.22, 0.18)
    return jnp.clip(values, -reach, reach).astype(kind)


def setup_inputs(seed: int = 0) -> dict:
    key_of = jax.random.split(jax.random.key(seed), 8)
    queries = noise(key_of[0], (TOKENS, HEADS * HD), 1.0, 6.0, ((0, 96), (1, 8)))
    key_rows = noise(key_of[1], (TOKENS, HEADS * HD), 1.0, 6.0, ((0, 96), (1, 8)))
    value_rows = draw_value_rows(jax.random.fold_in(key_of[7], 71), 0)
    out_grad = noise(key_of[3], (TOKENS, HEADS * HD), 1.0, 6.0, ((0, 96), (1, 8)))
    norm_gain = jnp.clip(1.0 + 0.18 * jax.random.normal(key_of[4], (HEADS * HD,), jnp.float32), 0.1, 1.9)
    dial_start = draw_dial_start(jax.random.fold_in(key_of[7], 71), 0)
    dial_end = draw_dial_end(jax.random.fold_in(key_of[7], 71), 0)
    return dict(queries=queries, key_rows=key_rows, value_rows=value_rows, out_grad=out_grad, norm_gain=norm_gain, dial_start=dial_start, dial_end=dial_end)


EPSILON = 1e-06
PRECISE = lax.Precision.HIGHEST

def widen(array_in):
    return array_in.astype(jnp.float32)

def reference(queries, key_rows, value_rows, out_grad, norm_gain, dial_start, dial_end):
    score_scale = HD ** (-0.5)
    width_all = HEADS * HD
    block_count = N_SEQ
    shape_heads = (block_count, TOK_DEV, HEADS, HD)
    query_blk = queries.reshape(shape_heads)
    key_blk = key_rows.reshape(shape_heads)
    value_blk = value_rows.reshape(shape_heads)
    grad_blk = out_grad.reshape(block_count, TOK_DEV, width_all)
    start_blk = dial_start.reshape(block_count, TOK_DEV)
    end_blk = dial_end.reshape(block_count, TOK_DEV)
    begin_blk = jnp.arange(block_count, dtype=jnp.int32) * TOK_DEV
    local_pos = jnp.arange(TOK_DEV, dtype=jnp.int32)

    def block_weights(query_wide, key_wide, start_b, block_begin):
        position = block_begin + local_pos
        inside = (position[None, :] >= start_b[:, None]) & (local_pos[None, :] <= local_pos[:, None])
        scores = jnp.einsum('thd,shd->hts', query_wide, key_wide, precision=PRECISE)
        weights = jnp.where(inside[None], score_scale * scores, 0.0).astype(jnp.bfloat16)
        return (inside, widen(lax.optimization_barrier(weights)))

    def forward_step(carried, stacked):
        query_b, key_b, value_b, grad_b, start_b, block_begin = stacked
        position = block_begin + local_pos
        query_wide = widen(query_b)
        key_wide = widen(key_b)
        value_wide = widen(value_b)
        inside, weights_wide = block_weights(query_wide, key_wide, start_b, block_begin)
        local_mix = jnp.einsum('hts,she->the', weights_wide, value_wide, precision=PRECISE)
        across = score_scale * jnp.einsum('thd,hde->the', query_wide, carried, precision=PRECISE)
        from_before = (start_b < block_begin).astype(jnp.float32)
        attended = (local_mix + from_before[:, None, None] * across).reshape(TOK_DEV, width_all)
        grad_wide = widen(grad_b)
        square_sum = lax.optimization_barrier(jnp.sum(attended * attended, axis=1))
        cross_sum = lax.optimization_barrier(jnp.sum(norm_gain * grad_wide * attended, axis=1))
        inv_rms = lax.rsqrt(square_sum / width_all + EPSILON)
        normed_b = (attended * inv_rms[:, None] * norm_gain).astype(jnp.bfloat16)
        grad_attn = inv_rms[:, None] * norm_gain * grad_wide - attended * (inv_rms * inv_rms * inv_rms * cross_sum / width_all)[:, None]
        grad_weight = grad_attn.astype(jnp.bfloat16).reshape(TOK_DEV, HEADS, HD)
        last_start = start_b[TOK_DEV - 1]
        keep_rows = (position >= last_start).astype(jnp.float32)
        element = jnp.einsum('shd,she->hde', key_wide * keep_rows[:, None, None], value_wide, precision=PRECISE)
        reset_flag = (last_start >= block_begin).astype(jnp.float32)
        return (element + (1.0 - reset_flag) * carried, (normed_b, grad_weight, carried))
    carry_zero = jnp.zeros((HEADS, HD, HD), jnp.float32)
    unused, (normed_all, grad_all, carried_all) = lax.scan(forward_step, carry_zero, (query_blk, key_blk, value_blk, grad_blk, start_blk, begin_blk))

    def backward_step(returned, stacked):
        query_b, key_b, value_b, grad_weight, carried, start_b, end_b, block_begin = stacked
        position = block_begin + local_pos
        query_wide = widen(query_b)
        key_wide = widen(key_b)
        value_wide = widen(value_b)
        inside, weights_wide = block_weights(query_wide, key_wide, start_b, block_begin)
        grad_wide = widen(grad_weight)
        grad_scores = jnp.einsum('the,she->hts', grad_wide, value_wide, precision=PRECISE)
        grad_mix = jnp.where(inside[None], score_scale * grad_scores, 0.0).astype(jnp.bfloat16)
        mix_wide = widen(lax.optimization_barrier(grad_mix))
        from_before = (start_b < block_begin).astype(jnp.float32)[:, None, None]
        to_after = (end_b > block_begin + TOK_DEV).astype(jnp.float32)[:, None, None]
        query_grad = jnp.einsum('hts,shd->thd', mix_wide, key_wide, precision=PRECISE) + from_before * score_scale * jnp.einsum('the,hde->thd', grad_wide, carried, precision=PRECISE)
        key_grad = jnp.einsum('hts,thd->shd', mix_wide, query_wide, precision=PRECISE) + to_after * score_scale * jnp.einsum('she,hde->shd', value_wide, returned, precision=PRECISE)
        value_grad = jnp.einsum('hts,the->she', weights_wide, grad_wide, precision=PRECISE) + to_after * score_scale * jnp.einsum('shd,hde->she', key_wide, returned, precision=PRECISE)
        first_end = end_b[0]
        keep_rows = (position < first_end).astype(jnp.float32)
        element = jnp.einsum('thd,the->hde', query_wide * keep_rows[:, None, None], grad_wide, precision=PRECISE)
        reset_flag = (first_end <= block_begin + TOK_DEV).astype(jnp.float32)
        outputs = (query_grad.reshape(TOK_DEV, width_all).astype(jnp.bfloat16), key_grad.reshape(TOK_DEV, width_all).astype(jnp.bfloat16), value_grad.reshape(TOK_DEV, width_all).astype(jnp.bfloat16))
        return (element + (1.0 - reset_flag) * returned, outputs)
    unused_back, (query_all, key_all, value_all) = lax.scan(backward_step, carry_zero, (query_blk, key_blk, value_blk, grad_all, carried_all, start_blk, end_blk, begin_blk), reverse=True)
    total = block_count * TOK_DEV
    return (normed_all.reshape(total, width_all), query_all.reshape(total, width_all), key_all.reshape(total, width_all), value_all.reshape(total, width_all))
```

```python
import jax
import jax.numpy as jnp
from jax import lax
from jax.sharding import PartitionSpec as P

HEADS = 64
HD = 128
SPAN = 4


EPSILON = 1e-06


def from_behind(x, axis, by):
    count = lax.axis_size(axis)
    pairs = [(i, i + by) for i in range(count) if 0 <= i + by < count]
    return lax.ppermute(x, axis, pairs)


def scan_window(element, reach, step):
    nearest = from_behind(element, "seq", step)
    second = from_behind(nearest, "seq", step)
    pair = nearest + (reach >= 2).astype(jnp.float32) * second
    far_pair = from_behind(pair, "seq", 2 * step)
    total = pair + (reach >= 3).astype(jnp.float32) * far_pair
    return (reach >= 1).astype(jnp.float32) * total


def join_states(earlier_part, later_part):
    return (
        later_part[0] + (1.0 - later_part[1]) * earlier_part[0],
        jnp.maximum(earlier_part[1], later_part[1]),
    )


def split_state(state):
    upper = state.astype(jnp.bfloat16)
    lower = (state - upper.astype(jnp.float32)).astype(jnp.bfloat16)
    return (upper, lower)


def state_product(form, rows, state):
    upper, lower = split_state(state)
    first = jnp.einsum(form, rows, upper, preferred_element_type=jnp.float32)
    return first + jnp.einsum(form, rows, lower, preferred_element_type=jnp.float32)


def shards(queries, key_rows, value_rows, out_grad, norm_gain, dial_start, dial_end):
    token_count = queries.shape[0]
    head_count = queries.shape[1] // HD
    score_scale = HD ** (-0.5)
    width_all = HEADS * HD
    block_begin = lax.axis_index("seq") * token_count
    local_pos = jnp.arange(token_count, dtype=jnp.int32)
    position = block_begin + local_pos
    query_h = queries.reshape(token_count, head_count, HD)
    key_h = key_rows.reshape(token_count, head_count, HD)
    value_h = value_rows.reshape(token_count, head_count, HD)
    last_start = dial_start[token_count - 1]
    keep_last = position >= last_start
    element = jnp.einsum(
        "shd,she->hde",
        jnp.where(keep_last[:, None, None], key_h, jnp.zeros((), jnp.bfloat16)),
        value_h,
        preferred_element_type=jnp.float32,
    )
    block_index = lax.axis_index("seq")
    reach_back = block_index - dial_start[0] // token_count
    carried = scan_window(element, reach_back, 1)
    inside = (position[None, :] >= dial_start[:, None]) & (local_pos[None, :] <= local_pos[:, None])
    scores = jnp.einsum("thd,shd->hts", query_h, key_h, preferred_element_type=jnp.float32)
    weights = jnp.where(inside[None], score_scale * scores, 0.0).astype(jnp.bfloat16)
    local_mix = jnp.einsum("hts,she->the", weights, value_h, preferred_element_type=jnp.float32)
    across = score_scale * state_product("thd,hde->the", query_h, carried)
    from_before = (dial_start < block_begin).astype(jnp.float32)[:, None, None]
    attended = (local_mix + from_before * across).reshape(token_count, head_count * HD)
    grad_wide = out_grad.astype(jnp.float32)
    square_sum, cross_sum = lax.psum(
        (jnp.sum(attended * attended, axis=1), jnp.sum(norm_gain * grad_wide * attended, axis=1)),
        "head",
    )
    inv_rms = lax.rsqrt(square_sum / width_all + EPSILON)
    normed = (attended * inv_rms[:, None] * norm_gain).astype(jnp.bfloat16)
    grad_attn = (
        inv_rms[:, None] * norm_gain * grad_wide
        - attended * (inv_rms * inv_rms * inv_rms * cross_sum / width_all)[:, None]
    )
    grad_weight = grad_attn.astype(jnp.bfloat16).reshape(token_count, head_count, HD)
    first_end = dial_end[0]
    keep_first = position < first_end
    back_element = jnp.einsum(
        "thd,the->hde",
        jnp.where(keep_first[:, None, None], query_h, jnp.zeros((), jnp.bfloat16)),
        grad_weight,
        preferred_element_type=jnp.float32,
    )
    reach_ahead = (dial_end[token_count - 1] + token_count - 1) // token_count - 1 - block_index
    returned = scan_window(back_element, reach_ahead, -1)
    grad_scores = jnp.einsum(
        "the,she->hts", grad_weight, value_h, preferred_element_type=jnp.float32
    )
    grad_mix = jnp.where(inside[None], score_scale * grad_scores, 0.0).astype(jnp.bfloat16)
    to_after = (dial_end > block_begin + token_count).astype(jnp.float32)[:, None, None]
    query_grad = jnp.einsum(
        "hts,shd->thd", grad_mix, key_h, preferred_element_type=jnp.float32
    ) + from_before * score_scale * state_product("the,hde->thd", grad_weight, carried)
    key_grad = jnp.einsum(
        "hts,thd->shd", grad_mix, query_h, preferred_element_type=jnp.float32
    ) + to_after * score_scale * state_product("she,hde->shd", value_h, returned)
    value_grad = jnp.einsum(
        "hts,the->she", weights, grad_weight, preferred_element_type=jnp.float32
    ) + to_after * score_scale * state_product("shd,hde->she", key_h, returned)
    flat_shape = (token_count, head_count * HD)
    return (
        normed,
        query_grad.reshape(flat_shape).astype(jnp.bfloat16),
        key_grad.reshape(flat_shape).astype(jnp.bfloat16),
        value_grad.reshape(flat_shape).astype(jnp.bfloat16),
    )


def solution(mesh):
    placed = (
        P("seq", "head"),
        P("seq", "head"),
        P("seq", "head"),
        P("seq", "head"),
        P("head"),
        P("seq"),
        P("seq"),
    )
    return jax.shard_map(
        shards,
        mesh=mesh,
        in_specs=placed,
        out_specs=(P("seq", "head"), P("seq", "head"), P("seq", "head"), P("seq", "head")),
        check_vma=False,
    )
```

```python
import functools

import jax
import jax.numpy as jnp
from jax import lax
from jax.experimental import pallas as pl
from jax.experimental.pallas import tpu as pltpu
from jax.sharding import PartitionSpec as P

HEADS = 64
HD = 128
SPAN = 4


EPSILON = 1e-06


def from_behind(x, axis, by):
    count = lax.axis_size(axis)
    pairs = [(i, i + by) for i in range(count) if 0 <= i + by < count]
    return lax.ppermute(x, axis, pairs)


def window_kernel(count, step, masks_ref, element_ref, out_ref, slots, send_sems, recv_sems):
    me = lax.axis_index("seq")
    head = lax.axis_index("head")

    def inside_axis(offset):
        return (me + offset >= 0) & (me + offset < count)

    def peer(offset):
        return (me + offset, head)

    barrier = pltpu.get_barrier_semaphore()
    offsets = (step, 2 * step, -step, -2 * step)
    for offset in offsets:
        ring_peer = (lax.rem(me + offset + count, count), head)
        pl.semaphore_signal(barrier, inc=1, device_id=ring_peer, device_id_type=pl.DeviceIdType.MESH)
    pl.semaphore_wait(barrier, len(offsets))

    def transfer(round_index, source, landing, distance):
        copy = pltpu.make_async_remote_copy(
            src_ref=source,
            dst_ref=slots.at[landing],
            send_sem=send_sems.at[round_index],
            recv_sem=recv_sems.at[round_index],
            device_id=peer(distance),
            device_id_type=pl.DeviceIdType.MESH,
        )

        @pl.when(inside_axis(distance))
        def _():
            copy.start()

        @pl.when(inside_axis(-distance))
        def _():
            copy.wait_recv()

        @pl.when(jnp.logical_not(inside_axis(-distance)))
        def _():
            slots[landing] = jnp.zeros(slots.shape[1:], jnp.float32)

        return copy

    def finish(copy, distance):
        @pl.when(inside_axis(distance))
        def _():
            copy.wait_send()

    first = transfer(0, element_ref, 0, step)
    second = transfer(1, slots.at[0], 1, step)
    slots[2] = slots[0] + masks_ref[1] * slots[1]
    third = transfer(2, slots.at[2], 3, 2 * step)
    out_ref[...] = masks_ref[0] * (slots[2] + masks_ref[2] * slots[3])
    finish(first, step)
    finish(second, step)
    finish(third, 2 * step)


def scan_window(element, reach, step, ident):
    count = lax.axis_size("seq")
    masks = jnp.stack([reach >= 1, reach >= 2, reach >= 3]).astype(jnp.float32)
    return pl.pallas_call(
        functools.partial(window_kernel, count, step),
        out_shape=jax.ShapeDtypeStruct(element.shape, jnp.float32),
        in_specs=[pl.BlockSpec(memory_space=pltpu.SMEM), pl.BlockSpec(memory_space=pltpu.VMEM)],
        out_specs=pl.BlockSpec(memory_space=pltpu.VMEM),
        scratch_shapes=[
            pltpu.VMEM((4,) + element.shape, jnp.float32),
            pltpu.SemaphoreType.DMA((3,)),
            pltpu.SemaphoreType.DMA((3,)),
        ],
        compiler_params=pltpu.CompilerParams(collective_id=ident, has_side_effects=True),
    )(masks, element)


def join_states(earlier_part, later_part):
    return (
        later_part[0] + (1.0 - later_part[1]) * earlier_part[0],
        jnp.maximum(earlier_part[1], later_part[1]),
    )


def split_state(state):
    upper = state.astype(jnp.bfloat16)
    lower = (state - upper.astype(jnp.float32)).astype(jnp.bfloat16)
    return (upper, lower)


def state_product(form, rows, state):
    upper, lower = split_state(state)
    first = jnp.einsum(form, rows, upper, preferred_element_type=jnp.float32)
    return first + jnp.einsum(form, rows, lower, preferred_element_type=jnp.float32)


def shards(queries, key_rows, value_rows, out_grad, norm_gain, dial_start, dial_end):
    token_count = queries.shape[0]
    head_count = queries.shape[1] // HD
    score_scale = HD ** (-0.5)
    width_all = HEADS * HD
    block_begin = lax.axis_index("seq") * token_count
    local_pos = jnp.arange(token_count, dtype=jnp.int32)
    position = block_begin + local_pos
    query_h = queries.reshape(token_count, head_count, HD)
    key_h = key_rows.reshape(token_count, head_count, HD)
    value_h = value_rows.reshape(token_count, head_count, HD)
    last_start = dial_start[token_count - 1]
    keep_last = position >= last_start
    element = jnp.einsum(
        "shd,she->hde",
        jnp.where(keep_last[:, None, None], key_h, jnp.zeros((), jnp.bfloat16)),
        value_h,
        preferred_element_type=jnp.float32,
    )
    block_index = lax.axis_index("seq")
    reach_back = block_index - dial_start[0] // token_count
    carried = scan_window(element, reach_back, 1, 0)
    inside = (position[None, :] >= dial_start[:, None]) & (local_pos[None, :] <= local_pos[:, None])
    scores = jnp.einsum("thd,shd->hts", query_h, key_h, preferred_element_type=jnp.float32)
    weights = jnp.where(inside[None], score_scale * scores, 0.0).astype(jnp.bfloat16)
    local_mix = jnp.einsum("hts,she->the", weights, value_h, preferred_element_type=jnp.float32)
    across = score_scale * state_product("thd,hde->the", query_h, carried)
    from_before = (dial_start < block_begin).astype(jnp.float32)[:, None, None]
    attended = (local_mix + from_before * across).reshape(token_count, head_count * HD)
    grad_wide = out_grad.astype(jnp.float32)
    square_sum, cross_sum = lax.psum(
        (jnp.sum(attended * attended, axis=1), jnp.sum(norm_gain * grad_wide * attended, axis=1)),
        "head",
    )
    inv_rms = lax.rsqrt(square_sum / width_all + EPSILON)
    normed = (attended * inv_rms[:, None] * norm_gain).astype(jnp.bfloat16)
    grad_attn = (
        inv_rms[:, None] * norm_gain * grad_wide
        - attended * (inv_rms * inv_rms * inv_rms * cross_sum / width_all)[:, None]
    )
    grad_weight = grad_attn.astype(jnp.bfloat16).reshape(token_count, head_count, HD)
    first_end = dial_end[0]
    keep_first = position < first_end
    back_element = jnp.einsum(
        "thd,the->hde",
        jnp.where(keep_first[:, None, None], query_h, jnp.zeros((), jnp.bfloat16)),
        grad_weight,
        preferred_element_type=jnp.float32,
    )
    reach_ahead = (dial_end[token_count - 1] + token_count - 1) // token_count - 1 - block_index
    returned = scan_window(back_element, reach_ahead, -1, 1)
    grad_scores = jnp.einsum(
        "the,she->hts", grad_weight, value_h, preferred_element_type=jnp.float32
    )
    grad_mix = jnp.where(inside[None], score_scale * grad_scores, 0.0).astype(jnp.bfloat16)
    to_after = (dial_end > block_begin + token_count).astype(jnp.float32)[:, None, None]
    query_grad = jnp.einsum(
        "hts,shd->thd", grad_mix, key_h, preferred_element_type=jnp.float32
    ) + from_before * score_scale * state_product("the,hde->thd", grad_weight, carried)
    key_grad = jnp.einsum(
        "hts,thd->shd", grad_mix, query_h, preferred_element_type=jnp.float32
    ) + to_after * score_scale * state_product("she,hde->shd", value_h, returned)
    value_grad = jnp.einsum(
        "hts,the->she", weights, grad_weight, preferred_element_type=jnp.float32
    ) + to_after * score_scale * state_product("shd,hde->she", key_h, returned)
    flat_shape = (token_count, head_count * HD)
    return (
        normed,
        query_grad.reshape(flat_shape).astype(jnp.bfloat16),
        key_grad.reshape(flat_shape).astype(jnp.bfloat16),
        value_grad.reshape(flat_shape).astype(jnp.bfloat16),
    )


def solution(mesh):
    placed = (
        P("seq", "head"),
        P("seq", "head"),
        P("seq", "head"),
        P("seq", "head"),
        P("head"),
        P("seq"),
        P("seq"),
    )
    return jax.shard_map(
        shards,
        mesh=mesh,
        in_specs=placed,
        out_specs=(P("seq", "head"), P("seq", "head"), P("seq", "head"), P("seq", "head")),
        check_vma=False,
    )
```

```python
import functools

import jax
import jax.numpy as jnp
from jax import lax
from jax.experimental import pallas as pl
from jax.experimental.pallas import tpu as pltpu
from jax.sharding import PartitionSpec as P

HEADS = 64
HD = 128
SPAN = 4


EPSILON = 1e-06


def from_behind(x, axis, by):
    count = lax.axis_size(axis)
    pairs = [(i, i + by) for i in range(count) if 0 <= i + by < count]
    return lax.ppermute(x, axis, pairs)


def scan_window(element, reach, step):
    nearest = from_behind(element, "seq", step)
    second = from_behind(nearest, "seq", step)
    pair = nearest + (reach >= 2).astype(jnp.float32) * second
    far_pair = from_behind(pair, "seq", 2 * step)
    total = pair + (reach >= 3).astype(jnp.float32) * far_pair
    return (reach >= 1).astype(jnp.float32) * total


def head_sum_kernel(count, parts_ref, out_ref, slots, send_sems, recv_sems):
    me = lax.axis_index("head")
    row = lax.axis_index("seq")
    barrier = pltpu.get_barrier_semaphore()
    for shift in range(1, count):
        peer = (row, lax.rem(me + shift, count))
        pl.semaphore_signal(barrier, inc=1, device_id=peer, device_id_type=pl.DeviceIdType.MESH)
    pl.semaphore_wait(barrier, count - 1)
    copies = []
    for shift in range(1, count):
        copy = pltpu.make_async_remote_copy(
            src_ref=parts_ref,
            dst_ref=slots.at[me],
            send_sem=send_sems.at[shift],
            recv_sem=recv_sems.at[me],
            device_id=(row, lax.rem(me + shift, count)),
            device_id_type=pl.DeviceIdType.MESH,
        )
        copy.start()
        copies.append(copy)
    slots[me] = parts_ref[...]
    for shift in range(1, count):
        source = lax.rem(me + count - shift, count)
        pltpu.make_async_remote_copy(
            src_ref=parts_ref,
            dst_ref=slots.at[source],
            send_sem=send_sems.at[shift],
            recv_sem=recv_sems.at[source],
            device_id=(row, source),
            device_id_type=pl.DeviceIdType.MESH,
        ).wait_recv()
    total = slots[0]
    for index in range(1, count):
        total = total + slots[index]
    out_ref[...] = total
    for copy in copies:
        copy.wait_send()


def head_sum(square_sum, cross_sum):
    count = lax.axis_size("head")
    rows = square_sum.shape[0]
    parts = jnp.concatenate(
        [square_sum[None], cross_sum[None], jnp.zeros((6, rows), jnp.float32)], axis=0
    )
    total = pl.pallas_call(
        functools.partial(head_sum_kernel, count),
        out_shape=jax.ShapeDtypeStruct(parts.shape, jnp.float32),
        in_specs=[pl.BlockSpec(memory_space=pltpu.VMEM)],
        out_specs=pl.BlockSpec(memory_space=pltpu.VMEM),
        scratch_shapes=[
            pltpu.VMEM((count,) + parts.shape, jnp.float32),
            pltpu.SemaphoreType.DMA((count,)),
            pltpu.SemaphoreType.DMA((count,)),
        ],
        compiler_params=pltpu.CompilerParams(collective_id=2, has_side_effects=True),
    )(parts)
    return total[0], total[1]


def join_states(earlier_part, later_part):
    return (
        later_part[0] + (1.0 - later_part[1]) * earlier_part[0],
        jnp.maximum(earlier_part[1], later_part[1]),
    )


def split_state(state):
    upper = state.astype(jnp.bfloat16)
    lower = (state - upper.astype(jnp.float32)).astype(jnp.bfloat16)
    return (upper, lower)


def state_product(form, rows, state):
    upper, lower = split_state(state)
    first = jnp.einsum(form, rows, upper, preferred_element_type=jnp.float32)
    return first + jnp.einsum(form, rows, lower, preferred_element_type=jnp.float32)


def shards(queries, key_rows, value_rows, out_grad, norm_gain, dial_start, dial_end):
    token_count = queries.shape[0]
    head_count = queries.shape[1] // HD
    score_scale = HD ** (-0.5)
    width_all = HEADS * HD
    block_begin = lax.axis_index("seq") * token_count
    local_pos = jnp.arange(token_count, dtype=jnp.int32)
    position = block_begin + local_pos
    query_h = queries.reshape(token_count, head_count, HD)
    key_h = key_rows.reshape(token_count, head_count, HD)
    value_h = value_rows.reshape(token_count, head_count, HD)
    last_start = dial_start[token_count - 1]
    keep_last = position >= last_start
    element = jnp.einsum(
        "shd,she->hde",
        jnp.where(keep_last[:, None, None], key_h, jnp.zeros((), jnp.bfloat16)),
        value_h,
        preferred_element_type=jnp.float32,
    )
    block_index = lax.axis_index("seq")
    reach_back = block_index - dial_start[0] // token_count
    carried = scan_window(element, reach_back, 1)
    inside = (position[None, :] >= dial_start[:, None]) & (local_pos[None, :] <= local_pos[:, None])
    scores = jnp.einsum("thd,shd->hts", query_h, key_h, preferred_element_type=jnp.float32)
    weights = jnp.where(inside[None], score_scale * scores, 0.0).astype(jnp.bfloat16)
    local_mix = jnp.einsum("hts,she->the", weights, value_h, preferred_element_type=jnp.float32)
    across = score_scale * state_product("thd,hde->the", query_h, carried)
    from_before = (dial_start < block_begin).astype(jnp.float32)[:, None, None]
    attended = (local_mix + from_before * across).reshape(token_count, head_count * HD)
    grad_wide = out_grad.astype(jnp.float32)
    square_sum, cross_sum = head_sum(
        jnp.sum(attended * attended, axis=1), jnp.sum(norm_gain * grad_wide * attended, axis=1)
    )
    inv_rms = lax.rsqrt(square_sum / width_all + EPSILON)
    normed = (attended * inv_rms[:, None] * norm_gain).astype(jnp.bfloat16)
    grad_attn = (
        inv_rms[:, None] * norm_gain * grad_wide
        - attended * (inv_rms * inv_rms * inv_rms * cross_sum / width_all)[:, None]
    )
    grad_weight = grad_attn.astype(jnp.bfloat16).reshape(token_count, head_count, HD)
    first_end = dial_end[0]
    keep_first = position < first_end
    back_element = jnp.einsum(
        "thd,the->hde",
        jnp.where(keep_first[:, None, None], query_h, jnp.zeros((), jnp.bfloat16)),
        grad_weight,
        preferred_element_type=jnp.float32,
    )
    reach_ahead = (dial_end[token_count - 1] + token_count - 1) // token_count - 1 - block_index
    returned = scan_window(back_element, reach_ahead, -1)
    grad_scores = jnp.einsum(
        "the,she->hts", grad_weight, value_h, preferred_element_type=jnp.float32
    )
    grad_mix = jnp.where(inside[None], score_scale * grad_scores, 0.0).astype(jnp.bfloat16)
    to_after = (dial_end > block_begin + token_count).astype(jnp.float32)[:, None, None]
    query_grad = jnp.einsum(
        "hts,shd->thd", grad_mix, key_h, preferred_element_type=jnp.float32
    ) + from_before * score_scale * state_product("the,hde->thd", grad_weight, carried)
    key_grad = jnp.einsum(
        "hts,thd->shd", grad_mix, query_h, preferred_element_type=jnp.float32
    ) + to_after * score_scale * state_product("she,hde->shd", value_h, returned)
    value_grad = jnp.einsum(
        "hts,the->she", weights, grad_weight, preferred_element_type=jnp.float32
    ) + to_after * score_scale * state_product("shd,hde->she", key_h, returned)
    flat_shape = (token_count, head_count * HD)
    return (
        normed,
        query_grad.reshape(flat_shape).astype(jnp.bfloat16),
        key_grad.reshape(flat_shape).astype(jnp.bfloat16),
        value_grad.reshape(flat_shape).astype(jnp.bfloat16),
    )


def solution(mesh):
    placed = (
        P("seq", "head"),
        P("seq", "head"),
        P("seq", "head"),
        P("seq", "head"),
        P("head"),
        P("seq"),
        P("seq"),
    )
    return jax.shard_map(
        shards,
        mesh=mesh,
        in_specs=placed,
        out_specs=(P("seq", "head"), P("seq", "head"), P("seq", "head"), P("seq", "head")),
        check_vma=False,
    )
```

```python
import functools

import jax
import jax.numpy as jnp
from jax import lax
from jax.experimental import pallas as pl
from jax.experimental.pallas import tpu as pltpu
from jax.sharding import PartitionSpec as P

HEADS = 64
HD = 128
SPAN = 4


EPSILON = 1e-06


def from_behind(x, axis, by):
    count = lax.axis_size(axis)
    pairs = [(i, i + by) for i in range(count) if 0 <= i + by < count]
    return lax.ppermute(x, axis, pairs)


def window_kernel(count, step, masks_ref, element_ref, out_ref, slots, send_sems, recv_sems):
    me = lax.axis_index("seq")
    head = lax.axis_index("head")
    heads = element_ref.shape[0]

    def inside_axis(offset):
        return (me + offset >= 0) & (me + offset < count)

    barrier = pltpu.get_barrier_semaphore()
    offsets = (step, 2 * step, -step, -2 * step)
    for offset in offsets:
        ring_peer = (lax.rem(me + offset + count, count), head)
        pl.semaphore_signal(barrier, inc=1, device_id=ring_peer, device_id_type=pl.DeviceIdType.MESH)
    pl.semaphore_wait(barrier, len(offsets))

    def describe(round_index, source, landing, part, distance):
        return pltpu.make_async_remote_copy(
            src_ref=source,
            dst_ref=slots.at[landing, part],
            send_sem=send_sems.at[round_index, part],
            recv_sem=recv_sems.at[round_index, part],
            device_id=(me + distance, head),
            device_id_type=pl.DeviceIdType.MESH,
        )

    def send(copy, distance):
        @pl.when(inside_axis(distance))
        def _():
            copy.start()

    def land(copy, landing, part, distance):
        @pl.when(inside_axis(-distance))
        def _():
            copy.wait_recv()

        @pl.when(jnp.logical_not(inside_axis(-distance)))
        def _():
            slots[landing, part] = jnp.zeros(slots.shape[2:], jnp.float32)

    rounds = [[], [], []]
    for part in range(heads):
        copy = describe(0, element_ref.at[part], 0, part, step)
        send(copy, step)
        rounds[0].append(copy)
    for part in range(heads):
        land(rounds[0][part], 0, part, step)
        copy = describe(1, slots.at[0, part], 1, part, step)
        send(copy, step)
        rounds[1].append(copy)
    for part in range(heads):
        land(rounds[1][part], 1, part, step)
        slots[2, part] = slots[0, part] + masks_ref[1] * slots[1, part]
        copy = describe(2, slots.at[2, part], 3, part, 2 * step)
        send(copy, 2 * step)
        rounds[2].append(copy)
    for part in range(heads):
        land(rounds[2][part], 3, part, 2 * step)
        out_ref[part] = masks_ref[0] * (slots[2, part] + masks_ref[2] * slots[3, part])
    for round_index, distance in enumerate((step, step, 2 * step)):
        for copy in rounds[round_index]:
            @pl.when(inside_axis(distance))
            def _():
                copy.wait_send()


def scan_window(element, reach, step, ident):
    count = lax.axis_size("seq")
    heads = element.shape[0]
    masks = jnp.stack([reach >= 1, reach >= 2, reach >= 3]).astype(jnp.float32)
    return pl.pallas_call(
        functools.partial(window_kernel, count, step),
        out_shape=jax.ShapeDtypeStruct(element.shape, jnp.float32),
        in_specs=[pl.BlockSpec(memory_space=pltpu.SMEM), pl.BlockSpec(memory_space=pltpu.VMEM)],
        out_specs=pl.BlockSpec(memory_space=pltpu.VMEM),
        scratch_shapes=[
            pltpu.VMEM((4,) + element.shape, jnp.float32),
            pltpu.SemaphoreType.DMA((3, heads)),
            pltpu.SemaphoreType.DMA((3, heads)),
        ],
        compiler_params=pltpu.CompilerParams(collective_id=ident, has_side_effects=True),
    )(masks, element)

def head_sum_kernel(count, parts_ref, out_ref, slots, send_sems, recv_sems):
    me = lax.axis_index("head")
    row = lax.axis_index("seq")
    barrier = pltpu.get_barrier_semaphore()
    for shift in range(1, count):
        peer = (row, lax.rem(me + shift, count))
        pl.semaphore_signal(barrier, inc=1, device_id=peer, device_id_type=pl.DeviceIdType.MESH)
    pl.semaphore_wait(barrier, count - 1)
    copies = []
    for shift in range(1, count):
        copy = pltpu.make_async_remote_copy(
            src_ref=parts_ref,
            dst_ref=slots.at[me],
            send_sem=send_sems.at[shift],
            recv_sem=recv_sems.at[me],
            device_id=(row, lax.rem(me + shift, count)),
            device_id_type=pl.DeviceIdType.MESH,
        )
        copy.start()
        copies.append(copy)
    slots[me] = parts_ref[...]
    for shift in range(1, count):
        source = lax.rem(me + count - shift, count)
        pltpu.make_async_remote_copy(
            src_ref=parts_ref,
            dst_ref=slots.at[source],
            send_sem=send_sems.at[shift],
            recv_sem=recv_sems.at[source],
            device_id=(row, source),
            device_id_type=pl.DeviceIdType.MESH,
        ).wait_recv()
    total = slots[0]
    for index in range(1, count):
        total = total + slots[index]
    out_ref[...] = total
    for copy in copies:
        copy.wait_send()


def head_sum(square_sum, cross_sum):
    count = lax.axis_size("head")
    rows = square_sum.shape[0]
    parts = jnp.concatenate(
        [square_sum[None], cross_sum[None], jnp.zeros((6, rows), jnp.float32)], axis=0
    )
    total = pl.pallas_call(
        functools.partial(head_sum_kernel, count),
        out_shape=jax.ShapeDtypeStruct(parts.shape, jnp.float32),
        in_specs=[pl.BlockSpec(memory_space=pltpu.VMEM)],
        out_specs=pl.BlockSpec(memory_space=pltpu.VMEM),
        scratch_shapes=[
            pltpu.VMEM((count,) + parts.shape, jnp.float32),
            pltpu.SemaphoreType.DMA((count,)),
            pltpu.SemaphoreType.DMA((count,)),
        ],
        compiler_params=pltpu.CompilerParams(collective_id=2, has_side_effects=True),
    )(parts)
    return total[0], total[1]


def join_states(earlier_part, later_part):
    return (
        later_part[0] + (1.0 - later_part[1]) * earlier_part[0],
        jnp.maximum(earlier_part[1], later_part[1]),
    )


def split_state(state):
    upper = state.astype(jnp.bfloat16)
    lower = (state - upper.astype(jnp.float32)).astype(jnp.bfloat16)
    return (upper, lower)


def state_product(form, rows, state):
    upper, lower = split_state(state)
    first = jnp.einsum(form, rows, upper, preferred_element_type=jnp.float32)
    return first + jnp.einsum(form, rows, lower, preferred_element_type=jnp.float32)


def shards(queries, key_rows, value_rows, out_grad, norm_gain, dial_start, dial_end):
    token_count = queries.shape[0]
    head_count = queries.shape[1] // HD
    score_scale = HD ** (-0.5)
    width_all = HEADS * HD
    block_begin = lax.axis_index("seq") * token_count
    local_pos = jnp.arange(token_count, dtype=jnp.int32)
    position = block_begin + local_pos
    query_h = queries.reshape(token_count, head_count, HD)
    key_h = key_rows.reshape(token_count, head_count, HD)
    value_h = value_rows.reshape(token_count, head_count, HD)
    last_start = dial_start[token_count - 1]
    keep_last = position >= last_start
    element = jnp.einsum(
        "shd,she->hde",
        jnp.where(keep_last[:, None, None], key_h, jnp.zeros((), jnp.bfloat16)),
        value_h,
        preferred_element_type=jnp.float32,
    )
    block_index = lax.axis_index("seq")
    reach_back = block_index - dial_start[0] // token_count
    carried = scan_window(element, reach_back, 1, 0)
    inside = (position[None, :] >= dial_start[:, None]) & (local_pos[None, :] <= local_pos[:, None])
    scores = jnp.einsum("thd,shd->hts", query_h, key_h, preferred_element_type=jnp.float32)
    weights = jnp.where(inside[None], score_scale * scores, 0.0).astype(jnp.bfloat16)
    local_mix = jnp.einsum("hts,she->the", weights, value_h, preferred_element_type=jnp.float32)
    across = score_scale * state_product("thd,hde->the", query_h, carried)
    from_before = (dial_start < block_begin).astype(jnp.float32)[:, None, None]
    attended = (local_mix + from_before * across).reshape(token_count, head_count * HD)
    grad_wide = out_grad.astype(jnp.float32)
    square_sum, cross_sum = head_sum(
        jnp.sum(attended * attended, axis=1), jnp.sum(norm_gain * grad_wide * attended, axis=1)
    )
    inv_rms = lax.rsqrt(square_sum / width_all + EPSILON)
    normed = (attended * inv_rms[:, None] * norm_gain).astype(jnp.bfloat16)
    grad_attn = (
        inv_rms[:, None] * norm_gain * grad_wide
        - attended * (inv_rms * inv_rms * inv_rms * cross_sum / width_all)[:, None]
    )
    grad_weight = grad_attn.astype(jnp.bfloat16).reshape(token_count, head_count, HD)
    first_end = dial_end[0]
    keep_first = position < first_end
    back_element = jnp.einsum(
        "thd,the->hde",
        jnp.where(keep_first[:, None, None], query_h, jnp.zeros((), jnp.bfloat16)),
        grad_weight,
        preferred_element_type=jnp.float32,
    )
    reach_ahead = (dial_end[token_count - 1] + token_count - 1) // token_count - 1 - block_index
    returned = scan_window(back_element, reach_ahead, -1, 1)
    grad_scores = jnp.einsum(
        "the,she->hts", grad_weight, value_h, preferred_element_type=jnp.float32
    )
    grad_mix = jnp.where(inside[None], score_scale * grad_scores, 0.0).astype(jnp.bfloat16)
    to_after = (dial_end > block_begin + token_count).astype(jnp.float32)[:, None, None]
    query_grad = jnp.einsum(
        "hts,shd->thd", grad_mix, key_h, preferred_element_type=jnp.float32
    ) + from_before * score_scale * state_product("the,hde->thd", grad_weight, carried)
    key_grad = jnp.einsum(
        "hts,thd->shd", grad_mix, query_h, preferred_element_type=jnp.float32
    ) + to_after * score_scale * state_product("she,hde->shd", value_h, returned)
    value_grad = jnp.einsum(
        "hts,the->she", weights, grad_weight, preferred_element_type=jnp.float32
    ) + to_after * score_scale * state_product("shd,hde->she", key_h, returned)
    flat_shape = (token_count, head_count * HD)
    return (
        normed,
        query_grad.reshape(flat_shape).astype(jnp.bfloat16),
        key_grad.reshape(flat_shape).astype(jnp.bfloat16),
        value_grad.reshape(flat_shape).astype(jnp.bfloat16),
    )


def solution(mesh):
    placed = (
        P("seq", "head"),
        P("seq", "head"),
        P("seq", "head"),
        P("seq", "head"),
        P("head"),
        P("seq"),
        P("seq"),
    )
    return jax.shard_map(
        shards,
        mesh=mesh,
        in_specs=placed,
        out_specs=(P("seq", "head"), P("seq", "head"), P("seq", "head"), P("seq", "head")),
        check_vma=False,
    )
```

```python
import functools

import jax
import jax.numpy as jnp
from jax import lax
from jax.experimental import pallas as pl
from jax.experimental.pallas import tpu as pltpu
from jax.sharding import PartitionSpec as P

HEADS = 64
HD = 128
SPAN = 4


EPSILON = 1e-06


def from_behind(x, axis, by):
    count = lax.axis_size(axis)
    pairs = [(i, i + by) for i in range(count) if 0 <= i + by < count]
    return lax.ppermute(x, axis, pairs)


def scan_window_permutes(element, reach, step):
    nearest = from_behind(element, "seq", step)
    second = from_behind(nearest, "seq", step)
    pair = nearest + (reach >= 2).astype(jnp.float32) * second
    far_pair = from_behind(pair, "seq", 2 * step)
    total = pair + (reach >= 3).astype(jnp.float32) * far_pair
    return (reach >= 1).astype(jnp.float32) * total


def chain_kernel(count, step, flag_ref, element_ref, out_ref, link_slot, state_slot, sent_slot, send_sems, recv_sems):
    me = lax.axis_index("seq")
    head = lax.axis_index("head")
    heads = element_ref.shape[0]
    rank = lax.rem(me, 4)
    pos = rank if step == 1 else 3 - rank
    ahead_exists = (me + step >= 0) & (me + step < count)
    behind_exists = (me - step >= 0) & (me - step < count)

    barrier = pltpu.get_barrier_semaphore()
    for offset in (1, -1):
        ring_peer = (lax.rem(me + offset + count, count), head)
        pl.semaphore_signal(barrier, inc=1, device_id=ring_peer, device_id_type=pl.DeviceIdType.MESH)
    pl.semaphore_wait(barrier, 2)

    def describe(kind, part, source, landing):
        return pltpu.make_async_remote_copy(
            src_ref=source,
            dst_ref=landing.at[part],
            send_sem=send_sems.at[kind, part],
            recv_sem=recv_sems.at[kind, part],
            device_id=(me + step, head),
            device_id_type=pl.DeviceIdType.MESH,
        )

    flag = flag_ref[0]
    sends = []
    for part in range(heads):
        @pl.when(pos >= 1)
        def _():
            describe(0, part, link_slot.at[part], link_slot).wait_recv()
            link_slot[part] = element_ref[part] + flag * link_slot[part]

        @pl.when(pos == 0)
        def _():
            link_slot[part] = element_ref[part]

        into_link = describe(0, part, link_slot.at[part], link_slot)
        into_state = pltpu.make_async_remote_copy(
            src_ref=link_slot.at[part],
            dst_ref=state_slot.at[part],
            send_sem=send_sems.at[0, part],
            recv_sem=recv_sems.at[1, part],
            device_id=(me + step, head),
            device_id_type=pl.DeviceIdType.MESH,
        )

        @pl.when(pos <= 2)
        def _():
            into_link.start()

        @pl.when((pos == 3) & ahead_exists)
        def _():
            into_state.start()

        sends.append((into_link, into_state))
    state_sends = []
    for part in range(heads):
        @pl.when(behind_exists)
        def _():
            describe(1, part, state_slot.at[part], state_slot).wait_recv()

        @pl.when(jnp.logical_not(behind_exists))
        def _():
            state_slot[part] = jnp.zeros(state_slot.shape[1:], jnp.float32)

        out_ref[part] = state_slot[part]
        copy = describe(1, part, sent_slot.at[part], state_slot)

        @pl.when(pos <= 2)
        def _():
            sent_slot[part] = element_ref[part] + flag * state_slot[part]
            copy.start()

        state_sends.append(copy)
    for part in range(heads):
        into_link, into_state = sends[part]

        @pl.when(pos <= 2)
        def _():
            into_link.wait_send()

        @pl.when((pos == 3) & ahead_exists)
        def _():
            into_state.wait_send()

        @pl.when(pos <= 2)
        def _():
            state_sends[part].wait_send()


def scan_window(element, flag, reach, step, ident):
    count = lax.axis_size("seq")
    if count % 4:
        return scan_window_permutes(element, reach, step)
    heads = element.shape[0]
    return pl.pallas_call(
        functools.partial(chain_kernel, count, step),
        out_shape=jax.ShapeDtypeStruct(element.shape, jnp.float32),
        in_specs=[pl.BlockSpec(memory_space=pltpu.SMEM), pl.BlockSpec(memory_space=pltpu.VMEM)],
        out_specs=pl.BlockSpec(memory_space=pltpu.VMEM),
        scratch_shapes=[
            pltpu.VMEM(element.shape, jnp.float32),
            pltpu.VMEM(element.shape, jnp.float32),
            pltpu.VMEM(element.shape, jnp.float32),
            pltpu.SemaphoreType.DMA((2, heads)),
            pltpu.SemaphoreType.DMA((2, heads)),
        ],
        compiler_params=pltpu.CompilerParams(collective_id=ident, has_side_effects=True),
    )(flag.astype(jnp.float32).reshape(1), element)

def head_sum_kernel(count, parts_ref, out_ref, slots, send_sems, recv_sems):
    me = lax.axis_index("head")
    row = lax.axis_index("seq")
    barrier = pltpu.get_barrier_semaphore()
    for shift in range(1, count):
        peer = (row, lax.rem(me + shift, count))
        pl.semaphore_signal(barrier, inc=1, device_id=peer, device_id_type=pl.DeviceIdType.MESH)
    pl.semaphore_wait(barrier, count - 1)
    copies = []
    for shift in range(1, count):
        copy = pltpu.make_async_remote_copy(
            src_ref=parts_ref,
            dst_ref=slots.at[me],
            send_sem=send_sems.at[shift],
            recv_sem=recv_sems.at[me],
            device_id=(row, lax.rem(me + shift, count)),
            device_id_type=pl.DeviceIdType.MESH,
        )
        copy.start()
        copies.append(copy)
    slots[me] = parts_ref[...]
    for shift in range(1, count):
        source = lax.rem(me + count - shift, count)
        pltpu.make_async_remote_copy(
            src_ref=parts_ref,
            dst_ref=slots.at[source],
            send_sem=send_sems.at[shift],
            recv_sem=recv_sems.at[source],
            device_id=(row, source),
            device_id_type=pl.DeviceIdType.MESH,
        ).wait_recv()
    total = slots[0]
    for index in range(1, count):
        total = total + slots[index]
    out_ref[...] = total
    for copy in copies:
        copy.wait_send()


def head_sum(square_sum, cross_sum):
    count = lax.axis_size("head")
    rows = square_sum.shape[0]
    parts = jnp.concatenate(
        [square_sum[None], cross_sum[None], jnp.zeros((6, rows), jnp.float32)], axis=0
    )
    total = pl.pallas_call(
        functools.partial(head_sum_kernel, count),
        out_shape=jax.ShapeDtypeStruct(parts.shape, jnp.float32),
        in_specs=[pl.BlockSpec(memory_space=pltpu.VMEM)],
        out_specs=pl.BlockSpec(memory_space=pltpu.VMEM),
        scratch_shapes=[
            pltpu.VMEM((count,) + parts.shape, jnp.float32),
            pltpu.SemaphoreType.DMA((count,)),
            pltpu.SemaphoreType.DMA((count,)),
        ],
        compiler_params=pltpu.CompilerParams(collective_id=2, has_side_effects=True),
    )(parts)
    return total[0], total[1]


def join_states(earlier_part, later_part):
    return (
        later_part[0] + (1.0 - later_part[1]) * earlier_part[0],
        jnp.maximum(earlier_part[1], later_part[1]),
    )


def split_state(state):
    upper = state.astype(jnp.bfloat16)
    lower = (state - upper.astype(jnp.float32)).astype(jnp.bfloat16)
    return (upper, lower)


def state_product(form, rows, state):
    upper, lower = split_state(state)
    first = jnp.einsum(form, rows, upper, preferred_element_type=jnp.float32)
    return first + jnp.einsum(form, rows, lower, preferred_element_type=jnp.float32)


def shards(queries, key_rows, value_rows, out_grad, norm_gain, dial_start, dial_end):
    token_count = queries.shape[0]
    head_count = queries.shape[1] // HD
    score_scale = HD ** (-0.5)
    width_all = HEADS * HD
    block_begin = lax.axis_index("seq") * token_count
    local_pos = jnp.arange(token_count, dtype=jnp.int32)
    position = block_begin + local_pos
    query_h = queries.reshape(token_count, head_count, HD)
    key_h = key_rows.reshape(token_count, head_count, HD)
    value_h = value_rows.reshape(token_count, head_count, HD)
    last_start = dial_start[token_count - 1]
    keep_last = position >= last_start
    element = jnp.einsum(
        "shd,she->hde",
        jnp.where(keep_last[:, None, None], key_h, jnp.zeros((), jnp.bfloat16)),
        value_h,
        preferred_element_type=jnp.float32,
    )
    block_index = lax.axis_index("seq")
    reach_back = block_index - dial_start[0] // token_count
    carried = scan_window(element, last_start < block_begin, reach_back, 1, 0)
    inside = (position[None, :] >= dial_start[:, None]) & (local_pos[None, :] <= local_pos[:, None])
    scores = jnp.einsum("thd,shd->hts", query_h, key_h, preferred_element_type=jnp.float32)
    weights = jnp.where(inside[None], score_scale * scores, 0.0).astype(jnp.bfloat16)
    local_mix = jnp.einsum("hts,she->the", weights, value_h, preferred_element_type=jnp.float32)
    across = score_scale * state_product("thd,hde->the", query_h, carried)
    from_before = (dial_start < block_begin).astype(jnp.float32)[:, None, None]
    attended = (local_mix + from_before * across).reshape(token_count, head_count * HD)
    grad_wide = out_grad.astype(jnp.float32)
    square_sum, cross_sum = head_sum(
        jnp.sum(attended * attended, axis=1), jnp.sum(norm_gain * grad_wide * attended, axis=1)
    )
    inv_rms = lax.rsqrt(square_sum / width_all + EPSILON)
    normed = (attended * inv_rms[:, None] * norm_gain).astype(jnp.bfloat16)
    grad_attn = (
        inv_rms[:, None] * norm_gain * grad_wide
        - attended * (inv_rms * inv_rms * inv_rms * cross_sum / width_all)[:, None]
    )
    grad_weight = grad_attn.astype(jnp.bfloat16).reshape(token_count, head_count, HD)
    first_end = dial_end[0]
    keep_first = position < first_end
    back_element = jnp.einsum(
        "thd,the->hde",
        jnp.where(keep_first[:, None, None], query_h, jnp.zeros((), jnp.bfloat16)),
        grad_weight,
        preferred_element_type=jnp.float32,
    )
    reach_ahead = (dial_end[token_count - 1] + token_count - 1) // token_count - 1 - block_index
    returned = scan_window(back_element, first_end > block_begin + token_count, reach_ahead, -1, 1)
    grad_scores = jnp.einsum(
        "the,she->hts", grad_weight, value_h, preferred_element_type=jnp.float32
    )
    grad_mix = jnp.where(inside[None], score_scale * grad_scores, 0.0).astype(jnp.bfloat16)
    to_after = (dial_end > block_begin + token_count).astype(jnp.float32)[:, None, None]
    query_grad = jnp.einsum(
        "hts,shd->thd", grad_mix, key_h, preferred_element_type=jnp.float32
    ) + from_before * score_scale * state_product("the,hde->thd", grad_weight, carried)
    key_grad = jnp.einsum(
        "hts,thd->shd", grad_mix, query_h, preferred_element_type=jnp.float32
    ) + to_after * score_scale * state_product("she,hde->shd", value_h, returned)
    value_grad = jnp.einsum(
        "hts,the->she", weights, grad_weight, preferred_element_type=jnp.float32
    ) + to_after * score_scale * state_product("shd,hde->she", key_h, returned)
    flat_shape = (token_count, head_count * HD)
    return (
        normed,
        query_grad.reshape(flat_shape).astype(jnp.bfloat16),
        key_grad.reshape(flat_shape).astype(jnp.bfloat16),
        value_grad.reshape(flat_shape).astype(jnp.bfloat16),
    )


def solution(mesh):
    placed = (
        P("seq", "head"),
        P("seq", "head"),
        P("seq", "head"),
        P("seq", "head"),
        P("head"),
        P("seq"),
        P("seq"),
    )
    return jax.shard_map(
        shards,
        mesh=mesh,
        in_specs=placed,
        out_specs=(P("seq", "head"), P("seq", "head"), P("seq", "head"), P("seq", "head")),
        check_vma=False,
    )
```

```python
import functools

import jax
import jax.numpy as jnp
from jax import lax
from jax.experimental import pallas as pl
from jax.experimental.pallas import tpu as pltpu
from jax.sharding import PartitionSpec as P

HEADS = 64
HD = 128
SPAN = 4


EPSILON = 1e-06


def from_behind(x, axis, by):
    count = lax.axis_size(axis)
    pairs = [(i, i + by) for i in range(count) if 0 <= i + by < count]
    return lax.ppermute(x, axis, pairs)


def scan_window_permutes(element, reach, step):
    nearest = from_behind(element, "seq", step)
    second = from_behind(nearest, "seq", step)
    pair = nearest + (reach >= 2).astype(jnp.float32) * second
    far_pair = from_behind(pair, "seq", 2 * step)
    total = pair + (reach >= 3).astype(jnp.float32) * far_pair
    return (reach >= 1).astype(jnp.float32) * total


def chain_kernel(count, step, side_work, extra_in, flag_ref, element_ref, *refs):
    side_in = refs[:extra_in]
    out_ref = refs[extra_in]
    link_slot, state_slot, sent_slot, send_sems, recv_sems = refs[-5:]
    side_out = refs[extra_in + 1:-5]
    me = lax.axis_index("seq")
    head = lax.axis_index("head")
    heads = element_ref.shape[0]
    rank = lax.rem(me, 4)
    pos = rank if step == 1 else 3 - rank
    ahead_exists = (me + step >= 0) & (me + step < count)
    behind_exists = (me - step >= 0) & (me - step < count)

    barrier = pltpu.get_barrier_semaphore()
    for offset in (1, -1):
        ring_peer = (lax.rem(me + offset + count, count), head)
        pl.semaphore_signal(barrier, inc=1, device_id=ring_peer, device_id_type=pl.DeviceIdType.MESH)
    pl.semaphore_wait(barrier, 2)

    def describe(kind, part, source, landing):
        return pltpu.make_async_remote_copy(
            src_ref=source,
            dst_ref=landing.at[part],
            send_sem=send_sems.at[kind, part],
            recv_sem=recv_sems.at[kind, part],
            device_id=(me + step, head),
            device_id_type=pl.DeviceIdType.MESH,
        )

    flag = flag_ref[0]
    sends = []
    for part in range(heads):
        @pl.when(pos >= 1)
        def _():
            describe(0, part, link_slot.at[part], link_slot).wait_recv()
            link_slot[part] = element_ref[part] + flag * link_slot[part]

        @pl.when(pos == 0)
        def _():
            link_slot[part] = element_ref[part]

        into_link = describe(0, part, link_slot.at[part], link_slot)
        into_state = pltpu.make_async_remote_copy(
            src_ref=link_slot.at[part],
            dst_ref=state_slot.at[part],
            send_sem=send_sems.at[0, part],
            recv_sem=recv_sems.at[1, part],
            device_id=(me + step, head),
            device_id_type=pl.DeviceIdType.MESH,
        )

        @pl.when(pos <= 2)
        def _():
            into_link.start()

        @pl.when((pos == 3) & ahead_exists)
        def _():
            into_state.start()

        sends.append((into_link, into_state))
    side_work(side_in, side_out)
    state_sends = []
    for part in range(heads):
        @pl.when(behind_exists)
        def _():
            describe(1, part, state_slot.at[part], state_slot).wait_recv()

        @pl.when(jnp.logical_not(behind_exists))
        def _():
            state_slot[part] = jnp.zeros(state_slot.shape[1:], jnp.float32)

        out_ref[part] = state_slot[part]
        copy = describe(1, part, sent_slot.at[part], state_slot)

        @pl.when(pos <= 2)
        def _():
            sent_slot[part] = element_ref[part] + flag * state_slot[part]
            copy.start()

        state_sends.append(copy)
    for part in range(heads):
        into_link, into_state = sends[part]

        @pl.when(pos <= 2)
        def _():
            into_link.wait_send()

        @pl.when((pos == 3) & ahead_exists)
        def _():
            into_state.wait_send()

        @pl.when(pos <= 2)
        def _():
            state_sends[part].wait_send()


def forward_local(scale, side_in, side_out):
    query_ref, key_ref, value_ref, inside_ref = side_in
    (mix_ref,) = side_out
    inside = inside_ref[...] > 0.5
    for part in range(query_ref.shape[1] // HD):
        cols = pl.ds(part * HD, HD)
        scores = lax.dot_general(
            query_ref[:, cols], key_ref[:, cols], (((1,), (1,)), ((), ())),
            preferred_element_type=jnp.float32,
        )
        weights = jnp.where(inside, scale * scores, 0.0).astype(jnp.bfloat16)
        mix_ref[:, cols] = jnp.dot(weights, value_ref[:, cols], preferred_element_type=jnp.float32)


def backward_local(scale, side_in, side_out):
    query_ref, key_ref, value_ref, grad_ref, inside_ref = side_in
    query_out, key_out, value_out = side_out
    inside = inside_ref[...] > 0.5
    contract_last = (((1,), (1,)), ((), ()))
    for part in range(query_ref.shape[1] // HD):
        cols = pl.ds(part * HD, HD)
        query_h = query_ref[:, cols]
        key_h = key_ref[:, cols]
        grad_h = grad_ref[:, cols]
        scores = lax.dot_general(query_h, key_h, contract_last, preferred_element_type=jnp.float32)
        scaled = jnp.where(inside, scale * scores, 0.0)
        grad_scores = lax.dot_general(
            grad_h, value_ref[:, cols], contract_last, preferred_element_type=jnp.float32
        )
        mixed = jnp.where(inside, scale * grad_scores, 0.0)
        query_out[:, cols] = jnp.dot(mixed.astype(jnp.bfloat16), key_h, preferred_element_type=jnp.float32)
        key_out[:, cols] = jnp.dot(mixed.T.astype(jnp.bfloat16), query_h, preferred_element_type=jnp.float32)
        value_out[:, cols] = jnp.dot(scaled.T.astype(jnp.bfloat16), grad_h, preferred_element_type=jnp.float32)


def scan_window(element, flag, step, ident, side_work, side_inputs, side_shapes):
    count = lax.axis_size("seq")
    heads = element.shape[0]
    vmem = pl.BlockSpec(memory_space=pltpu.VMEM)
    return pl.pallas_call(
        functools.partial(chain_kernel, count, step, side_work, len(side_inputs)),
        out_shape=(jax.ShapeDtypeStruct(element.shape, jnp.float32),) + tuple(side_shapes),
        in_specs=[pl.BlockSpec(memory_space=pltpu.SMEM)] + [vmem] * (1 + len(side_inputs)),
        out_specs=(vmem,) * (1 + len(side_shapes)),
        scratch_shapes=[
            pltpu.VMEM(element.shape, jnp.float32),
            pltpu.VMEM(element.shape, jnp.float32),
            pltpu.VMEM(element.shape, jnp.float32),
            pltpu.SemaphoreType.DMA((2, heads)),
            pltpu.SemaphoreType.DMA((2, heads)),
        ],
        compiler_params=pltpu.CompilerParams(collective_id=ident, has_side_effects=True),
    )(flag.astype(jnp.float32).reshape(1), element, *side_inputs)

def head_sum_kernel(count, parts_ref, out_ref, slots, send_sems, recv_sems):
    me = lax.axis_index("head")
    row = lax.axis_index("seq")
    barrier = pltpu.get_barrier_semaphore()
    for shift in range(1, count):
        peer = (row, lax.rem(me + shift, count))
        pl.semaphore_signal(barrier, inc=1, device_id=peer, device_id_type=pl.DeviceIdType.MESH)
    pl.semaphore_wait(barrier, count - 1)
    copies = []
    for shift in range(1, count):
        copy = pltpu.make_async_remote_copy(
            src_ref=parts_ref,
            dst_ref=slots.at[me],
            send_sem=send_sems.at[shift],
            recv_sem=recv_sems.at[me],
            device_id=(row, lax.rem(me + shift, count)),
            device_id_type=pl.DeviceIdType.MESH,
        )
        copy.start()
        copies.append(copy)
    slots[me] = parts_ref[...]
    for shift in range(1, count):
        source = lax.rem(me + count - shift, count)
        pltpu.make_async_remote_copy(
            src_ref=parts_ref,
            dst_ref=slots.at[source],
            send_sem=send_sems.at[shift],
            recv_sem=recv_sems.at[source],
            device_id=(row, source),
            device_id_type=pl.DeviceIdType.MESH,
        ).wait_recv()
    total = slots[0]
    for index in range(1, count):
        total = total + slots[index]
    out_ref[...] = total
    for copy in copies:
        copy.wait_send()


def head_sum(square_sum, cross_sum):
    count = lax.axis_size("head")
    rows = square_sum.shape[0]
    parts = jnp.concatenate(
        [square_sum[None], cross_sum[None], jnp.zeros((6, rows), jnp.float32)], axis=0
    )
    total = pl.pallas_call(
        functools.partial(head_sum_kernel, count),
        out_shape=jax.ShapeDtypeStruct(parts.shape, jnp.float32),
        in_specs=[pl.BlockSpec(memory_space=pltpu.VMEM)],
        out_specs=pl.BlockSpec(memory_space=pltpu.VMEM),
        scratch_shapes=[
            pltpu.VMEM((count,) + parts.shape, jnp.float32),
            pltpu.SemaphoreType.DMA((count,)),
            pltpu.SemaphoreType.DMA((count,)),
        ],
        compiler_params=pltpu.CompilerParams(collective_id=2, has_side_effects=True),
    )(parts)
    return total[0], total[1]


def join_states(earlier_part, later_part):
    return (
        later_part[0] + (1.0 - later_part[1]) * earlier_part[0],
        jnp.maximum(earlier_part[1], later_part[1]),
    )


def split_state(state):
    upper = state.astype(jnp.bfloat16)
    lower = (state - upper.astype(jnp.float32)).astype(jnp.bfloat16)
    return (upper, lower)


def state_product(form, rows, state):
    upper, lower = split_state(state)
    first = jnp.einsum(form, rows, upper, preferred_element_type=jnp.float32)
    return first + jnp.einsum(form, rows, lower, preferred_element_type=jnp.float32)


def shards(queries, key_rows, value_rows, out_grad, norm_gain, dial_start, dial_end):
    token_count = queries.shape[0]
    head_count = queries.shape[1] // HD
    score_scale = HD ** (-0.5)
    width_all = HEADS * HD
    block_begin = lax.axis_index("seq") * token_count
    local_pos = jnp.arange(token_count, dtype=jnp.int32)
    position = block_begin + local_pos
    query_h = queries.reshape(token_count, head_count, HD)
    key_h = key_rows.reshape(token_count, head_count, HD)
    value_h = value_rows.reshape(token_count, head_count, HD)
    last_start = dial_start[token_count - 1]
    keep_last = position >= last_start
    element = jnp.einsum(
        "shd,she->hde",
        jnp.where(keep_last[:, None, None], key_h, jnp.zeros((), jnp.bfloat16)),
        value_h,
        preferred_element_type=jnp.float32,
    )
    inside = (position[None, :] >= dial_start[:, None]) & (local_pos[None, :] <= local_pos[:, None])
    inside_wide = inside.astype(jnp.float32)
    flat_shape = (token_count, head_count * HD)
    wide_shape = jax.ShapeDtypeStruct(flat_shape, jnp.float32)
    carried, local_flat = scan_window(
        element, last_start < block_begin, 1, 0,
        functools.partial(forward_local, score_scale),
        (queries, key_rows, value_rows, inside_wide), (wide_shape,),
    )
    local_mix = local_flat.reshape(token_count, head_count, HD)
    across = score_scale * state_product("thd,hde->the", query_h, carried)
    from_before = (dial_start < block_begin).astype(jnp.float32)[:, None, None]
    attended = (local_mix + from_before * across).reshape(token_count, head_count * HD)
    grad_wide = out_grad.astype(jnp.float32)
    square_sum, cross_sum = head_sum(
        jnp.sum(attended * attended, axis=1), jnp.sum(norm_gain * grad_wide * attended, axis=1)
    )
    inv_rms = lax.rsqrt(square_sum / width_all + EPSILON)
    normed = (attended * inv_rms[:, None] * norm_gain).astype(jnp.bfloat16)
    grad_attn = (
        inv_rms[:, None] * norm_gain * grad_wide
        - attended * (inv_rms * inv_rms * inv_rms * cross_sum / width_all)[:, None]
    )
    grad_weight = grad_attn.astype(jnp.bfloat16).reshape(token_count, head_count, HD)
    first_end = dial_end[0]
    keep_first = position < first_end
    back_element = jnp.einsum(
        "thd,the->hde",
        jnp.where(keep_first[:, None, None], query_h, jnp.zeros((), jnp.bfloat16)),
        grad_weight,
        preferred_element_type=jnp.float32,
    )
    returned, query_local, key_local, value_local = scan_window(
        back_element, first_end > block_begin + token_count, -1, 1,
        functools.partial(backward_local, score_scale),
        (queries, key_rows, value_rows, grad_weight.reshape(flat_shape), inside_wide),
        (wide_shape,) * 3,
    )
    to_after = (dial_end > block_begin + token_count).astype(jnp.float32)[:, None, None]
    query_grad = query_local.reshape(token_count, head_count, HD) + from_before * score_scale * state_product("the,hde->thd", grad_weight, carried)
    key_grad = key_local.reshape(token_count, head_count, HD) + to_after * score_scale * state_product("she,hde->shd", value_h, returned)
    value_grad = value_local.reshape(token_count, head_count, HD) + to_after * score_scale * state_product("shd,hde->she", key_h, returned)
    return (
        normed,
        query_grad.reshape(flat_shape).astype(jnp.bfloat16),
        key_grad.reshape(flat_shape).astype(jnp.bfloat16),
        value_grad.reshape(flat_shape).astype(jnp.bfloat16),
    )


def solution(mesh):
    placed = (
        P("seq", "head"),
        P("seq", "head"),
        P("seq", "head"),
        P("seq", "head"),
        P("head"),
        P("seq"),
        P("seq"),
    )
    return jax.shard_map(
        shards,
        mesh=mesh,
        in_specs=placed,
        out_specs=(P("seq", "head"), P("seq", "head"), P("seq", "head"), P("seq", "head")),
        check_vma=False,
    )
```

```python
import functools

import jax
import jax.numpy as jnp
from jax import lax
from jax.experimental import pallas as pl
from jax.experimental.pallas import tpu as pltpu
from jax.sharding import PartitionSpec as P

HEADS = 64
HD = 128
SPAN = 4
PIECES = 2


EPSILON = 1e-06


def from_behind(x, axis, by):
    count = lax.axis_size(axis)
    pairs = [(i, i + by) for i in range(count) if 0 <= i + by < count]
    return lax.ppermute(x, axis, pairs)


def scan_window_permutes(element, reach, step):
    nearest = from_behind(element, "seq", step)
    second = from_behind(nearest, "seq", step)
    pair = nearest + (reach >= 2).astype(jnp.float32) * second
    far_pair = from_behind(pair, "seq", 2 * step)
    total = pair + (reach >= 3).astype(jnp.float32) * far_pair
    return (reach >= 1).astype(jnp.float32) * total


def chain_kernel(count, step, flag_ref, element_ref, out_ref, link_slot, state_slot, sent_slot, send_sems, recv_sems):
    me = lax.axis_index("seq")
    head = lax.axis_index("head")
    heads = element_ref.shape[0]
    rank = lax.rem(me, 4)
    pos = rank if step == 1 else 3 - rank
    ahead_exists = (me + step >= 0) & (me + step < count)
    behind_exists = (me - step >= 0) & (me - step < count)

    barrier = pltpu.get_barrier_semaphore()
    for offset in (1, -1):
        ring_peer = (lax.rem(me + offset + count, count), head)
        pl.semaphore_signal(barrier, inc=1, device_id=ring_peer, device_id_type=pl.DeviceIdType.MESH)
    pl.semaphore_wait(barrier, 2)

    def describe(kind, part, source, landing):
        return pltpu.make_async_remote_copy(
            src_ref=source,
            dst_ref=landing.at[part],
            send_sem=send_sems.at[kind, part],
            recv_sem=recv_sems.at[kind, part],
            device_id=(me + step, head),
            device_id_type=pl.DeviceIdType.MESH,
        )

    flag = flag_ref[0]
    sends = []
    for part in range(heads):
        @pl.when(pos >= 1)
        def _():
            describe(0, part, link_slot.at[part], link_slot).wait_recv()
            link_slot[part] = element_ref[part] + flag * link_slot[part]

        @pl.when(pos == 0)
        def _():
            link_slot[part] = element_ref[part]

        into_link = describe(0, part, link_slot.at[part], link_slot)
        into_state = pltpu.make_async_remote_copy(
            src_ref=link_slot.at[part],
            dst_ref=state_slot.at[part],
            send_sem=send_sems.at[0, part],
            recv_sem=recv_sems.at[1, part],
            device_id=(me + step, head),
            device_id_type=pl.DeviceIdType.MESH,
        )

        @pl.when(pos <= 2)
        def _():
            into_link.start()

        @pl.when((pos == 3) & ahead_exists)
        def _():
            into_state.start()

        sends.append((into_link, into_state))
    state_sends = []
    for part in range(heads):
        @pl.when(behind_exists)
        def _():
            describe(1, part, state_slot.at[part], state_slot).wait_recv()

        @pl.when(jnp.logical_not(behind_exists))
        def _():
            state_slot[part] = jnp.zeros(state_slot.shape[1:], jnp.float32)

        out_ref[part] = state_slot[part]
        copy = describe(1, part, sent_slot.at[part], state_slot)

        @pl.when(pos <= 2)
        def _():
            sent_slot[part] = element_ref[part] + flag * state_slot[part]
            copy.start()

        state_sends.append(copy)
    for part in range(heads):
        into_link, into_state = sends[part]

        @pl.when(pos <= 2)
        def _():
            into_link.wait_send()

        @pl.when((pos == 3) & ahead_exists)
        def _():
            into_state.wait_send()

        @pl.when(pos <= 2)
        def _():
            state_sends[part].wait_send()


def scan_window(element, flag, reach, step, ident):
    count = lax.axis_size("seq")
    if count % 4:
        return scan_window_permutes(element, reach, step)
    shape = element.shape
    element = element.reshape(shape[0] * PIECES, shape[1] // PIECES, shape[2])
    heads = element.shape[0]
    return pl.pallas_call(
        functools.partial(chain_kernel, count, step),
        out_shape=jax.ShapeDtypeStruct(element.shape, jnp.float32),
        in_specs=[pl.BlockSpec(memory_space=pltpu.SMEM), pl.BlockSpec(memory_space=pltpu.VMEM)],
        out_specs=pl.BlockSpec(memory_space=pltpu.VMEM),
        scratch_shapes=[
            pltpu.VMEM(element.shape, jnp.float32),
            pltpu.VMEM(element.shape, jnp.float32),
            pltpu.VMEM(element.shape, jnp.float32),
            pltpu.SemaphoreType.DMA((2, heads)),
            pltpu.SemaphoreType.DMA((2, heads)),
        ],
        compiler_params=pltpu.CompilerParams(collective_id=ident, has_side_effects=True),
    )(flag.astype(jnp.float32).reshape(1), element).reshape(shape)

def head_sum_kernel(count, parts_ref, out_ref, slots, send_sems, recv_sems):
    me = lax.axis_index("head")
    row = lax.axis_index("seq")
    barrier = pltpu.get_barrier_semaphore()
    for shift in range(1, count):
        peer = (row, lax.rem(me + shift, count))
        pl.semaphore_signal(barrier, inc=1, device_id=peer, device_id_type=pl.DeviceIdType.MESH)
    pl.semaphore_wait(barrier, count - 1)
    copies = []
    for shift in range(1, count):
        copy = pltpu.make_async_remote_copy(
            src_ref=parts_ref,
            dst_ref=slots.at[me],
            send_sem=send_sems.at[shift],
            recv_sem=recv_sems.at[me],
            device_id=(row, lax.rem(me + shift, count)),
            device_id_type=pl.DeviceIdType.MESH,
        )
        copy.start()
        copies.append(copy)
    slots[me] = parts_ref[...]
    for shift in range(1, count):
        source = lax.rem(me + count - shift, count)
        pltpu.make_async_remote_copy(
            src_ref=parts_ref,
            dst_ref=slots.at[source],
            send_sem=send_sems.at[shift],
            recv_sem=recv_sems.at[source],
            device_id=(row, source),
            device_id_type=pl.DeviceIdType.MESH,
        ).wait_recv()
    total = slots[0]
    for index in range(1, count):
        total = total + slots[index]
    out_ref[...] = total
    for copy in copies:
        copy.wait_send()


def head_sum(square_sum, cross_sum):
    count = lax.axis_size("head")
    rows = square_sum.shape[0]
    parts = jnp.concatenate(
        [square_sum[None], cross_sum[None], jnp.zeros((6, rows), jnp.float32)], axis=0
    )
    total = pl.pallas_call(
        functools.partial(head_sum_kernel, count),
        out_shape=jax.ShapeDtypeStruct(parts.shape, jnp.float32),
        in_specs=[pl.BlockSpec(memory_space=pltpu.VMEM)],
        out_specs=pl.BlockSpec(memory_space=pltpu.VMEM),
        scratch_shapes=[
            pltpu.VMEM((count,) + parts.shape, jnp.float32),
            pltpu.SemaphoreType.DMA((count,)),
            pltpu.SemaphoreType.DMA((count,)),
        ],
        compiler_params=pltpu.CompilerParams(collective_id=2, has_side_effects=True),
    )(parts)
    return total[0], total[1]


def join_states(earlier_part, later_part):
    return (
        later_part[0] + (1.0 - later_part[1]) * earlier_part[0],
        jnp.maximum(earlier_part[1], later_part[1]),
    )


def split_state(state):
    upper = state.astype(jnp.bfloat16)
    lower = (state - upper.astype(jnp.float32)).astype(jnp.bfloat16)
    return (upper, lower)


def state_product(form, rows, state):
    upper, lower = split_state(state)
    first = jnp.einsum(form, rows, upper, preferred_element_type=jnp.float32)
    return first + jnp.einsum(form, rows, lower, preferred_element_type=jnp.float32)


def shards(queries, key_rows, value_rows, out_grad, norm_gain, dial_start, dial_end):
    token_count = queries.shape[0]
    head_count = queries.shape[1] // HD
    score_scale = HD ** (-0.5)
    width_all = HEADS * HD
    block_begin = lax.axis_index("seq") * token_count
    local_pos = jnp.arange(token_count, dtype=jnp.int32)
    position = block_begin + local_pos
    query_h = queries.reshape(token_count, head_count, HD)
    key_h = key_rows.reshape(token_count, head_count, HD)
    value_h = value_rows.reshape(token_count, head_count, HD)
    last_start = dial_start[token_count - 1]
    keep_last = position >= last_start
    element = jnp.einsum(
        "shd,she->hde",
        jnp.where(keep_last[:, None, None], key_h, jnp.zeros((), jnp.bfloat16)),
        value_h,
        preferred_element_type=jnp.float32,
    )
    block_index = lax.axis_index("seq")
    reach_back = block_index - dial_start[0] // token_count
    carried = scan_window(element, last_start < block_begin, reach_back, 1, 0)
    inside = (position[None, :] >= dial_start[:, None]) & (local_pos[None, :] <= local_pos[:, None])
    scores = jnp.einsum("thd,shd->hts", query_h, key_h, preferred_element_type=jnp.float32)
    weights = jnp.where(inside[None], score_scale * scores, 0.0).astype(jnp.bfloat16)
    local_mix = jnp.einsum("hts,she->the", weights, value_h, preferred_element_type=jnp.float32)
    across = score_scale * state_product("thd,hde->the", query_h, carried)
    from_before = (dial_start < block_begin).astype(jnp.float32)[:, None, None]
    attended = (local_mix + from_before * across).reshape(token_count, head_count * HD)
    grad_wide = out_grad.astype(jnp.float32)
    square_sum, cross_sum = head_sum(
        jnp.sum(attended * attended, axis=1), jnp.sum(norm_gain * grad_wide * attended, axis=1)
    )
    inv_rms = lax.rsqrt(square_sum / width_all + EPSILON)
    normed = (attended * inv_rms[:, None] * norm_gain).astype(jnp.bfloat16)
    grad_attn = (
        inv_rms[:, None] * norm_gain * grad_wide
        - attended * (inv_rms * inv_rms * inv_rms * cross_sum / width_all)[:, None]
    )
    grad_weight = grad_attn.astype(jnp.bfloat16).reshape(token_count, head_count, HD)
    first_end = dial_end[0]
    keep_first = position < first_end
    back_element = jnp.einsum(
        "thd,the->hde",
        jnp.where(keep_first[:, None, None], query_h, jnp.zeros((), jnp.bfloat16)),
        grad_weight,
        preferred_element_type=jnp.float32,
    )
    reach_ahead = (dial_end[token_count - 1] + token_count - 1) // token_count - 1 - block_index
    returned = scan_window(back_element, first_end > block_begin + token_count, reach_ahead, -1, 1)
    grad_scores = jnp.einsum(
        "the,she->hts", grad_weight, value_h, preferred_element_type=jnp.float32
    )
    grad_mix = jnp.where(inside[None], score_scale * grad_scores, 0.0).astype(jnp.bfloat16)
    to_after = (dial_end > block_begin + token_count).astype(jnp.float32)[:, None, None]
    query_grad = jnp.einsum(
        "hts,shd->thd", grad_mix, key_h, preferred_element_type=jnp.float32
    ) + from_before * score_scale * state_product("the,hde->thd", grad_weight, carried)
    key_grad = jnp.einsum(
        "hts,thd->shd", grad_mix, query_h, preferred_element_type=jnp.float32
    ) + to_after * score_scale * state_product("she,hde->shd", value_h, returned)
    value_grad = jnp.einsum(
        "hts,the->she", weights, grad_weight, preferred_element_type=jnp.float32
    ) + to_after * score_scale * state_product("shd,hde->she", key_h, returned)
    flat_shape = (token_count, head_count * HD)
    return (
        normed,
        query_grad.reshape(flat_shape).astype(jnp.bfloat16),
        key_grad.reshape(flat_shape).astype(jnp.bfloat16),
        value_grad.reshape(flat_shape).astype(jnp.bfloat16),
    )


def solution(mesh):
    placed = (
        P("seq", "head"),
        P("seq", "head"),
        P("seq", "head"),
        P("seq", "head"),
        P("head"),
        P("seq"),
        P("seq"),
    )
    return jax.shard_map(
        shards,
        mesh=mesh,
        in_specs=placed,
        out_specs=(P("seq", "head"), P("seq", "head"), P("seq", "head"), P("seq", "head")),
        check_vma=False,
    )
```

```python
import functools

import jax
import jax.numpy as jnp
from jax import lax
from jax.experimental import pallas as pl
from jax.experimental.pallas import tpu as pltpu
from jax.sharding import PartitionSpec as P

HEADS = 64
HD = 128
SPAN = 4
PIECES = 2


EPSILON = 1e-06


def from_behind(x, axis, by):
    count = lax.axis_size(axis)
    pairs = [(i, i + by) for i in range(count) if 0 <= i + by < count]
    return lax.ppermute(x, axis, pairs)


def scan_window_permutes(element, reach, step):
    nearest = from_behind(element, "seq", step)
    second = from_behind(nearest, "seq", step)
    pair = nearest + (reach >= 2).astype(jnp.float32) * second
    far_pair = from_behind(pair, "seq", 2 * step)
    total = pair + (reach >= 3).astype(jnp.float32) * far_pair
    return (reach >= 1).astype(jnp.float32) * total


def chain_kernel(count, step, flag_ref, element_ref, out_ref, link_slot, state_slot, sent_slot, send_sems, recv_sems):
    me = lax.axis_index("seq")
    head = lax.axis_index("head")
    heads = element_ref.shape[0]
    pos = lax.rem(me, 4) if step == 1 else 3 - lax.rem(me + 2, 4)
    ahead_exists = (me + step >= 0) & (me + step < count)
    behind_exists = (me - step >= 0) & (me - step < count)

    barrier = pltpu.get_barrier_semaphore()
    for offset in (1, -1):
        ring_peer = (lax.rem(me + offset + count, count), head)
        pl.semaphore_signal(barrier, inc=1, device_id=ring_peer, device_id_type=pl.DeviceIdType.MESH)
    pl.semaphore_wait(barrier, 2)

    def describe(kind, part, source, landing):
        return pltpu.make_async_remote_copy(
            src_ref=source,
            dst_ref=landing.at[part],
            send_sem=send_sems.at[kind, part],
            recv_sem=recv_sems.at[kind, part],
            device_id=(me + step, head),
            device_id_type=pl.DeviceIdType.MESH,
        )

    flag = flag_ref[0]
    sends = []
    for part in range(heads):
        @pl.when((pos >= 1) & behind_exists)
        def _():
            describe(0, part, link_slot.at[part], link_slot).wait_recv()
            link_slot[part] = element_ref[part] + flag * link_slot[part]

        @pl.when((pos == 0) | jnp.logical_not(behind_exists))
        def _():
            link_slot[part] = element_ref[part]

        into_link = describe(0, part, link_slot.at[part], link_slot)
        into_state = pltpu.make_async_remote_copy(
            src_ref=link_slot.at[part],
            dst_ref=state_slot.at[part],
            send_sem=send_sems.at[0, part],
            recv_sem=recv_sems.at[1, part],
            device_id=(me + step, head),
            device_id_type=pl.DeviceIdType.MESH,
        )

        @pl.when((pos <= 2) & ahead_exists)
        def _():
            into_link.start()

        @pl.when((pos == 3) & ahead_exists)
        def _():
            into_state.start()

        sends.append((into_link, into_state))
    state_sends = []
    for part in range(heads):
        @pl.when(behind_exists)
        def _():
            describe(1, part, state_slot.at[part], state_slot).wait_recv()

        @pl.when(jnp.logical_not(behind_exists))
        def _():
            state_slot[part] = jnp.zeros(state_slot.shape[1:], jnp.float32)

        out_ref[part] = state_slot[part]
        copy = describe(1, part, sent_slot.at[part], state_slot)

        @pl.when((pos <= 2) & ahead_exists)
        def _():
            sent_slot[part] = element_ref[part] + flag * state_slot[part]
            copy.start()

        state_sends.append(copy)
    for part in range(heads):
        into_link, into_state = sends[part]

        @pl.when((pos <= 2) & ahead_exists)
        def _():
            into_link.wait_send()

        @pl.when((pos == 3) & ahead_exists)
        def _():
            into_state.wait_send()

        @pl.when((pos <= 2) & ahead_exists)
        def _():
            state_sends[part].wait_send()


def scan_window(element, flag, reach, step, ident):
    count = lax.axis_size("seq")
    if count % 4:
        return scan_window_permutes(element, reach, step)
    shape = element.shape
    element = element.reshape(shape[0] * PIECES, shape[1] // PIECES, shape[2])
    heads = element.shape[0]
    return pl.pallas_call(
        functools.partial(chain_kernel, count, step),
        out_shape=jax.ShapeDtypeStruct(element.shape, jnp.float32),
        in_specs=[pl.BlockSpec(memory_space=pltpu.SMEM), pl.BlockSpec(memory_space=pltpu.VMEM)],
        out_specs=pl.BlockSpec(memory_space=pltpu.VMEM),
        scratch_shapes=[
            pltpu.VMEM(element.shape, jnp.float32),
            pltpu.VMEM(element.shape, jnp.float32),
            pltpu.VMEM(element.shape, jnp.float32),
            pltpu.SemaphoreType.DMA((2, heads)),
            pltpu.SemaphoreType.DMA((2, heads)),
        ],
        compiler_params=pltpu.CompilerParams(collective_id=ident, has_side_effects=True),
    )(flag.astype(jnp.float32).reshape(1), element).reshape(shape)

def head_sum_kernel(count, parts_ref, out_ref, slots, send_sems, recv_sems):
    me = lax.axis_index("head")
    row = lax.axis_index("seq")
    barrier = pltpu.get_barrier_semaphore()
    for shift in range(1, count):
        peer = (row, lax.rem(me + shift, count))
        pl.semaphore_signal(barrier, inc=1, device_id=peer, device_id_type=pl.DeviceIdType.MESH)
    pl.semaphore_wait(barrier, count - 1)
    copies = []
    for shift in range(1, count):
        copy = pltpu.make_async_remote_copy(
            src_ref=parts_ref,
            dst_ref=slots.at[me],
            send_sem=send_sems.at[shift],
            recv_sem=recv_sems.at[me],
            device_id=(row, lax.rem(me + shift, count)),
            device_id_type=pl.DeviceIdType.MESH,
        )
        copy.start()
        copies.append(copy)
    slots[me] = parts_ref[...]
    for shift in range(1, count):
        source = lax.rem(me + count - shift, count)
        pltpu.make_async_remote_copy(
            src_ref=parts_ref,
            dst_ref=slots.at[source],
            send_sem=send_sems.at[shift],
            recv_sem=recv_sems.at[source],
            device_id=(row, source),
            device_id_type=pl.DeviceIdType.MESH,
        ).wait_recv()
    total = slots[0]
    for index in range(1, count):
        total = total + slots[index]
    out_ref[...] = total
    for copy in copies:
        copy.wait_send()


def head_sum(square_sum, cross_sum):
    count = lax.axis_size("head")
    rows = square_sum.shape[0]
    parts = jnp.concatenate(
        [square_sum[None], cross_sum[None], jnp.zeros((6, rows), jnp.float32)], axis=0
    )
    total = pl.pallas_call(
        functools.partial(head_sum_kernel, count),
        out_shape=jax.ShapeDtypeStruct(parts.shape, jnp.float32),
        in_specs=[pl.BlockSpec(memory_space=pltpu.VMEM)],
        out_specs=pl.BlockSpec(memory_space=pltpu.VMEM),
        scratch_shapes=[
            pltpu.VMEM((count,) + parts.shape, jnp.float32),
            pltpu.SemaphoreType.DMA((count,)),
            pltpu.SemaphoreType.DMA((count,)),
        ],
        compiler_params=pltpu.CompilerParams(collective_id=2, has_side_effects=True),
    )(parts)
    return total[0], total[1]


def join_states(earlier_part, later_part):
    return (
        later_part[0] + (1.0 - later_part[1]) * earlier_part[0],
        jnp.maximum(earlier_part[1], later_part[1]),
    )


def split_state(state):
    upper = state.astype(jnp.bfloat16)
    lower = (state - upper.astype(jnp.float32)).astype(jnp.bfloat16)
    return (upper, lower)


def state_product(form, rows, state):
    upper, lower = split_state(state)
    first = jnp.einsum(form, rows, upper, preferred_element_type=jnp.float32)
    return first + jnp.einsum(form, rows, lower, preferred_element_type=jnp.float32)


def shards(queries, key_rows, value_rows, out_grad, norm_gain, dial_start, dial_end):
    token_count = queries.shape[0]
    head_count = queries.shape[1] // HD
    score_scale = HD ** (-0.5)
    width_all = HEADS * HD
    block_begin = lax.axis_index("seq") * token_count
    local_pos = jnp.arange(token_count, dtype=jnp.int32)
    position = block_begin + local_pos
    query_h = queries.reshape(token_count, head_count, HD)
    key_h = key_rows.reshape(token_count, head_count, HD)
    value_h = value_rows.reshape(token_count, head_count, HD)
    last_start = dial_start[token_count - 1]
    keep_last = position >= last_start
    element = jnp.einsum(
        "shd,she->hde",
        jnp.where(keep_last[:, None, None], key_h, jnp.zeros((), jnp.bfloat16)),
        value_h,
        preferred_element_type=jnp.float32,
    )
    block_index = lax.axis_index("seq")
    reach_back = block_index - dial_start[0] // token_count
    carried = scan_window(element, last_start < block_begin, reach_back, 1, 0)
    inside = (position[None, :] >= dial_start[:, None]) & (local_pos[None, :] <= local_pos[:, None])
    scores = jnp.einsum("thd,shd->hts", query_h, key_h, preferred_element_type=jnp.float32)
    weights = jnp.where(inside[None], score_scale * scores, 0.0).astype(jnp.bfloat16)
    local_mix = jnp.einsum("hts,she->the", weights, value_h, preferred_element_type=jnp.float32)
    across = score_scale * state_product("thd,hde->the", query_h, carried)
    from_before = (dial_start < block_begin).astype(jnp.float32)[:, None, None]
    attended = (local_mix + from_before * across).reshape(token_count, head_count * HD)
    grad_wide = out_grad.astype(jnp.float32)
    square_sum, cross_sum = head_sum(
        jnp.sum(attended * attended, axis=1), jnp.sum(norm_gain * grad_wide * attended, axis=1)
    )
    inv_rms = lax.rsqrt(square_sum / width_all + EPSILON)
    normed = (attended * inv_rms[:, None] * norm_gain).astype(jnp.bfloat16)
    grad_attn = (
        inv_rms[:, None] * norm_gain * grad_wide
        - attended * (inv_rms * inv_rms * inv_rms * cross_sum / width_all)[:, None]
    )
    grad_weight = grad_attn.astype(jnp.bfloat16).reshape(token_count, head_count, HD)
    first_end = dial_end[0]
    keep_first = position < first_end
    back_element = jnp.einsum(
        "thd,the->hde",
        jnp.where(keep_first[:, None, None], query_h, jnp.zeros((), jnp.bfloat16)),
        grad_weight,
        preferred_element_type=jnp.float32,
    )
    reach_ahead = (dial_end[token_count - 1] + token_count - 1) // token_count - 1 - block_index
    returned = scan_window(back_element, first_end > block_begin + token_count, reach_ahead, -1, 1)
    grad_scores = jnp.einsum(
        "the,she->hts", grad_weight, value_h, preferred_element_type=jnp.float32
    )
    grad_mix = jnp.where(inside[None], score_scale * grad_scores, 0.0).astype(jnp.bfloat16)
    to_after = (dial_end > block_begin + token_count).astype(jnp.float32)[:, None, None]
    query_grad = jnp.einsum(
        "hts,shd->thd", grad_mix, key_h, preferred_element_type=jnp.float32
    ) + from_before * score_scale * state_product("the,hde->thd", grad_weight, carried)
    key_grad = jnp.einsum(
        "hts,thd->shd", grad_mix, query_h, preferred_element_type=jnp.float32
    ) + to_after * score_scale * state_product("she,hde->shd", value_h, returned)
    value_grad = jnp.einsum(
        "hts,the->she", weights, grad_weight, preferred_element_type=jnp.float32
    ) + to_after * score_scale * state_product("shd,hde->she", key_h, returned)
    flat_shape = (token_count, head_count * HD)
    return (
        normed,
        query_grad.reshape(flat_shape).astype(jnp.bfloat16),
        key_grad.reshape(flat_shape).astype(jnp.bfloat16),
        value_grad.reshape(flat_shape).astype(jnp.bfloat16),
    )


def solution(mesh):
    placed = (
        P("seq", "head"),
        P("seq", "head"),
        P("seq", "head"),
        P("seq", "head"),
        P("head"),
        P("seq"),
        P("seq"),
    )
    return jax.shard_map(
        shards,
        mesh=mesh,
        in_specs=placed,
        out_specs=(P("seq", "head"), P("seq", "head"), P("seq", "head"), P("seq", "head")),
        check_vma=False,
    )
```

```python
import functools

import jax
import jax.numpy as jnp
from jax import lax
from jax.experimental import pallas as pl
from jax.experimental.pallas import tpu as pltpu
from jax.sharding import PartitionSpec as P

HEADS = 64
HD = 128
SPAN = 4
PIECES = 4


EPSILON = 1e-06


def from_behind(x, axis, by):
    count = lax.axis_size(axis)
    pairs = [(i, i + by) for i in range(count) if 0 <= i + by < count]
    return lax.ppermute(x, axis, pairs)


def scan_window_permutes(element, reach, step):
    nearest = from_behind(element, "seq", step)
    second = from_behind(nearest, "seq", step)
    pair = nearest + (reach >= 2).astype(jnp.float32) * second
    far_pair = from_behind(pair, "seq", 2 * step)
    total = pair + (reach >= 3).astype(jnp.float32) * far_pair
    return (reach >= 1).astype(jnp.float32) * total


def chain_kernel(count, step, flag_ref, element_ref, out_ref, link_slot, state_slot, sent_slot, send_sems, recv_sems):
    me = lax.axis_index("seq")
    head = lax.axis_index("head")
    heads = element_ref.shape[0]
    pos = lax.rem(me, 4) if step == 1 else 3 - lax.rem(me + 2, 4)
    ahead_exists = (me + step >= 0) & (me + step < count)
    behind_exists = (me - step >= 0) & (me - step < count)

    barrier = pltpu.get_barrier_semaphore()
    for offset in (1, -1):
        ring_peer = (lax.rem(me + offset + count, count), head)
        pl.semaphore_signal(barrier, inc=1, device_id=ring_peer, device_id_type=pl.DeviceIdType.MESH)
    pl.semaphore_wait(barrier, 2)

    def describe(kind, part, source, landing):
        return pltpu.make_async_remote_copy(
            src_ref=source,
            dst_ref=landing.at[part],
            send_sem=send_sems.at[kind, part],
            recv_sem=recv_sems.at[kind, part],
            device_id=(me + step, head),
            device_id_type=pl.DeviceIdType.MESH,
        )

    flag = flag_ref[0]
    sends = []
    for part in range(heads):
        @pl.when((pos >= 1) & behind_exists)
        def _():
            describe(0, part, link_slot.at[part], link_slot).wait_recv()
            link_slot[part] = element_ref[part] + flag * link_slot[part]

        @pl.when((pos == 0) | jnp.logical_not(behind_exists))
        def _():
            link_slot[part] = element_ref[part]

        into_link = describe(0, part, link_slot.at[part], link_slot)
        into_state = pltpu.make_async_remote_copy(
            src_ref=link_slot.at[part],
            dst_ref=state_slot.at[part],
            send_sem=send_sems.at[0, part],
            recv_sem=recv_sems.at[1, part],
            device_id=(me + step, head),
            device_id_type=pl.DeviceIdType.MESH,
        )

        @pl.when((pos <= 2) & ahead_exists)
        def _():
            into_link.start()

        @pl.when((pos == 3) & ahead_exists)
        def _():
            into_state.start()

        sends.append((into_link, into_state))
    state_sends = []
    for part in range(heads):
        @pl.when(behind_exists)
        def _():
            describe(1, part, state_slot.at[part], state_slot).wait_recv()

        @pl.when(jnp.logical_not(behind_exists))
        def _():
            state_slot[part] = jnp.zeros(state_slot.shape[1:], jnp.float32)

        out_ref[part] = state_slot[part]
        copy = describe(1, part, sent_slot.at[part], state_slot)

        @pl.when((pos <= 2) & ahead_exists)
        def _():
            sent_slot[part] = element_ref[part] + flag * state_slot[part]
            copy.start()

        state_sends.append(copy)
    for part in range(heads):
        into_link, into_state = sends[part]

        @pl.when((pos <= 2) & ahead_exists)
        def _():
            into_link.wait_send()

        @pl.when((pos == 3) & ahead_exists)
        def _():
            into_state.wait_send()

        @pl.when((pos <= 2) & ahead_exists)
        def _():
            state_sends[part].wait_send()


def scan_window(element, flag, reach, step, ident):
    count = lax.axis_size("seq")
    if count % 4:
        return scan_window_permutes(element, reach, step)
    shape = element.shape
    element = element.reshape(shape[0] * PIECES, shape[1] // PIECES, shape[2])
    heads = element.shape[0]
    return pl.pallas_call(
        functools.partial(chain_kernel, count, step),
        out_shape=jax.ShapeDtypeStruct(element.shape, jnp.float32),
        in_specs=[pl.BlockSpec(memory_space=pltpu.SMEM), pl.BlockSpec(memory_space=pltpu.VMEM)],
        out_specs=pl.BlockSpec(memory_space=pltpu.VMEM),
        scratch_shapes=[
            pltpu.VMEM(element.shape, jnp.float32),
            pltpu.VMEM(element.shape, jnp.float32),
            pltpu.VMEM(element.shape, jnp.float32),
            pltpu.SemaphoreType.DMA((2, heads)),
            pltpu.SemaphoreType.DMA((2, heads)),
        ],
        compiler_params=pltpu.CompilerParams(collective_id=ident, has_side_effects=True),
    )(flag.astype(jnp.float32).reshape(1), element).reshape(shape)

def head_sum_kernel(count, parts_ref, out_ref, slots, send_sems, recv_sems):
    me = lax.axis_index("head")
    row = lax.axis_index("seq")
    barrier = pltpu.get_barrier_semaphore()
    for shift in range(1, count):
        peer = (row, lax.rem(me + shift, count))
        pl.semaphore_signal(barrier, inc=1, device_id=peer, device_id_type=pl.DeviceIdType.MESH)
    pl.semaphore_wait(barrier, count - 1)
    copies = []
    for shift in range(1, count):
        copy = pltpu.make_async_remote_copy(
            src_ref=parts_ref,
            dst_ref=slots.at[me],
            send_sem=send_sems.at[shift],
            recv_sem=recv_sems.at[me],
            device_id=(row, lax.rem(me + shift, count)),
            device_id_type=pl.DeviceIdType.MESH,
        )
        copy.start()
        copies.append(copy)
    slots[me] = parts_ref[...]
    for shift in range(1, count):
        source = lax.rem(me + count - shift, count)
        pltpu.make_async_remote_copy(
            src_ref=parts_ref,
            dst_ref=slots.at[source],
            send_sem=send_sems.at[shift],
            recv_sem=recv_sems.at[source],
            device_id=(row, source),
            device_id_type=pl.DeviceIdType.MESH,
        ).wait_recv()
    total = slots[0]
    for index in range(1, count):
        total = total + slots[index]
    out_ref[...] = total
    for copy in copies:
        copy.wait_send()


def head_sum(square_sum, cross_sum):
    count = lax.axis_size("head")
    rows = square_sum.shape[0]
    parts = jnp.concatenate(
        [square_sum[None], cross_sum[None], jnp.zeros((6, rows), jnp.float32)], axis=0
    )
    total = pl.pallas_call(
        functools.partial(head_sum_kernel, count),
        out_shape=jax.ShapeDtypeStruct(parts.shape, jnp.float32),
        in_specs=[pl.BlockSpec(memory_space=pltpu.VMEM)],
        out_specs=pl.BlockSpec(memory_space=pltpu.VMEM),
        scratch_shapes=[
            pltpu.VMEM((count,) + parts.shape, jnp.float32),
            pltpu.SemaphoreType.DMA((count,)),
            pltpu.SemaphoreType.DMA((count,)),
        ],
        compiler_params=pltpu.CompilerParams(collective_id=2, has_side_effects=True),
    )(parts)
    return total[0], total[1]


def join_states(earlier_part, later_part):
    return (
        later_part[0] + (1.0 - later_part[1]) * earlier_part[0],
        jnp.maximum(earlier_part[1], later_part[1]),
    )


def split_state(state):
    upper = state.astype(jnp.bfloat16)
    lower = (state - upper.astype(jnp.float32)).astype(jnp.bfloat16)
    return (upper, lower)


def state_product(form, rows, state):
    upper, lower = split_state(state)
    first = jnp.einsum(form, rows, upper, preferred_element_type=jnp.float32)
    return first + jnp.einsum(form, rows, lower, preferred_element_type=jnp.float32)


def shards(queries, key_rows, value_rows, out_grad, norm_gain, dial_start, dial_end):
    token_count = queries.shape[0]
    head_count = queries.shape[1] // HD
    score_scale = HD ** (-0.5)
    width_all = HEADS * HD
    block_begin = lax.axis_index("seq") * token_count
    local_pos = jnp.arange(token_count, dtype=jnp.int32)
    position = block_begin + local_pos
    query_h = queries.reshape(token_count, head_count, HD)
    key_h = key_rows.reshape(token_count, head_count, HD)
    value_h = value_rows.reshape(token_count, head_count, HD)
    last_start = dial_start[token_count - 1]
    keep_last = position >= last_start
    element = jnp.einsum(
        "shd,she->hde",
        jnp.where(keep_last[:, None, None], key_h, jnp.zeros((), jnp.bfloat16)),
        value_h,
        preferred_element_type=jnp.float32,
    )
    block_index = lax.axis_index("seq")
    reach_back = block_index - dial_start[0] // token_count
    carried = scan_window(element, last_start < block_begin, reach_back, 1, 0)
    inside = (position[None, :] >= dial_start[:, None]) & (local_pos[None, :] <= local_pos[:, None])
    scores = jnp.einsum("thd,shd->hts", query_h, key_h, preferred_element_type=jnp.float32)
    weights = jnp.where(inside[None], score_scale * scores, 0.0).astype(jnp.bfloat16)
    local_mix = jnp.einsum("hts,she->the", weights, value_h, preferred_element_type=jnp.float32)
    across = score_scale * state_product("thd,hde->the", query_h, carried)
    from_before = (dial_start < block_begin).astype(jnp.float32)[:, None, None]
    attended = (local_mix + from_before * across).reshape(token_count, head_count * HD)
    grad_wide = out_grad.astype(jnp.float32)
    square_sum, cross_sum = head_sum(
        jnp.sum(attended * attended, axis=1), jnp.sum(norm_gain * grad_wide * attended, axis=1)
    )
    inv_rms = lax.rsqrt(square_sum / width_all + EPSILON)
    normed = (attended * inv_rms[:, None] * norm_gain).astype(jnp.bfloat16)
    grad_attn = (
        inv_rms[:, None] * norm_gain * grad_wide
        - attended * (inv_rms * inv_rms * inv_rms * cross_sum / width_all)[:, None]
    )
    grad_weight = grad_attn.astype(jnp.bfloat16).reshape(token_count, head_count, HD)
    first_end = dial_end[0]
    keep_first = position < first_end
    back_element = jnp.einsum(
        "thd,the->hde",
        jnp.where(keep_first[:, None, None], query_h, jnp.zeros((), jnp.bfloat16)),
        grad_weight,
        preferred_element_type=jnp.float32,
    )
    reach_ahead = (dial_end[token_count - 1] + token_count - 1) // token_count - 1 - block_index
    returned = scan_window(back_element, first_end > block_begin + token_count, reach_ahead, -1, 1)
    grad_scores = jnp.einsum(
        "the,she->hts", grad_weight, value_h, preferred_element_type=jnp.float32
    )
    grad_mix = jnp.where(inside[None], score_scale * grad_scores, 0.0).astype(jnp.bfloat16)
    to_after = (dial_end > block_begin + token_count).astype(jnp.float32)[:, None, None]
    query_grad = jnp.einsum(
        "hts,shd->thd", grad_mix, key_h, preferred_element_type=jnp.float32
    ) + from_before * score_scale * state_product("the,hde->thd", grad_weight, carried)
    key_grad = jnp.einsum(
        "hts,thd->shd", grad_mix, query_h, preferred_element_type=jnp.float32
    ) + to_after * score_scale * state_product("she,hde->shd", value_h, returned)
    value_grad = jnp.einsum(
        "hts,the->she", weights, grad_weight, preferred_element_type=jnp.float32
    ) + to_after * score_scale * state_product("shd,hde->she", key_h, returned)
    flat_shape = (token_count, head_count * HD)
    return (
        normed,
        query_grad.reshape(flat_shape).astype(jnp.bfloat16),
        key_grad.reshape(flat_shape).astype(jnp.bfloat16),
        value_grad.reshape(flat_shape).astype(jnp.bfloat16),
    )


def solution(mesh):
    placed = (
        P("seq", "head"),
        P("seq", "head"),
        P("seq", "head"),
        P("seq", "head"),
        P("head"),
        P("seq"),
        P("seq"),
    )
    return jax.shard_map(
        shards,
        mesh=mesh,
        in_specs=placed,
        out_specs=(P("seq", "head"), P("seq", "head"), P("seq", "head"), P("seq", "head")),
        check_vma=False,
    )
```

```python
import functools

import jax
import jax.numpy as jnp
from jax import lax
from jax.experimental import pallas as pl
from jax.experimental.pallas import tpu as pltpu
from jax.sharding import PartitionSpec as P

HEADS = 64
HD = 128
SPAN = 4
PIECES = 8


EPSILON = 1e-06


def from_behind(x, axis, by):
    count = lax.axis_size(axis)
    pairs = [(i, i + by) for i in range(count) if 0 <= i + by < count]
    return lax.ppermute(x, axis, pairs)


def scan_window_permutes(element, reach, step):
    nearest = from_behind(element, "seq", step)
    second = from_behind(nearest, "seq", step)
    pair = nearest + (reach >= 2).astype(jnp.float32) * second
    far_pair = from_behind(pair, "seq", 2 * step)
    total = pair + (reach >= 3).astype(jnp.float32) * far_pair
    return (reach >= 1).astype(jnp.float32) * total


def chain_kernel(count, step, flag_ref, element_ref, out_ref, link_slot, state_slot, sent_slot, send_sems, recv_sems):
    me = lax.axis_index("seq")
    head = lax.axis_index("head")
    heads = element_ref.shape[0]
    pos = lax.rem(me, 4) if step == 1 else 3 - lax.rem(me + 2, 4)
    ahead_exists = (me + step >= 0) & (me + step < count)
    behind_exists = (me - step >= 0) & (me - step < count)

    barrier = pltpu.get_barrier_semaphore()
    for offset in (1, -1):
        ring_peer = (lax.rem(me + offset + count, count), head)
        pl.semaphore_signal(barrier, inc=1, device_id=ring_peer, device_id_type=pl.DeviceIdType.MESH)
    pl.semaphore_wait(barrier, 2)

    def describe(kind, part, source, landing):
        return pltpu.make_async_remote_copy(
            src_ref=source,
            dst_ref=landing.at[part],
            send_sem=send_sems.at[kind, part],
            recv_sem=recv_sems.at[kind, part],
            device_id=(me + step, head),
            device_id_type=pl.DeviceIdType.MESH,
        )

    flag = flag_ref[0]
    sends = []
    for part in range(heads):
        @pl.when((pos >= 1) & behind_exists)
        def _():
            describe(0, part, link_slot.at[part], link_slot).wait_recv()
            link_slot[part] = element_ref[part] + flag * link_slot[part]

        @pl.when((pos == 0) | jnp.logical_not(behind_exists))
        def _():
            link_slot[part] = element_ref[part]

        into_link = describe(0, part, link_slot.at[part], link_slot)
        into_state = pltpu.make_async_remote_copy(
            src_ref=link_slot.at[part],
            dst_ref=state_slot.at[part],
            send_sem=send_sems.at[0, part],
            recv_sem=recv_sems.at[1, part],
            device_id=(me + step, head),
            device_id_type=pl.DeviceIdType.MESH,
        )

        @pl.when((pos <= 2) & ahead_exists)
        def _():
            into_link.start()

        @pl.when((pos == 3) & ahead_exists)
        def _():
            into_state.start()

        sends.append((into_link, into_state))
    state_sends = []
    for part in range(heads):
        @pl.when(behind_exists)
        def _():
            describe(1, part, state_slot.at[part], state_slot).wait_recv()

        @pl.when(jnp.logical_not(behind_exists))
        def _():
            state_slot[part] = jnp.zeros(state_slot.shape[1:], jnp.float32)

        out_ref[part] = state_slot[part]
        copy = describe(1, part, sent_slot.at[part], state_slot)

        @pl.when((pos <= 2) & ahead_exists)
        def _():
            sent_slot[part] = element_ref[part] + flag * state_slot[part]
            copy.start()

        state_sends.append(copy)
    for part in range(heads):
        into_link, into_state = sends[part]

        @pl.when((pos <= 2) & ahead_exists)
        def _():
            into_link.wait_send()

        @pl.when((pos == 3) & ahead_exists)
        def _():
            into_state.wait_send()

        @pl.when((pos <= 2) & ahead_exists)
        def _():
            state_sends[part].wait_send()


def scan_window(element, flag, reach, step, ident):
    count = lax.axis_size("seq")
    if count % 4:
        return scan_window_permutes(element, reach, step)
    shape = element.shape
    element = element.reshape(shape[0] * PIECES, shape[1] // PIECES, shape[2])
    heads = element.shape[0]
    return pl.pallas_call(
        functools.partial(chain_kernel, count, step),
        out_shape=jax.ShapeDtypeStruct(element.shape, jnp.float32),
        in_specs=[pl.BlockSpec(memory_space=pltpu.SMEM), pl.BlockSpec(memory_space=pltpu.VMEM)],
        out_specs=pl.BlockSpec(memory_space=pltpu.VMEM),
        scratch_shapes=[
            pltpu.VMEM(element.shape, jnp.float32),
            pltpu.VMEM(element.shape, jnp.float32),
            pltpu.VMEM(element.shape, jnp.float32),
            pltpu.SemaphoreType.DMA((2, heads)),
            pltpu.SemaphoreType.DMA((2, heads)),
        ],
        compiler_params=pltpu.CompilerParams(collective_id=ident, has_side_effects=True),
    )(flag.astype(jnp.float32).reshape(1), element).reshape(shape)

def head_sum_kernel(count, parts_ref, out_ref, slots, send_sems, recv_sems):
    me = lax.axis_index("head")
    row = lax.axis_index("seq")
    barrier = pltpu.get_barrier_semaphore()
    for shift in range(1, count):
        peer = (row, lax.rem(me + shift, count))
        pl.semaphore_signal(barrier, inc=1, device_id=peer, device_id_type=pl.DeviceIdType.MESH)
    pl.semaphore_wait(barrier, count - 1)
    copies = []
    for shift in range(1, count):
        copy = pltpu.make_async_remote_copy(
            src_ref=parts_ref,
            dst_ref=slots.at[me],
            send_sem=send_sems.at[shift],
            recv_sem=recv_sems.at[me],
            device_id=(row, lax.rem(me + shift, count)),
            device_id_type=pl.DeviceIdType.MESH,
        )
        copy.start()
        copies.append(copy)
    slots[me] = parts_ref[...]
    for shift in range(1, count):
        source = lax.rem(me + count - shift, count)
        pltpu.make_async_remote_copy(
            src_ref=parts_ref,
            dst_ref=slots.at[source],
            send_sem=send_sems.at[shift],
            recv_sem=recv_sems.at[source],
            device_id=(row, source),
            device_id_type=pl.DeviceIdType.MESH,
        ).wait_recv()
    total = slots[0]
    for index in range(1, count):
        total = total + slots[index]
    out_ref[...] = total
    for copy in copies:
        copy.wait_send()


def head_sum(square_sum, cross_sum):
    count = lax.axis_size("head")
    rows = square_sum.shape[0]
    parts = jnp.concatenate(
        [square_sum[None], cross_sum[None], jnp.zeros((6, rows), jnp.float32)], axis=0
    )
    total = pl.pallas_call(
        functools.partial(head_sum_kernel, count),
        out_shape=jax.ShapeDtypeStruct(parts.shape, jnp.float32),
        in_specs=[pl.BlockSpec(memory_space=pltpu.VMEM)],
        out_specs=pl.BlockSpec(memory_space=pltpu.VMEM),
        scratch_shapes=[
            pltpu.VMEM((count,) + parts.shape, jnp.float32),
            pltpu.SemaphoreType.DMA((count,)),
            pltpu.SemaphoreType.DMA((count,)),
        ],
        compiler_params=pltpu.CompilerParams(collective_id=2, has_side_effects=True),
    )(parts)
    return total[0], total[1]


def join_states(earlier_part, later_part):
    return (
        later_part[0] + (1.0 - later_part[1]) * earlier_part[0],
        jnp.maximum(earlier_part[1], later_part[1]),
    )


def split_state(state):
    upper = state.astype(jnp.bfloat16)
    lower = (state - upper.astype(jnp.float32)).astype(jnp.bfloat16)
    return (upper, lower)


def state_product(form, rows, state):
    upper, lower = split_state(state)
    first = jnp.einsum(form, rows, upper, preferred_element_type=jnp.float32)
    return first + jnp.einsum(form, rows, lower, preferred_element_type=jnp.float32)


def shards(queries, key_rows, value_rows, out_grad, norm_gain, dial_start, dial_end):
    token_count = queries.shape[0]
    head_count = queries.shape[1] // HD
    score_scale = HD ** (-0.5)
    width_all = HEADS * HD
    block_begin = lax.axis_index("seq") * token_count
    local_pos = jnp.arange(token_count, dtype=jnp.int32)
    position = block_begin + local_pos
    query_h = queries.reshape(token_count, head_count, HD)
    key_h = key_rows.reshape(token_count, head_count, HD)
    value_h = value_rows.reshape(token_count, head_count, HD)
    last_start = dial_start[token_count - 1]
    keep_last = position >= last_start
    element = jnp.einsum(
        "shd,she->hde",
        jnp.where(keep_last[:, None, None], key_h, jnp.zeros((), jnp.bfloat16)),
        value_h,
        preferred_element_type=jnp.float32,
    )
    block_index = lax.axis_index("seq")
    reach_back = block_index - dial_start[0] // token_count
    carried = scan_window(element, last_start < block_begin, reach_back, 1, 0)
    inside = (position[None, :] >= dial_start[:, None]) & (local_pos[None, :] <= local_pos[:, None])
    scores = jnp.einsum("thd,shd->hts", query_h, key_h, preferred_element_type=jnp.float32)
    weights = jnp.where(inside[None], score_scale * scores, 0.0).astype(jnp.bfloat16)
    local_mix = jnp.einsum("hts,she->the", weights, value_h, preferred_element_type=jnp.float32)
    across = score_scale * state_product("thd,hde->the", query_h, carried)
    from_before = (dial_start < block_begin).astype(jnp.float32)[:, None, None]
    attended = (local_mix + from_before * across).reshape(token_count, head_count * HD)
    grad_wide = out_grad.astype(jnp.float32)
    square_sum, cross_sum = head_sum(
        jnp.sum(attended * attended, axis=1), jnp.sum(norm_gain * grad_wide * attended, axis=1)
    )
    inv_rms = lax.rsqrt(square_sum / width_all + EPSILON)
    normed = (attended * inv_rms[:, None] * norm_gain).astype(jnp.bfloat16)
    grad_attn = (
        inv_rms[:, None] * norm_gain * grad_wide
        - attended * (inv_rms * inv_rms * inv_rms * cross_sum / width_all)[:, None]
    )
    grad_weight = grad_attn.astype(jnp.bfloat16).reshape(token_count, head_count, HD)
    first_end = dial_end[0]
    keep_first = position < first_end
    back_element = jnp.einsum(
        "thd,the->hde",
        jnp.where(keep_first[:, None, None], query_h, jnp.zeros((), jnp.bfloat16)),
        grad_weight,
        preferred_element_type=jnp.float32,
    )
    reach_ahead = (dial_end[token_count - 1] + token_count - 1) // token_count - 1 - block_index
    returned = scan_window(back_element, first_end > block_begin + token_count, reach_ahead, -1, 1)
    grad_scores = jnp.einsum(
        "the,she->hts", grad_weight, value_h, preferred_element_type=jnp.float32
    )
    grad_mix = jnp.where(inside[None], score_scale * grad_scores, 0.0).astype(jnp.bfloat16)
    to_after = (dial_end > block_begin + token_count).astype(jnp.float32)[:, None, None]
    query_grad = jnp.einsum(
        "hts,shd->thd", grad_mix, key_h, preferred_element_type=jnp.float32
    ) + from_before * score_scale * state_product("the,hde->thd", grad_weight, carried)
    key_grad = jnp.einsum(
        "hts,thd->shd", grad_mix, query_h, preferred_element_type=jnp.float32
    ) + to_after * score_scale * state_product("she,hde->shd", value_h, returned)
    value_grad = jnp.einsum(
        "hts,the->she", weights, grad_weight, preferred_element_type=jnp.float32
    ) + to_after * score_scale * state_product("shd,hde->she", key_h, returned)
    flat_shape = (token_count, head_count * HD)
    return (
        normed,
        query_grad.reshape(flat_shape).astype(jnp.bfloat16),
        key_grad.reshape(flat_shape).astype(jnp.bfloat16),
        value_grad.reshape(flat_shape).astype(jnp.bfloat16),
    )


def solution(mesh):
    placed = (
        P("seq", "head"),
        P("seq", "head"),
        P("seq", "head"),
        P("seq", "head"),
        P("head"),
        P("seq"),
        P("seq"),
    )
    return jax.shard_map(
        shards,
        mesh=mesh,
        in_specs=placed,
        out_specs=(P("seq", "head"), P("seq", "head"), P("seq", "head"), P("seq", "head")),
        check_vma=False,
    )
```

```python
import functools

import jax
import jax.numpy as jnp
from jax import lax
from jax.experimental import pallas as pl
from jax.experimental.pallas import tpu as pltpu
from jax.sharding import PartitionSpec as P

HEADS = 64
HD = 128
SPAN = 4
PIECES = 4


EPSILON = 1e-06


def from_behind(x, axis, by):
    count = lax.axis_size(axis)
    pairs = [(i, i + by) for i in range(count) if 0 <= i + by < count]
    return lax.ppermute(x, axis, pairs)


def scan_window_permutes(element, reach, step):
    nearest = from_behind(element, "seq", step)
    second = from_behind(nearest, "seq", step)
    pair = nearest + (reach >= 2).astype(jnp.float32) * second
    far_pair = from_behind(pair, "seq", 2 * step)
    total = pair + (reach >= 3).astype(jnp.float32) * far_pair
    return (reach >= 1).astype(jnp.float32) * total


def chain_kernel(count, step, flag_ref, element_ref, out_ref, link_slot, state_slot, sent_slot, send_sems, recv_sems):
    me = lax.axis_index("seq")
    head = lax.axis_index("head")
    heads = element_ref.shape[0]
    pos = lax.rem(me, 4) if step == 1 else 3 - lax.rem(me + 2, 4)
    ahead_exists = (me + step >= 0) & (me + step < count)
    behind_exists = (me - step >= 0) & (me - step < count)

    barrier = pltpu.get_barrier_semaphore()
    for offset in (1, -1):
        ring_peer = (lax.rem(me + offset + count, count), head)
        pl.semaphore_signal(barrier, inc=1, device_id=ring_peer, device_id_type=pl.DeviceIdType.MESH)
    pl.semaphore_wait(barrier, 2)

    def describe(kind, part, source, landing):
        return pltpu.make_async_remote_copy(
            src_ref=source,
            dst_ref=landing.at[part],
            send_sem=send_sems.at[kind, part],
            recv_sem=recv_sems.at[kind, part],
            device_id=(me + step, head),
            device_id_type=pl.DeviceIdType.MESH,
        )

    flag = flag_ref[0]
    sends = []
    for part in range(heads):
        @pl.when((pos >= 1) & behind_exists)
        def _():
            describe(0, part, link_slot.at[part], link_slot).wait_recv()
            link_slot[part] = element_ref[part] + flag * link_slot[part]

        @pl.when((pos == 0) | jnp.logical_not(behind_exists))
        def _():
            link_slot[part] = element_ref[part]

        into_link = describe(0, part, link_slot.at[part], link_slot)
        into_state = pltpu.make_async_remote_copy(
            src_ref=link_slot.at[part],
            dst_ref=state_slot.at[part],
            send_sem=send_sems.at[0, part],
            recv_sem=recv_sems.at[1, part],
            device_id=(me + step, head),
            device_id_type=pl.DeviceIdType.MESH,
        )

        @pl.when((pos <= 2) & ahead_exists)
        def _():
            into_link.start()

        @pl.when((pos == 3) & ahead_exists)
        def _():
            into_state.start()

        sends.append((into_link, into_state))
    state_sends = []
    for part in range(heads):
        @pl.when(behind_exists)
        def _():
            describe(1, part, state_slot.at[part], state_slot).wait_recv()

        @pl.when(jnp.logical_not(behind_exists))
        def _():
            state_slot[part] = jnp.zeros(state_slot.shape[1:], jnp.float32)

        out_ref[part] = state_slot[part]
        copy = describe(1, part, sent_slot.at[part], state_slot)

        @pl.when((pos <= 2) & ahead_exists)
        def _():
            sent_slot[part] = element_ref[part] + flag * state_slot[part]
            copy.start()

        state_sends.append(copy)
    for part in range(heads):
        into_link, into_state = sends[part]

        @pl.when((pos <= 2) & ahead_exists)
        def _():
            into_link.wait_send()

        @pl.when((pos == 3) & ahead_exists)
        def _():
            into_state.wait_send()

        @pl.when((pos <= 2) & ahead_exists)
        def _():
            state_sends[part].wait_send()


def scan_window(element, flag, reach, step, ident):
    count = lax.axis_size("seq")
    if count % 4:
        return scan_window_permutes(element, reach, step)
    shape = element.shape
    element = element.reshape(shape[0] * PIECES, shape[1] // PIECES, shape[2])
    heads = element.shape[0]
    return pl.pallas_call(
        functools.partial(chain_kernel, count, step),
        out_shape=jax.ShapeDtypeStruct(element.shape, jnp.float32),
        in_specs=[pl.BlockSpec(memory_space=pltpu.SMEM), pl.BlockSpec(memory_space=pltpu.VMEM)],
        out_specs=pl.BlockSpec(memory_space=pltpu.VMEM),
        scratch_shapes=[
            pltpu.VMEM(element.shape, jnp.float32),
            pltpu.VMEM(element.shape, jnp.float32),
            pltpu.VMEM(element.shape, jnp.float32),
            pltpu.SemaphoreType.DMA((2, heads)),
            pltpu.SemaphoreType.DMA((2, heads)),
        ],
        compiler_params=pltpu.CompilerParams(collective_id=ident, has_side_effects=True),
    )(flag.astype(jnp.float32).reshape(1), element).reshape(shape)

def head_sum_kernel(count, parts_ref, out_ref, slots, send_sems, recv_sems):
    me = lax.axis_index("head")
    row = lax.axis_index("seq")
    barrier = pltpu.get_barrier_semaphore()
    for shift in range(1, count):
        peer = (row, lax.rem(me + shift, count))
        pl.semaphore_signal(barrier, inc=1, device_id=peer, device_id_type=pl.DeviceIdType.MESH)
    pl.semaphore_wait(barrier, count - 1)
    copies = []
    for shift in range(1, count):
        copy = pltpu.make_async_remote_copy(
            src_ref=parts_ref,
            dst_ref=slots.at[me],
            send_sem=send_sems.at[shift],
            recv_sem=recv_sems.at[me],
            device_id=(row, lax.rem(me + shift, count)),
            device_id_type=pl.DeviceIdType.MESH,
        )
        copy.start()
        copies.append(copy)
    slots[me] = parts_ref[...]
    for shift in range(1, count):
        source = lax.rem(me + count - shift, count)
        pltpu.make_async_remote_copy(
            src_ref=parts_ref,
            dst_ref=slots.at[source],
            send_sem=send_sems.at[shift],
            recv_sem=recv_sems.at[source],
            device_id=(row, source),
            device_id_type=pl.DeviceIdType.MESH,
        ).wait_recv()
    total = slots[0]
    for index in range(1, count):
        total = total + slots[index]
    out_ref[...] = total
    for copy in copies:
        copy.wait_send()


def head_sum(square_sum, cross_sum):
    count = lax.axis_size("head")
    rows = square_sum.shape[0]
    parts = jnp.concatenate(
        [square_sum[None], cross_sum[None], jnp.zeros((6, rows), jnp.float32)], axis=0
    )
    total = pl.pallas_call(
        functools.partial(head_sum_kernel, count),
        out_shape=jax.ShapeDtypeStruct(parts.shape, jnp.float32),
        in_specs=[pl.BlockSpec(memory_space=pltpu.VMEM)],
        out_specs=pl.BlockSpec(memory_space=pltpu.VMEM),
        scratch_shapes=[
            pltpu.VMEM((count,) + parts.shape, jnp.float32),
            pltpu.SemaphoreType.DMA((count,)),
            pltpu.SemaphoreType.DMA((count,)),
        ],
        compiler_params=pltpu.CompilerParams(collective_id=2, has_side_effects=True),
    )(parts)
    return total[0], total[1]


def gradient_kernel(scale, query_ref, key_ref, value_ref, grad_ref, inside_ref, before_ref, after_ref,
                    carried_ref, returned_ref, query_out, key_out, value_out):
    inside = inside_ref[...] > 0.5
    before = before_ref[...]
    after = after_ref[...]
    contract_last = (((1,), (1,)), ((), ()))

    def halves(state):
        upper = state.astype(jnp.bfloat16)
        return upper, (state - upper.astype(jnp.float32)).astype(jnp.bfloat16)

    def across(rows, state, form):
        upper, lower = halves(state)
        if form == "nt":
            first = lax.dot_general(rows, upper, contract_last, preferred_element_type=jnp.float32)
            return first + lax.dot_general(rows, lower, contract_last, preferred_element_type=jnp.float32)
        first = jnp.dot(rows, upper, preferred_element_type=jnp.float32)
        return first + jnp.dot(rows, lower, preferred_element_type=jnp.float32)

    for part in range(query_ref.shape[1] // HD):
        cols = pl.ds(part * HD, HD)
        query_h = query_ref[:, cols]
        key_h = key_ref[:, cols]
        value_h = value_ref[:, cols]
        grad_h = grad_ref[:, cols]
        scores = lax.dot_general(query_h, key_h, contract_last, preferred_element_type=jnp.float32)
        scaled = jnp.where(inside, scale * scores, 0.0)
        grad_scores = lax.dot_general(grad_h, value_h, contract_last, preferred_element_type=jnp.float32)
        mixed = jnp.where(inside, scale * grad_scores, 0.0)
        carried = carried_ref[part]
        returned = returned_ref[part]
        query_out[:, cols] = (
            jnp.dot(mixed.astype(jnp.bfloat16), key_h, preferred_element_type=jnp.float32)
            + before * scale * across(grad_h, carried, "nt")
        ).astype(jnp.bfloat16)
        key_out[:, cols] = (
            jnp.dot(mixed.T.astype(jnp.bfloat16), query_h, preferred_element_type=jnp.float32)
            + after * scale * across(value_h, returned, "nt")
        ).astype(jnp.bfloat16)
        value_out[:, cols] = (
            jnp.dot(scaled.T.astype(jnp.bfloat16), grad_h, preferred_element_type=jnp.float32)
            + after * scale * across(key_h, returned, "nn")
        ).astype(jnp.bfloat16)


def gradients(scale, queries, key_rows, value_rows, grad_flat, inside, before, after, carried, returned):
    flat = jax.ShapeDtypeStruct(queries.shape, jnp.bfloat16)
    vmem = pl.BlockSpec(memory_space=pltpu.VMEM)
    rows = queries.shape[0]
    wide = lambda mask: jnp.broadcast_to(mask.astype(jnp.float32)[:, None], (rows, HD))
    return pl.pallas_call(
        functools.partial(gradient_kernel, scale),
        out_shape=(flat, flat, flat),
        in_specs=[vmem] * 9,
        out_specs=(vmem, vmem, vmem),
    )(queries, key_rows, value_rows, grad_flat, inside.astype(jnp.float32), wide(before), wide(after), carried, returned)


def join_states(earlier_part, later_part):
    return (
        later_part[0] + (1.0 - later_part[1]) * earlier_part[0],
        jnp.maximum(earlier_part[1], later_part[1]),
    )


def split_state(state):
    upper = state.astype(jnp.bfloat16)
    lower = (state - upper.astype(jnp.float32)).astype(jnp.bfloat16)
    return (upper, lower)


def state_product(form, rows, state):
    upper, lower = split_state(state)
    first = jnp.einsum(form, rows, upper, preferred_element_type=jnp.float32)
    return first + jnp.einsum(form, rows, lower, preferred_element_type=jnp.float32)


def shards(queries, key_rows, value_rows, out_grad, norm_gain, dial_start, dial_end):
    token_count = queries.shape[0]
    head_count = queries.shape[1] // HD
    score_scale = HD ** (-0.5)
    width_all = HEADS * HD
    block_begin = lax.axis_index("seq") * token_count
    local_pos = jnp.arange(token_count, dtype=jnp.int32)
    position = block_begin + local_pos
    query_h = queries.reshape(token_count, head_count, HD)
    key_h = key_rows.reshape(token_count, head_count, HD)
    value_h = value_rows.reshape(token_count, head_count, HD)
    last_start = dial_start[token_count - 1]
    keep_last = position >= last_start
    element = jnp.einsum(
        "shd,she->hde",
        jnp.where(keep_last[:, None, None], key_h, jnp.zeros((), jnp.bfloat16)),
        value_h,
        preferred_element_type=jnp.float32,
    )
    block_index = lax.axis_index("seq")
    reach_back = block_index - dial_start[0] // token_count
    carried = scan_window(element, last_start < block_begin, reach_back, 1, 0)
    inside = (position[None, :] >= dial_start[:, None]) & (local_pos[None, :] <= local_pos[:, None])
    scores = jnp.einsum("thd,shd->hts", query_h, key_h, preferred_element_type=jnp.float32)
    weights = jnp.where(inside[None], score_scale * scores, 0.0).astype(jnp.bfloat16)
    local_mix = jnp.einsum("hts,she->the", weights, value_h, preferred_element_type=jnp.float32)
    across = score_scale * state_product("thd,hde->the", query_h, carried)
    from_before = (dial_start < block_begin).astype(jnp.float32)[:, None, None]
    attended = (local_mix + from_before * across).reshape(token_count, head_count * HD)
    grad_wide = out_grad.astype(jnp.float32)
    square_sum, cross_sum = head_sum(
        jnp.sum(attended * attended, axis=1), jnp.sum(norm_gain * grad_wide * attended, axis=1)
    )
    inv_rms = lax.rsqrt(square_sum / width_all + EPSILON)
    normed = (attended * inv_rms[:, None] * norm_gain).astype(jnp.bfloat16)
    grad_attn = (
        inv_rms[:, None] * norm_gain * grad_wide
        - attended * (inv_rms * inv_rms * inv_rms * cross_sum / width_all)[:, None]
    )
    grad_weight = grad_attn.astype(jnp.bfloat16).reshape(token_count, head_count, HD)
    first_end = dial_end[0]
    keep_first = position < first_end
    back_element = jnp.einsum(
        "thd,the->hde",
        jnp.where(keep_first[:, None, None], query_h, jnp.zeros((), jnp.bfloat16)),
        grad_weight,
        preferred_element_type=jnp.float32,
    )
    reach_ahead = (dial_end[token_count - 1] + token_count - 1) // token_count - 1 - block_index
    returned = scan_window(back_element, first_end > block_begin + token_count, reach_ahead, -1, 1)
    query_grad, key_grad, value_grad = gradients(
        score_scale, queries, key_rows, value_rows, grad_weight.reshape(queries.shape), inside,
        dial_start < block_begin, dial_end > block_begin + token_count, carried, returned,
    )
    return (normed, query_grad, key_grad, value_grad)


def solution(mesh):
    placed = (
        P("seq", "head"),
        P("seq", "head"),
        P("seq", "head"),
        P("seq", "head"),
        P("head"),
        P("seq"),
        P("seq"),
    )
    return jax.shard_map(
        shards,
        mesh=mesh,
        in_specs=placed,
        out_specs=(P("seq", "head"), P("seq", "head"), P("seq", "head"), P("seq", "head")),
        check_vma=False,
    )
```

```python
import functools

import jax
import jax.numpy as jnp
from jax import lax
from jax.experimental import pallas as pl
from jax.experimental.pallas import tpu as pltpu
from jax.sharding import PartitionSpec as P

HEADS = 64
HD = 128
SPAN = 4
PIECES = 4


EPSILON = 1e-06


def from_behind(x, axis, by):
    count = lax.axis_size(axis)
    pairs = [(i, i + by) for i in range(count) if 0 <= i + by < count]
    return lax.ppermute(x, axis, pairs)


def scan_window_permutes(element, reach, step):
    nearest = from_behind(element, "seq", step)
    second = from_behind(nearest, "seq", step)
    pair = nearest + (reach >= 2).astype(jnp.float32) * second
    far_pair = from_behind(pair, "seq", 2 * step)
    total = pair + (reach >= 3).astype(jnp.float32) * far_pair
    return (reach >= 1).astype(jnp.float32) * total


def chain_kernel(count, step, side_work, extra_in, flag_ref, element_ref, *refs):
    side_in = refs[:extra_in]
    out_ref = refs[extra_in]
    link_slot, state_slot, sent_slot, send_sems, recv_sems = refs[-5:]
    side_out = refs[extra_in + 1:-5]
    me = lax.axis_index("seq")
    head = lax.axis_index("head")
    heads = element_ref.shape[0]
    pos = lax.rem(me, 4) if step == 1 else 3 - lax.rem(me + 2, 4)
    ahead_exists = (me + step >= 0) & (me + step < count)
    behind_exists = (me - step >= 0) & (me - step < count)

    barrier = pltpu.get_barrier_semaphore()
    for offset in (1, -1):
        ring_peer = (lax.rem(me + offset + count, count), head)
        pl.semaphore_signal(barrier, inc=1, device_id=ring_peer, device_id_type=pl.DeviceIdType.MESH)
    pl.semaphore_wait(barrier, 2)

    def describe(kind, part, source, landing):
        return pltpu.make_async_remote_copy(
            src_ref=source,
            dst_ref=landing.at[part],
            send_sem=send_sems.at[kind, part],
            recv_sem=recv_sems.at[kind, part],
            device_id=(me + step, head),
            device_id_type=pl.DeviceIdType.MESH,
        )

    flag = flag_ref[0]
    sends = []
    for part in range(heads):
        @pl.when((pos >= 1) & behind_exists)
        def _():
            describe(0, part, link_slot.at[part], link_slot).wait_recv()
            link_slot[part] = element_ref[part] + flag * link_slot[part]

        @pl.when((pos == 0) | jnp.logical_not(behind_exists))
        def _():
            link_slot[part] = element_ref[part]

        into_link = describe(0, part, link_slot.at[part], link_slot)
        into_state = pltpu.make_async_remote_copy(
            src_ref=link_slot.at[part],
            dst_ref=state_slot.at[part],
            send_sem=send_sems.at[0, part],
            recv_sem=recv_sems.at[1, part],
            device_id=(me + step, head),
            device_id_type=pl.DeviceIdType.MESH,
        )

        @pl.when((pos <= 2) & ahead_exists)
        def _():
            into_link.start()

        @pl.when((pos == 3) & ahead_exists)
        def _():
            into_state.start()

        sends.append((into_link, into_state))
    side_work(side_in, side_out)
    state_sends = []
    for part in range(heads):
        @pl.when(behind_exists)
        def _():
            describe(1, part, state_slot.at[part], state_slot).wait_recv()

        @pl.when(jnp.logical_not(behind_exists))
        def _():
            state_slot[part] = jnp.zeros(state_slot.shape[1:], jnp.float32)

        out_ref[part] = state_slot[part]
        copy = describe(1, part, sent_slot.at[part], state_slot)

        @pl.when((pos <= 2) & ahead_exists)
        def _():
            sent_slot[part] = element_ref[part] + flag * state_slot[part]
            copy.start()

        state_sends.append(copy)
    for part in range(heads):
        into_link, into_state = sends[part]

        @pl.when((pos <= 2) & ahead_exists)
        def _():
            into_link.wait_send()

        @pl.when((pos == 3) & ahead_exists)
        def _():
            into_state.wait_send()

        @pl.when((pos <= 2) & ahead_exists)
        def _():
            state_sends[part].wait_send()


def no_side_work(side_in, side_out):
    del side_in, side_out


def backward_local(scale, side_in, side_out):
    query_ref, key_ref, value_ref, grad_ref, inside_ref = side_in
    query_out, key_out, value_out = side_out
    inside = inside_ref[...] > 0.5
    contract_last = (((1,), (1,)), ((), ()))
    for part in range(query_ref.shape[1] // HD):
        cols = pl.ds(part * HD, HD)
        query_h = query_ref[:, cols]
        key_h = key_ref[:, cols]
        grad_h = grad_ref[:, cols]
        scores = lax.dot_general(query_h, key_h, contract_last, preferred_element_type=jnp.float32)
        scaled = jnp.where(inside, scale * scores, 0.0)
        grad_scores = lax.dot_general(
            grad_h, value_ref[:, cols], contract_last, preferred_element_type=jnp.float32
        )
        mixed = jnp.where(inside, scale * grad_scores, 0.0)
        query_out[:, cols] = jnp.dot(mixed.astype(jnp.bfloat16), key_h, preferred_element_type=jnp.float32)
        key_out[:, cols] = jnp.dot(mixed.T.astype(jnp.bfloat16), query_h, preferred_element_type=jnp.float32)
        value_out[:, cols] = jnp.dot(scaled.T.astype(jnp.bfloat16), grad_h, preferred_element_type=jnp.float32)


def scan_window(element, flag, step, ident, side_work=no_side_work, side_inputs=(), side_shapes=()):
    count = lax.axis_size("seq")
    shape = element.shape
    element = element.reshape(shape[0] * PIECES, shape[1] // PIECES, shape[2])
    heads = element.shape[0]
    vmem = pl.BlockSpec(memory_space=pltpu.VMEM)
    outs = pl.pallas_call(
        functools.partial(chain_kernel, count, step, side_work, len(side_inputs)),
        out_shape=(jax.ShapeDtypeStruct(element.shape, jnp.float32),) + tuple(side_shapes),
        in_specs=[pl.BlockSpec(memory_space=pltpu.SMEM)] + [vmem] * (1 + len(side_inputs)),
        out_specs=(vmem,) * (1 + len(side_shapes)),
        scratch_shapes=[
            pltpu.VMEM(element.shape, jnp.float32),
            pltpu.VMEM(element.shape, jnp.float32),
            pltpu.VMEM(element.shape, jnp.float32),
            pltpu.SemaphoreType.DMA((2, heads)),
            pltpu.SemaphoreType.DMA((2, heads)),
        ],
        compiler_params=pltpu.CompilerParams(collective_id=ident, has_side_effects=True),
    )(flag.astype(jnp.float32).reshape(1), element, *side_inputs)
    return (outs[0].reshape(shape),) + tuple(outs[1:])

def head_sum_kernel(count, parts_ref, out_ref, slots, send_sems, recv_sems):
    me = lax.axis_index("head")
    row = lax.axis_index("seq")
    barrier = pltpu.get_barrier_semaphore()
    for shift in range(1, count):
        peer = (row, lax.rem(me + shift, count))
        pl.semaphore_signal(barrier, inc=1, device_id=peer, device_id_type=pl.DeviceIdType.MESH)
    pl.semaphore_wait(barrier, count - 1)
    copies = []
    for shift in range(1, count):
        copy = pltpu.make_async_remote_copy(
            src_ref=parts_ref,
            dst_ref=slots.at[me],
            send_sem=send_sems.at[shift],
            recv_sem=recv_sems.at[me],
            device_id=(row, lax.rem(me + shift, count)),
            device_id_type=pl.DeviceIdType.MESH,
        )
        copy.start()
        copies.append(copy)
    slots[me] = parts_ref[...]
    for shift in range(1, count):
        source = lax.rem(me + count - shift, count)
        pltpu.make_async_remote_copy(
            src_ref=parts_ref,
            dst_ref=slots.at[source],
            send_sem=send_sems.at[shift],
            recv_sem=recv_sems.at[source],
            device_id=(row, source),
            device_id_type=pl.DeviceIdType.MESH,
        ).wait_recv()
    total = slots[0]
    for index in range(1, count):
        total = total + slots[index]
    out_ref[...] = total
    for copy in copies:
        copy.wait_send()


def head_sum(square_sum, cross_sum):
    count = lax.axis_size("head")
    rows = square_sum.shape[0]
    parts = jnp.concatenate(
        [square_sum[None], cross_sum[None], jnp.zeros((6, rows), jnp.float32)], axis=0
    )
    total = pl.pallas_call(
        functools.partial(head_sum_kernel, count),
        out_shape=jax.ShapeDtypeStruct(parts.shape, jnp.float32),
        in_specs=[pl.BlockSpec(memory_space=pltpu.VMEM)],
        out_specs=pl.BlockSpec(memory_space=pltpu.VMEM),
        scratch_shapes=[
            pltpu.VMEM((count,) + parts.shape, jnp.float32),
            pltpu.SemaphoreType.DMA((count,)),
            pltpu.SemaphoreType.DMA((count,)),
        ],
        compiler_params=pltpu.CompilerParams(collective_id=2, has_side_effects=True),
    )(parts)
    return total[0], total[1]


def gradient_kernel(scale, query_ref, key_ref, value_ref, grad_ref, before_ref, after_ref,
                    carried_ref, returned_ref, query_local, key_local, value_local,
                    query_out, key_out, value_out):
    before = before_ref[...]
    after = after_ref[...]
    contract_last = (((1,), (1,)), ((), ()))

    def halves(state):
        upper = state.astype(jnp.bfloat16)
        return upper, (state - upper.astype(jnp.float32)).astype(jnp.bfloat16)

    def across(rows, state, form):
        upper, lower = halves(state)
        if form == "nt":
            first = lax.dot_general(rows, upper, contract_last, preferred_element_type=jnp.float32)
            return first + lax.dot_general(rows, lower, contract_last, preferred_element_type=jnp.float32)
        first = jnp.dot(rows, upper, preferred_element_type=jnp.float32)
        return first + jnp.dot(rows, lower, preferred_element_type=jnp.float32)

    for part in range(query_ref.shape[1] // HD):
        cols = pl.ds(part * HD, HD)
        carried = carried_ref[part]
        returned = returned_ref[part]
        query_out[:, cols] = (
            query_local[:, cols] + before * scale * across(grad_ref[:, cols], carried, "nt")
        ).astype(jnp.bfloat16)
        key_out[:, cols] = (
            key_local[:, cols] + after * scale * across(value_ref[:, cols], returned, "nt")
        ).astype(jnp.bfloat16)
        value_out[:, cols] = (
            value_local[:, cols] + after * scale * across(key_ref[:, cols], returned, "nn")
        ).astype(jnp.bfloat16)


def gradients(scale, queries, key_rows, value_rows, grad_flat, before, after, carried, returned, local):
    flat = jax.ShapeDtypeStruct(queries.shape, jnp.bfloat16)
    vmem = pl.BlockSpec(memory_space=pltpu.VMEM)
    rows = queries.shape[0]
    wide = lambda mask: jnp.broadcast_to(mask.astype(jnp.float32)[:, None], (rows, HD))
    return pl.pallas_call(
        functools.partial(gradient_kernel, scale),
        out_shape=(flat, flat, flat),
        in_specs=[vmem] * 11,
        out_specs=(vmem, vmem, vmem),
    )(queries, key_rows, value_rows, grad_flat, wide(before), wide(after), carried, returned, *local)

def join_states(earlier_part, later_part):
    return (
        later_part[0] + (1.0 - later_part[1]) * earlier_part[0],
        jnp.maximum(earlier_part[1], later_part[1]),
    )


def split_state(state):
    upper = state.astype(jnp.bfloat16)
    lower = (state - upper.astype(jnp.float32)).astype(jnp.bfloat16)
    return (upper, lower)


def state_product(form, rows, state):
    upper, lower = split_state(state)
    first = jnp.einsum(form, rows, upper, preferred_element_type=jnp.float32)
    return first + jnp.einsum(form, rows, lower, preferred_element_type=jnp.float32)


def shards(queries, key_rows, value_rows, out_grad, norm_gain, dial_start, dial_end):
    token_count = queries.shape[0]
    head_count = queries.shape[1] // HD
    score_scale = HD ** (-0.5)
    width_all = HEADS * HD
    block_begin = lax.axis_index("seq") * token_count
    local_pos = jnp.arange(token_count, dtype=jnp.int32)
    position = block_begin + local_pos
    query_h = queries.reshape(token_count, head_count, HD)
    key_h = key_rows.reshape(token_count, head_count, HD)
    value_h = value_rows.reshape(token_count, head_count, HD)
    last_start = dial_start[token_count - 1]
    keep_last = position >= last_start
    element = jnp.einsum(
        "shd,she->hde",
        jnp.where(keep_last[:, None, None], key_h, jnp.zeros((), jnp.bfloat16)),
        value_h,
        preferred_element_type=jnp.float32,
    )
    carried = scan_window(element, last_start < block_begin, 1, 0)[0]
    inside = (position[None, :] >= dial_start[:, None]) & (local_pos[None, :] <= local_pos[:, None])
    scores = jnp.einsum("thd,shd->hts", query_h, key_h, preferred_element_type=jnp.float32)
    weights = jnp.where(inside[None], score_scale * scores, 0.0).astype(jnp.bfloat16)
    local_mix = jnp.einsum("hts,she->the", weights, value_h, preferred_element_type=jnp.float32)
    across = score_scale * state_product("thd,hde->the", query_h, carried)
    from_before = (dial_start < block_begin).astype(jnp.float32)[:, None, None]
    attended = (local_mix + from_before * across).reshape(token_count, head_count * HD)
    grad_wide = out_grad.astype(jnp.float32)
    square_sum, cross_sum = head_sum(
        jnp.sum(attended * attended, axis=1), jnp.sum(norm_gain * grad_wide * attended, axis=1)
    )
    inv_rms = lax.rsqrt(square_sum / width_all + EPSILON)
    normed = (attended * inv_rms[:, None] * norm_gain).astype(jnp.bfloat16)
    grad_attn = (
        inv_rms[:, None] * norm_gain * grad_wide
        - attended * (inv_rms * inv_rms * inv_rms * cross_sum / width_all)[:, None]
    )
    grad_weight = grad_attn.astype(jnp.bfloat16).reshape(token_count, head_count, HD)
    first_end = dial_end[0]
    keep_first = position < first_end
    back_element = jnp.einsum(
        "thd,the->hde",
        jnp.where(keep_first[:, None, None], query_h, jnp.zeros((), jnp.bfloat16)),
        grad_weight,
        preferred_element_type=jnp.float32,
    )
    wide_shape = jax.ShapeDtypeStruct(queries.shape, jnp.float32)
    grad_flat = grad_weight.reshape(queries.shape)
    returned, *local = scan_window(
        back_element, first_end > block_begin + token_count, -1, 1,
        functools.partial(backward_local, score_scale),
        (queries, key_rows, value_rows, grad_flat, inside.astype(jnp.float32)),
        (wide_shape,) * 3,
    )
    query_grad, key_grad, value_grad = gradients(
        score_scale, queries, key_rows, value_rows, grad_flat,
        dial_start < block_begin, dial_end > block_begin + token_count, carried, returned, local,
    )
    return (normed, query_grad, key_grad, value_grad)


def solution(mesh):
    placed = (
        P("seq", "head"),
        P("seq", "head"),
        P("seq", "head"),
        P("seq", "head"),
        P("head"),
        P("seq"),
        P("seq"),
    )
    return jax.shard_map(
        shards,
        mesh=mesh,
        in_specs=placed,
        out_specs=(P("seq", "head"), P("seq", "head"), P("seq", "head"), P("seq", "head")),
        check_vma=False,
    )
```

```python
import functools

import jax
import jax.numpy as jnp
from jax import lax
from jax.experimental import pallas as pl
from jax.experimental.pallas import tpu as pltpu
from jax.sharding import PartitionSpec as P

HEADS = 64
HD = 128
SPAN = 4
PIECES = 4


EPSILON = 1e-06


def from_behind(x, axis, by):
    count = lax.axis_size(axis)
    pairs = [(i, i + by) for i in range(count) if 0 <= i + by < count]
    return lax.ppermute(x, axis, pairs)


def scan_window_permutes(element, reach, step):
    nearest = from_behind(element, "seq", step)
    second = from_behind(nearest, "seq", step)
    pair = nearest + (reach >= 2).astype(jnp.float32) * second
    far_pair = from_behind(pair, "seq", 2 * step)
    total = pair + (reach >= 3).astype(jnp.float32) * far_pair
    return (reach >= 1).astype(jnp.float32) * total


def chain_kernel(count, step, side_work, extra_in, flag_ref, element_ref, *refs):
    side_in = refs[:extra_in]
    out_ref = refs[extra_in]
    link_slot, state_slot, sent_slot, send_sems, recv_sems = refs[-5:]
    side_out = refs[extra_in + 1:-5]
    me = lax.axis_index("seq")
    head = lax.axis_index("head")
    heads = element_ref.shape[0]
    pos = lax.rem(me, 4) if step == 1 else 3 - lax.rem(me + 2, 4)
    ahead_exists = (me + step >= 0) & (me + step < count)
    behind_exists = (me - step >= 0) & (me - step < count)

    barrier = pltpu.get_barrier_semaphore()
    for offset in (1, -1):
        ring_peer = (lax.rem(me + offset + count, count), head)
        pl.semaphore_signal(barrier, inc=1, device_id=ring_peer, device_id_type=pl.DeviceIdType.MESH)
    pl.semaphore_wait(barrier, 2)

    def describe(kind, part, source, landing):
        return pltpu.make_async_remote_copy(
            src_ref=source,
            dst_ref=landing.at[part],
            send_sem=send_sems.at[kind, part],
            recv_sem=recv_sems.at[kind, part],
            device_id=(me + step, head),
            device_id_type=pl.DeviceIdType.MESH,
        )

    flag = flag_ref[0]
    sends = []
    for part in range(heads):
        @pl.when((pos >= 1) & behind_exists)
        def _():
            describe(0, part, link_slot.at[part], link_slot).wait_recv()
            link_slot[part] = element_ref[part] + flag * link_slot[part]

        @pl.when((pos == 0) | jnp.logical_not(behind_exists))
        def _():
            link_slot[part] = element_ref[part]

        into_link = describe(0, part, link_slot.at[part], link_slot)
        into_state = pltpu.make_async_remote_copy(
            src_ref=link_slot.at[part],
            dst_ref=state_slot.at[part],
            send_sem=send_sems.at[0, part],
            recv_sem=recv_sems.at[1, part],
            device_id=(me + step, head),
            device_id_type=pl.DeviceIdType.MESH,
        )

        @pl.when((pos <= 2) & ahead_exists)
        def _():
            into_link.start()

        @pl.when((pos == 3) & ahead_exists)
        def _():
            into_state.start()

        sends.append((into_link, into_state))
    side_work(side_in, side_out)
    state_sends = []
    for part in range(heads):
        @pl.when(behind_exists)
        def _():
            describe(1, part, state_slot.at[part], state_slot).wait_recv()

        @pl.when(jnp.logical_not(behind_exists))
        def _():
            state_slot[part] = jnp.zeros(state_slot.shape[1:], jnp.float32)

        out_ref[part] = state_slot[part]
        copy = describe(1, part, sent_slot.at[part], state_slot)

        @pl.when((pos <= 2) & ahead_exists)
        def _():
            sent_slot[part] = element_ref[part] + flag * state_slot[part]
            copy.start()

        state_sends.append(copy)
    for part in range(heads):
        into_link, into_state = sends[part]

        @pl.when((pos <= 2) & ahead_exists)
        def _():
            into_link.wait_send()

        @pl.when((pos == 3) & ahead_exists)
        def _():
            into_state.wait_send()

        @pl.when((pos <= 2) & ahead_exists)
        def _():
            state_sends[part].wait_send()


def no_side_work(side_in, side_out):
    del side_in, side_out


def backward_local(scale, side_in, side_out):
    query_ref, key_ref, value_ref, grad_ref, inside_ref = side_in
    query_out, key_out, value_out = side_out
    inside = inside_ref[...] > 0.5
    contract_last = (((1,), (1,)), ((), ()))
    for part in range(query_ref.shape[1] // HD):
        cols = pl.ds(part * HD, HD)
        query_h = query_ref[:, cols]
        key_h = key_ref[:, cols]
        grad_h = grad_ref[:, cols]
        scores = lax.dot_general(query_h, key_h, contract_last, preferred_element_type=jnp.float32)
        scaled = jnp.where(inside, scale * scores, 0.0)
        grad_scores = lax.dot_general(
            grad_h, value_ref[:, cols], contract_last, preferred_element_type=jnp.float32
        )
        mixed = jnp.where(inside, scale * grad_scores, 0.0)
        query_out[:, cols] = jnp.dot(mixed.astype(jnp.bfloat16), key_h, preferred_element_type=jnp.float32)
        key_out[:, cols] = jnp.dot(mixed.T.astype(jnp.bfloat16), query_h, preferred_element_type=jnp.float32)
        value_out[:, cols] = jnp.dot(scaled.T.astype(jnp.bfloat16), grad_h, preferred_element_type=jnp.float32)


def scan_window(element, flag, step, ident, side_work=no_side_work, side_inputs=(), side_shapes=()):
    count = lax.axis_size("seq")
    shape = element.shape
    element = element.reshape(shape[0] * PIECES, shape[1] // PIECES, shape[2])
    heads = element.shape[0]
    vmem = pl.BlockSpec(memory_space=pltpu.VMEM)
    outs = pl.pallas_call(
        functools.partial(chain_kernel, count, step, side_work, len(side_inputs)),
        out_shape=(jax.ShapeDtypeStruct(element.shape, jnp.float32),) + tuple(side_shapes),
        in_specs=[pl.BlockSpec(memory_space=pltpu.SMEM)] + [vmem] * (1 + len(side_inputs)),
        out_specs=(vmem,) * (1 + len(side_shapes)),
        scratch_shapes=[
            pltpu.VMEM(element.shape, jnp.float32),
            pltpu.VMEM(element.shape, jnp.float32),
            pltpu.VMEM(element.shape, jnp.float32),
            pltpu.SemaphoreType.DMA((2, heads)),
            pltpu.SemaphoreType.DMA((2, heads)),
        ],
        compiler_params=pltpu.CompilerParams(collective_id=ident, has_side_effects=True),
    )(flag.astype(jnp.float32).reshape(1), element, *side_inputs)
    return (outs[0].reshape(shape),) + tuple(outs[1:])

def head_sum_kernel(count, parts_ref, out_ref, slots, send_sems, recv_sems):
    me = lax.axis_index("head")
    row = lax.axis_index("seq")
    barrier = pltpu.get_barrier_semaphore()
    for shift in range(1, count):
        peer = (row, lax.rem(me + shift, count))
        pl.semaphore_signal(barrier, inc=1, device_id=peer, device_id_type=pl.DeviceIdType.MESH)
    pl.semaphore_wait(barrier, count - 1)
    copies = []
    for shift in range(1, count):
        copy = pltpu.make_async_remote_copy(
            src_ref=parts_ref,
            dst_ref=slots.at[me],
            send_sem=send_sems.at[shift],
            recv_sem=recv_sems.at[me],
            device_id=(row, lax.rem(me + shift, count)),
            device_id_type=pl.DeviceIdType.MESH,
        )
        copy.start()
        copies.append(copy)
    slots[me] = parts_ref[...]
    for shift in range(1, count):
        source = lax.rem(me + count - shift, count)
        pltpu.make_async_remote_copy(
            src_ref=parts_ref,
            dst_ref=slots.at[source],
            send_sem=send_sems.at[shift],
            recv_sem=recv_sems.at[source],
            device_id=(row, source),
            device_id_type=pl.DeviceIdType.MESH,
        ).wait_recv()
    total = slots[0]
    for index in range(1, count):
        total = total + slots[index]
    out_ref[...] = total
    for copy in copies:
        copy.wait_send()


def head_sum(square_sum, cross_sum):
    count = lax.axis_size("head")
    rows = square_sum.shape[0]
    parts = jnp.concatenate(
        [square_sum[None], cross_sum[None], jnp.zeros((6, rows), jnp.float32)], axis=0
    )
    total = pl.pallas_call(
        functools.partial(head_sum_kernel, count),
        out_shape=jax.ShapeDtypeStruct(parts.shape, jnp.float32),
        in_specs=[pl.BlockSpec(memory_space=pltpu.VMEM)],
        out_specs=pl.BlockSpec(memory_space=pltpu.VMEM),
        scratch_shapes=[
            pltpu.VMEM((count,) + parts.shape, jnp.float32),
            pltpu.SemaphoreType.DMA((count,)),
            pltpu.SemaphoreType.DMA((count,)),
        ],
        compiler_params=pltpu.CompilerParams(collective_id=2, has_side_effects=True),
    )(parts)
    return total[0], total[1]


def gradient_kernel(scale, query_ref, key_ref, value_ref, grad_ref, before_ref, after_ref,
                    carried_ref, returned_ref, query_local, key_local, value_local,
                    query_out, key_out, value_out):
    before = before_ref[...]
    after = after_ref[...]
    contract_last = (((1,), (1,)), ((), ()))

    def halves(state):
        upper = state.astype(jnp.bfloat16)
        return upper, (state - upper.astype(jnp.float32)).astype(jnp.bfloat16)

    def across(rows, state, form):
        upper, lower = halves(state)
        if form == "nt":
            first = lax.dot_general(rows, upper, contract_last, preferred_element_type=jnp.float32)
            return first + lax.dot_general(rows, lower, contract_last, preferred_element_type=jnp.float32)
        first = jnp.dot(rows, upper, preferred_element_type=jnp.float32)
        return first + jnp.dot(rows, lower, preferred_element_type=jnp.float32)

    for part in range(query_ref.shape[1] // HD):
        cols = pl.ds(part * HD, HD)
        carried = carried_ref[part]
        returned = returned_ref[part]
        query_out[:, cols] = (
            query_local[:, cols] + before * scale * across(grad_ref[:, cols], carried, "nt")
        ).astype(jnp.bfloat16)
        key_out[:, cols] = (
            key_local[:, cols] + after * scale * across(value_ref[:, cols], returned, "nt")
        ).astype(jnp.bfloat16)
        value_out[:, cols] = (
            value_local[:, cols] + after * scale * across(key_ref[:, cols], returned, "nn")
        ).astype(jnp.bfloat16)


def gradients(scale, queries, key_rows, value_rows, grad_flat, before, after, carried, returned, local):
    flat = jax.ShapeDtypeStruct(queries.shape, jnp.bfloat16)
    vmem = pl.BlockSpec(memory_space=pltpu.VMEM)
    rows = queries.shape[0]
    wide = lambda mask: jnp.broadcast_to(mask.astype(jnp.float32)[:, None], (rows, HD))
    return pl.pallas_call(
        functools.partial(gradient_kernel, scale),
        out_shape=(flat, flat, flat),
        in_specs=[vmem] * 11,
        out_specs=(vmem, vmem, vmem),
    )(queries, key_rows, value_rows, grad_flat, wide(before), wide(after), carried, returned, *local)

def join_states(earlier_part, later_part):
    return (
        later_part[0] + (1.0 - later_part[1]) * earlier_part[0],
        jnp.maximum(earlier_part[1], later_part[1]),
    )


def split_state(state):
    upper = state.astype(jnp.bfloat16)
    lower = (state - upper.astype(jnp.float32)).astype(jnp.bfloat16)
    return (upper, lower)


def state_product(form, rows, state):
    upper, lower = split_state(state)
    first = jnp.einsum(form, rows, upper, preferred_element_type=jnp.float32)
    return first + jnp.einsum(form, rows, lower, preferred_element_type=jnp.float32)


def shards(queries, key_rows, value_rows, out_grad, norm_gain, dial_start, dial_end):
    token_count = queries.shape[0]
    head_count = queries.shape[1] // HD
    score_scale = HD ** (-0.5)
    width_all = HEADS * HD
    block_begin = lax.axis_index("seq") * token_count
    local_pos = jnp.arange(token_count, dtype=jnp.int32)
    position = block_begin + local_pos
    query_h = queries.reshape(token_count, head_count, HD)
    key_h = key_rows.reshape(token_count, head_count, HD)
    value_h = value_rows.reshape(token_count, head_count, HD)
    last_start = dial_start[token_count - 1]
    keep_last = position >= last_start
    element = jnp.einsum(
        "shd,she->hde",
        jnp.where(keep_last[:, None, None], key_h, jnp.zeros((), jnp.bfloat16)),
        value_h,
        preferred_element_type=jnp.float32,
    )
    carried = scan_window(element, last_start < block_begin, 1, 0)[0]
    carried, query_h, key_h, value_h = lax.optimization_barrier((carried, query_h, key_h, value_h))
    inside = (position[None, :] >= dial_start[:, None]) & (local_pos[None, :] <= local_pos[:, None])
    scores = jnp.einsum("thd,shd->hts", query_h, key_h, preferred_element_type=jnp.float32)
    weights = jnp.where(inside[None], score_scale * scores, 0.0).astype(jnp.bfloat16)
    local_mix = jnp.einsum("hts,she->the", weights, value_h, preferred_element_type=jnp.float32)
    across = score_scale * state_product("thd,hde->the", query_h, carried)
    from_before = (dial_start < block_begin).astype(jnp.float32)[:, None, None]
    attended = (local_mix + from_before * across).reshape(token_count, head_count * HD)
    grad_wide = out_grad.astype(jnp.float32)
    square_sum, cross_sum = head_sum(
        jnp.sum(attended * attended, axis=1), jnp.sum(norm_gain * grad_wide * attended, axis=1)
    )
    inv_rms = lax.rsqrt(square_sum / width_all + EPSILON)
    normed = (attended * inv_rms[:, None] * norm_gain).astype(jnp.bfloat16)
    grad_attn = (
        inv_rms[:, None] * norm_gain * grad_wide
        - attended * (inv_rms * inv_rms * inv_rms * cross_sum / width_all)[:, None]
    )
    grad_weight = grad_attn.astype(jnp.bfloat16).reshape(token_count, head_count, HD)
    first_end = dial_end[0]
    keep_first = position < first_end
    back_element = jnp.einsum(
        "thd,the->hde",
        jnp.where(keep_first[:, None, None], query_h, jnp.zeros((), jnp.bfloat16)),
        grad_weight,
        preferred_element_type=jnp.float32,
    )
    wide_shape = jax.ShapeDtypeStruct(queries.shape, jnp.float32)
    grad_flat = grad_weight.reshape(queries.shape)
    returned, *local = scan_window(
        back_element, first_end > block_begin + token_count, -1, 1,
        functools.partial(backward_local, score_scale),
        (queries, key_rows, value_rows, grad_flat, inside.astype(jnp.float32)),
        (wide_shape,) * 3,
    )
    query_grad, key_grad, value_grad = gradients(
        score_scale, queries, key_rows, value_rows, grad_flat,
        dial_start < block_begin, dial_end > block_begin + token_count, carried, returned, local,
    )
    return (normed, query_grad, key_grad, value_grad)


def solution(mesh):
    placed = (
        P("seq", "head"),
        P("seq", "head"),
        P("seq", "head"),
        P("seq", "head"),
        P("head"),
        P("seq"),
        P("seq"),
    )
    return jax.shard_map(
        shards,
        mesh=mesh,
        in_specs=placed,
        out_specs=(P("seq", "head"), P("seq", "head"), P("seq", "head"), P("seq", "head")),
        check_vma=False,
    )
```

```python
import functools

import jax
import jax.numpy as jnp
from jax import lax
from jax.experimental import pallas as pl
from jax.experimental.pallas import tpu as pltpu
from jax.sharding import PartitionSpec as P

HEADS = 64
HD = 128
SPAN = 4
PIECES = 4


EPSILON = 1e-06


def from_behind(x, axis, by):
    count = lax.axis_size(axis)
    pairs = [(i, i + by) for i in range(count) if 0 <= i + by < count]
    return lax.ppermute(x, axis, pairs)


def scan_window_permutes(element, reach, step):
    nearest = from_behind(element, "seq", step)
    second = from_behind(nearest, "seq", step)
    pair = nearest + (reach >= 2).astype(jnp.float32) * second
    far_pair = from_behind(pair, "seq", 2 * step)
    total = pair + (reach >= 3).astype(jnp.float32) * far_pair
    return (reach >= 1).astype(jnp.float32) * total


def chain_kernel(count, step, side_work, extra_in, flag_ref, element_ref, *refs):
    side_in = refs[:extra_in]
    out_ref = refs[extra_in]
    link_slot, state_slot, sent_slot, send_sems, recv_sems = refs[-5:]
    side_out = refs[extra_in + 1:-5]
    me = lax.axis_index("seq")
    head = lax.axis_index("head")
    heads = element_ref.shape[0]
    pos = lax.rem(me, 4) if step == 1 else 3 - lax.rem(me + 2, 4)
    ahead_exists = (me + step >= 0) & (me + step < count)
    behind_exists = (me - step >= 0) & (me - step < count)

    barrier = pltpu.get_barrier_semaphore()
    for offset in (1, -1):
        ring_peer = (lax.rem(me + offset + count, count), head)
        pl.semaphore_signal(barrier, inc=1, device_id=ring_peer, device_id_type=pl.DeviceIdType.MESH)
    pl.semaphore_wait(barrier, 2)

    def describe(kind, part, source, landing):
        return pltpu.make_async_remote_copy(
            src_ref=source,
            dst_ref=landing.at[part],
            send_sem=send_sems.at[kind, part],
            recv_sem=recv_sems.at[kind, part],
            device_id=(me + step, head),
            device_id_type=pl.DeviceIdType.MESH,
        )

    flag = flag_ref[0]
    sends = []
    for part in range(heads):
        @pl.when((pos >= 1) & behind_exists)
        def _():
            describe(0, part, link_slot.at[part], link_slot).wait_recv()
            link_slot[part] = element_ref[part] + flag * link_slot[part]

        @pl.when((pos == 0) | jnp.logical_not(behind_exists))
        def _():
            link_slot[part] = element_ref[part]

        into_link = describe(0, part, link_slot.at[part], link_slot)
        into_state = pltpu.make_async_remote_copy(
            src_ref=link_slot.at[part],
            dst_ref=state_slot.at[part],
            send_sem=send_sems.at[0, part],
            recv_sem=recv_sems.at[1, part],
            device_id=(me + step, head),
            device_id_type=pl.DeviceIdType.MESH,
        )

        @pl.when((pos <= 2) & ahead_exists)
        def _():
            into_link.start()

        @pl.when((pos == 3) & ahead_exists)
        def _():
            into_state.start()

        sends.append((into_link, into_state))
    side_work(side_in, side_out)
    state_sends = []
    for part in range(heads):
        @pl.when(behind_exists)
        def _():
            describe(1, part, state_slot.at[part], state_slot).wait_recv()

        @pl.when(jnp.logical_not(behind_exists))
        def _():
            state_slot[part] = jnp.zeros(state_slot.shape[1:], jnp.float32)

        out_ref[part] = state_slot[part]
        copy = describe(1, part, sent_slot.at[part], state_slot)

        @pl.when((pos <= 2) & ahead_exists)
        def _():
            sent_slot[part] = element_ref[part] + flag * state_slot[part]
            copy.start()

        state_sends.append(copy)
    for part in range(heads):
        into_link, into_state = sends[part]

        @pl.when((pos <= 2) & ahead_exists)
        def _():
            into_link.wait_send()

        @pl.when((pos == 3) & ahead_exists)
        def _():
            into_state.wait_send()

        @pl.when((pos <= 2) & ahead_exists)
        def _():
            state_sends[part].wait_send()


def no_side_work(side_in, side_out):
    del side_in, side_out


def backward_local(scale, side_in, side_out):
    query_ref, key_ref, value_ref, grad_ref, starts_ref = side_in
    query_out, key_out, value_out = side_out
    rows = query_ref.shape[0]
    row = lax.broadcasted_iota(jnp.int32, (rows, rows), 0)
    col = lax.broadcasted_iota(jnp.int32, (rows, rows), 1)
    begin = lax.axis_index("seq") * rows
    inside = (begin + col >= starts_ref[...]) & (col <= row)
    contract_last = (((1,), (1,)), ((), ()))
    for part in range(query_ref.shape[1] // HD):
        cols = pl.ds(part * HD, HD)
        query_h = query_ref[:, cols]
        key_h = key_ref[:, cols]
        grad_h = grad_ref[:, cols]
        scores = lax.dot_general(query_h, key_h, contract_last, preferred_element_type=jnp.float32)
        scaled = jnp.where(inside, scale * scores, 0.0)
        grad_scores = lax.dot_general(
            grad_h, value_ref[:, cols], contract_last, preferred_element_type=jnp.float32
        )
        mixed = jnp.where(inside, scale * grad_scores, 0.0)
        query_out[:, cols] = jnp.dot(mixed.astype(jnp.bfloat16), key_h, preferred_element_type=jnp.float32)
        key_out[:, cols] = jnp.dot(mixed.T.astype(jnp.bfloat16), query_h, preferred_element_type=jnp.float32)
        value_out[:, cols] = jnp.dot(scaled.T.astype(jnp.bfloat16), grad_h, preferred_element_type=jnp.float32)


def scan_window(element, flag, step, ident, side_work=no_side_work, side_inputs=(), side_shapes=()):
    count = lax.axis_size("seq")
    shape = element.shape
    element = element.reshape(shape[0] * PIECES, shape[1] // PIECES, shape[2])
    heads = element.shape[0]
    vmem = pl.BlockSpec(memory_space=pltpu.VMEM)
    outs = pl.pallas_call(
        functools.partial(chain_kernel, count, step, side_work, len(side_inputs)),
        out_shape=(jax.ShapeDtypeStruct(element.shape, jnp.float32),) + tuple(side_shapes),
        in_specs=[pl.BlockSpec(memory_space=pltpu.SMEM)] + [vmem] * (1 + len(side_inputs)),
        out_specs=(vmem,) * (1 + len(side_shapes)),
        scratch_shapes=[
            pltpu.VMEM(element.shape, jnp.float32),
            pltpu.VMEM(element.shape, jnp.float32),
            pltpu.VMEM(element.shape, jnp.float32),
            pltpu.SemaphoreType.DMA((2, heads)),
            pltpu.SemaphoreType.DMA((2, heads)),
        ],
        compiler_params=pltpu.CompilerParams(collective_id=ident, has_side_effects=True),
    )(flag.astype(jnp.float32).reshape(1), element, *side_inputs)
    return (outs[0].reshape(shape),) + tuple(outs[1:])

def head_sum_kernel(count, parts_ref, out_ref, slots, send_sems, recv_sems):
    me = lax.axis_index("head")
    row = lax.axis_index("seq")
    barrier = pltpu.get_barrier_semaphore()
    for shift in range(1, count):
        peer = (row, lax.rem(me + shift, count))
        pl.semaphore_signal(barrier, inc=1, device_id=peer, device_id_type=pl.DeviceIdType.MESH)
    pl.semaphore_wait(barrier, count - 1)
    copies = []
    for shift in range(1, count):
        copy = pltpu.make_async_remote_copy(
            src_ref=parts_ref,
            dst_ref=slots.at[me],
            send_sem=send_sems.at[shift],
            recv_sem=recv_sems.at[me],
            device_id=(row, lax.rem(me + shift, count)),
            device_id_type=pl.DeviceIdType.MESH,
        )
        copy.start()
        copies.append(copy)
    slots[me] = parts_ref[...]
    for shift in range(1, count):
        source = lax.rem(me + count - shift, count)
        pltpu.make_async_remote_copy(
            src_ref=parts_ref,
            dst_ref=slots.at[source],
            send_sem=send_sems.at[shift],
            recv_sem=recv_sems.at[source],
            device_id=(row, source),
            device_id_type=pl.DeviceIdType.MESH,
        ).wait_recv()
    total = slots[0]
    for index in range(1, count):
        total = total + slots[index]
    out_ref[...] = total
    for copy in copies:
        copy.wait_send()


def head_sum(square_sum, cross_sum):
    count = lax.axis_size("head")
    rows = square_sum.shape[0]
    parts = jnp.concatenate(
        [square_sum[None], cross_sum[None], jnp.zeros((6, rows), jnp.float32)], axis=0
    )
    total = pl.pallas_call(
        functools.partial(head_sum_kernel, count),
        out_shape=jax.ShapeDtypeStruct(parts.shape, jnp.float32),
        in_specs=[pl.BlockSpec(memory_space=pltpu.VMEM)],
        out_specs=pl.BlockSpec(memory_space=pltpu.VMEM),
        scratch_shapes=[
            pltpu.VMEM((count,) + parts.shape, jnp.float32),
            pltpu.SemaphoreType.DMA((count,)),
            pltpu.SemaphoreType.DMA((count,)),
        ],
        compiler_params=pltpu.CompilerParams(collective_id=2, has_side_effects=True),
    )(parts)
    return total[0], total[1]


def gradient_kernel(scale, query_ref, key_ref, value_ref, grad_ref, before_ref, after_ref,
                    carried_ref, returned_ref, query_local, key_local, value_local,
                    query_out, key_out, value_out):
    rows = query_ref.shape[0]
    begin = lax.axis_index("seq") * rows
    before = (before_ref[...] < begin).astype(jnp.float32)
    after = (after_ref[...] > begin + rows).astype(jnp.float32)
    contract_last = (((1,), (1,)), ((), ()))

    def halves(state):
        upper = state.astype(jnp.bfloat16)
        return upper, (state - upper.astype(jnp.float32)).astype(jnp.bfloat16)

    def across(rows, state, form):
        upper, lower = halves(state)
        if form == "nt":
            first = lax.dot_general(rows, upper, contract_last, preferred_element_type=jnp.float32)
            return first + lax.dot_general(rows, lower, contract_last, preferred_element_type=jnp.float32)
        first = jnp.dot(rows, upper, preferred_element_type=jnp.float32)
        return first + jnp.dot(rows, lower, preferred_element_type=jnp.float32)

    for part in range(query_ref.shape[1] // HD):
        cols = pl.ds(part * HD, HD)
        carried = carried_ref[part]
        returned = returned_ref[part]
        query_out[:, cols] = (
            query_local[:, cols] + before * scale * across(grad_ref[:, cols], carried, "nt")
        ).astype(jnp.bfloat16)
        key_out[:, cols] = (
            key_local[:, cols] + after * scale * across(value_ref[:, cols], returned, "nt")
        ).astype(jnp.bfloat16)
        value_out[:, cols] = (
            value_local[:, cols] + after * scale * across(key_ref[:, cols], returned, "nn")
        ).astype(jnp.bfloat16)


def gradients(scale, queries, key_rows, value_rows, grad_flat, before, after, carried, returned, local):
    flat = jax.ShapeDtypeStruct(queries.shape, jnp.bfloat16)
    vmem = pl.BlockSpec(memory_space=pltpu.VMEM)
    rows = queries.shape[0]
    wide = lambda bounds: bounds.reshape(rows, 1)
    return pl.pallas_call(
        functools.partial(gradient_kernel, scale),
        out_shape=(flat, flat, flat),
        in_specs=[vmem] * 11,
        out_specs=(vmem, vmem, vmem),
    )(queries, key_rows, value_rows, grad_flat, wide(before), wide(after), carried, returned, *local)

def join_states(earlier_part, later_part):
    return (
        later_part[0] + (1.0 - later_part[1]) * earlier_part[0],
        jnp.maximum(earlier_part[1], later_part[1]),
    )


def split_state(state):
    upper = state.astype(jnp.bfloat16)
    lower = (state - upper.astype(jnp.float32)).astype(jnp.bfloat16)
    return (upper, lower)


def state_product(form, rows, state):
    upper, lower = split_state(state)
    first = jnp.einsum(form, rows, upper, preferred_element_type=jnp.float32)
    return first + jnp.einsum(form, rows, lower, preferred_element_type=jnp.float32)


def shards(queries, key_rows, value_rows, out_grad, norm_gain, dial_start, dial_end):
    token_count = queries.shape[0]
    head_count = queries.shape[1] // HD
    score_scale = HD ** (-0.5)
    width_all = HEADS * HD
    block_begin = lax.axis_index("seq") * token_count
    local_pos = jnp.arange(token_count, dtype=jnp.int32)
    position = block_begin + local_pos
    query_h = queries.reshape(token_count, head_count, HD)
    key_h = key_rows.reshape(token_count, head_count, HD)
    value_h = value_rows.reshape(token_count, head_count, HD)
    last_start = dial_start[token_count - 1]
    keep_last = position >= last_start
    element = jnp.einsum(
        "shd,she->hde",
        jnp.where(keep_last[:, None, None], key_h, jnp.zeros((), jnp.bfloat16)),
        value_h,
        preferred_element_type=jnp.float32,
    )
    carried = scan_window(element, last_start < block_begin, 1, 0)[0]
    carried, query_h, key_h, value_h = lax.optimization_barrier((carried, query_h, key_h, value_h))
    inside = (position[None, :] >= dial_start[:, None]) & (local_pos[None, :] <= local_pos[:, None])
    scores = jnp.einsum("thd,shd->hts", query_h, key_h, preferred_element_type=jnp.float32)
    weights = jnp.where(inside[None], score_scale * scores, 0.0).astype(jnp.bfloat16)
    local_mix = jnp.einsum("hts,she->the", weights, value_h, preferred_element_type=jnp.float32)
    across = score_scale * state_product("thd,hde->the", query_h, carried)
    from_before = (dial_start < block_begin).astype(jnp.float32)[:, None, None]
    attended = (local_mix + from_before * across).reshape(token_count, head_count * HD)
    grad_wide = out_grad.astype(jnp.float32)
    square_sum, cross_sum = head_sum(
        jnp.sum(attended * attended, axis=1), jnp.sum(norm_gain * grad_wide * attended, axis=1)
    )
    inv_rms = lax.rsqrt(square_sum / width_all + EPSILON)
    normed = (attended * inv_rms[:, None] * norm_gain).astype(jnp.bfloat16)
    grad_attn = (
        inv_rms[:, None] * norm_gain * grad_wide
        - attended * (inv_rms * inv_rms * inv_rms * cross_sum / width_all)[:, None]
    )
    grad_weight = grad_attn.astype(jnp.bfloat16).reshape(token_count, head_count, HD)
    first_end = dial_end[0]
    keep_first = position < first_end
    back_element = jnp.einsum(
        "thd,the->hde",
        jnp.where(keep_first[:, None, None], query_h, jnp.zeros((), jnp.bfloat16)),
        grad_weight,
        preferred_element_type=jnp.float32,
    )
    wide_shape = jax.ShapeDtypeStruct(queries.shape, jnp.float32)
    grad_flat = grad_weight.reshape(queries.shape)
    returned, *local = scan_window(
        back_element, first_end > block_begin + token_count, -1, 1,
        functools.partial(backward_local, score_scale),
        (queries, key_rows, value_rows, grad_flat, dial_start.reshape(token_count, 1)),
        (wide_shape,) * 3,
    )
    query_grad, key_grad, value_grad = gradients(
        score_scale, queries, key_rows, value_rows, grad_flat,
        dial_start, dial_end, carried, returned, local,
    )
    return (normed, query_grad, key_grad, value_grad)


def solution(mesh):
    placed = (
        P("seq", "head"),
        P("seq", "head"),
        P("seq", "head"),
        P("seq", "head"),
        P("head"),
        P("seq"),
        P("seq"),
    )
    return jax.shard_map(
        shards,
        mesh=mesh,
        in_specs=placed,
        out_specs=(P("seq", "head"), P("seq", "head"), P("seq", "head"), P("seq", "head")),
        check_vma=False,
    )
```

```python
import functools

import jax
import jax.numpy as jnp
from jax import lax
from jax.experimental import pallas as pl
from jax.experimental.pallas import tpu as pltpu
from jax.sharding import PartitionSpec as P

HEADS = 64
HD = 128
SPAN = 4
PIECES = 4


EPSILON = 1e-06


def from_behind(x, axis, by):
    count = lax.axis_size(axis)
    pairs = [(i, i + by) for i in range(count) if 0 <= i + by < count]
    return lax.ppermute(x, axis, pairs)


def scan_window_permutes(element, reach, step):
    nearest = from_behind(element, "seq", step)
    second = from_behind(nearest, "seq", step)
    pair = nearest + (reach >= 2).astype(jnp.float32) * second
    far_pair = from_behind(pair, "seq", 2 * step)
    total = pair + (reach >= 3).astype(jnp.float32) * far_pair
    return (reach >= 1).astype(jnp.float32) * total


def chain_kernel(count, step, side_work, extra_in, flag_ref, element_ref, *refs):
    side_in = refs[:extra_in]
    out_ref = refs[extra_in]
    link_slot, state_slot, sent_slot, send_sems, recv_sems = refs[-5:]
    side_out = refs[extra_in + 1:-5]
    me = lax.axis_index("seq")
    head = lax.axis_index("head")
    heads = element_ref.shape[0]
    pos = lax.rem(me, 4) if step == 1 else 3 - lax.rem(me + 2, 4)
    ahead_exists = (me + step >= 0) & (me + step < count)
    behind_exists = (me - step >= 0) & (me - step < count)

    barrier = pltpu.get_barrier_semaphore()
    for offset in (1, -1):
        ring_peer = (lax.rem(me + offset + count, count), head)
        pl.semaphore_signal(barrier, inc=1, device_id=ring_peer, device_id_type=pl.DeviceIdType.MESH)
    pl.semaphore_wait(barrier, 2)

    def describe(kind, part, source, landing):
        return pltpu.make_async_remote_copy(
            src_ref=source,
            dst_ref=landing.at[part],
            send_sem=send_sems.at[kind, part],
            recv_sem=recv_sems.at[kind, part],
            device_id=(me + step, head),
            device_id_type=pl.DeviceIdType.MESH,
        )

    flag = flag_ref[0]
    sends = []
    for part in range(heads):
        @pl.when((pos >= 1) & behind_exists)
        def _():
            describe(0, part, link_slot.at[part], link_slot).wait_recv()
            link_slot[part] = element_ref[part] + flag * link_slot[part]

        @pl.when((pos == 0) | jnp.logical_not(behind_exists))
        def _():
            link_slot[part] = element_ref[part]

        into_link = describe(0, part, link_slot.at[part], link_slot)
        into_state = pltpu.make_async_remote_copy(
            src_ref=link_slot.at[part],
            dst_ref=state_slot.at[part],
            send_sem=send_sems.at[0, part],
            recv_sem=recv_sems.at[1, part],
            device_id=(me + step, head),
            device_id_type=pl.DeviceIdType.MESH,
        )

        @pl.when((pos <= 2) & ahead_exists)
        def _():
            into_link.start()

        @pl.when((pos == 3) & ahead_exists)
        def _():
            into_state.start()

        sends.append((into_link, into_state))
    side_work(side_in, side_out)
    state_sends = []
    for part in range(heads):
        @pl.when(behind_exists)
        def _():
            describe(1, part, state_slot.at[part], state_slot).wait_recv()

        @pl.when(jnp.logical_not(behind_exists))
        def _():
            state_slot[part] = jnp.zeros(state_slot.shape[1:], jnp.float32)

        out_ref[part] = state_slot[part]
        copy = describe(1, part, sent_slot.at[part], state_slot)

        @pl.when((pos <= 2) & ahead_exists)
        def _():
            sent_slot[part] = element_ref[part] + flag * state_slot[part]
            copy.start()

        state_sends.append(copy)
    for part in range(heads):
        into_link, into_state = sends[part]

        @pl.when((pos <= 2) & ahead_exists)
        def _():
            into_link.wait_send()

        @pl.when((pos == 3) & ahead_exists)
        def _():
            into_state.wait_send()

        @pl.when((pos <= 2) & ahead_exists)
        def _():
            state_sends[part].wait_send()


def no_side_work(side_in, side_out):
    del side_in, side_out


def backward_local(scale, side_in, side_out):
    query_ref, key_ref, value_ref, grad_ref, starts_ref = side_in
    query_out, key_out, value_out = side_out
    rows = query_ref.shape[0]
    row = lax.broadcasted_iota(jnp.int32, (rows, rows), 0)
    col = lax.broadcasted_iota(jnp.int32, (rows, rows), 1)
    begin = lax.axis_index("seq") * rows
    starts = jnp.broadcast_to(starts_ref[...], (rows, rows)).T
    inside = (begin + col >= starts) & (col <= row)
    contract_last = (((1,), (1,)), ((), ()))
    for part in range(query_ref.shape[1] // HD):
        cols = pl.ds(part * HD, HD)
        query_h = query_ref[:, cols]
        key_h = key_ref[:, cols]
        grad_h = grad_ref[:, cols]
        scores = lax.dot_general(query_h, key_h, contract_last, preferred_element_type=jnp.float32)
        scaled = jnp.where(inside, scale * scores, 0.0)
        grad_scores = lax.dot_general(
            grad_h, value_ref[:, cols], contract_last, preferred_element_type=jnp.float32
        )
        mixed = jnp.where(inside, scale * grad_scores, 0.0)
        query_out[:, cols] = jnp.dot(mixed.astype(jnp.bfloat16), key_h, preferred_element_type=jnp.float32)
        key_out[:, cols] = jnp.dot(mixed.T.astype(jnp.bfloat16), query_h, preferred_element_type=jnp.float32)
        value_out[:, cols] = jnp.dot(scaled.T.astype(jnp.bfloat16), grad_h, preferred_element_type=jnp.float32)


def scan_window(element, flag, step, ident, side_work=no_side_work, side_inputs=(), side_shapes=()):
    count = lax.axis_size("seq")
    shape = element.shape
    element = element.reshape(shape[0] * PIECES, shape[1] // PIECES, shape[2])
    heads = element.shape[0]
    vmem = pl.BlockSpec(memory_space=pltpu.VMEM)
    outs = pl.pallas_call(
        functools.partial(chain_kernel, count, step, side_work, len(side_inputs)),
        out_shape=(jax.ShapeDtypeStruct(element.shape, jnp.float32),) + tuple(side_shapes),
        in_specs=[pl.BlockSpec(memory_space=pltpu.SMEM)] + [vmem] * (1 + len(side_inputs)),
        out_specs=(vmem,) * (1 + len(side_shapes)),
        scratch_shapes=[
            pltpu.VMEM(element.shape, jnp.float32),
            pltpu.VMEM(element.shape, jnp.float32),
            pltpu.VMEM(element.shape, jnp.float32),
            pltpu.SemaphoreType.DMA((2, heads)),
            pltpu.SemaphoreType.DMA((2, heads)),
        ],
        compiler_params=pltpu.CompilerParams(collective_id=ident, has_side_effects=True),
    )(flag.astype(jnp.float32).reshape(1), element, *side_inputs)
    return (outs[0].reshape(shape),) + tuple(outs[1:])

def head_sum_kernel(count, parts_ref, out_ref, slots, send_sems, recv_sems):
    me = lax.axis_index("head")
    row = lax.axis_index("seq")
    barrier = pltpu.get_barrier_semaphore()
    for shift in range(1, count):
        peer = (row, lax.rem(me + shift, count))
        pl.semaphore_signal(barrier, inc=1, device_id=peer, device_id_type=pl.DeviceIdType.MESH)
    pl.semaphore_wait(barrier, count - 1)
    copies = []
    for shift in range(1, count):
        copy = pltpu.make_async_remote_copy(
            src_ref=parts_ref,
            dst_ref=slots.at[me],
            send_sem=send_sems.at[shift],
            recv_sem=recv_sems.at[me],
            device_id=(row, lax.rem(me + shift, count)),
            device_id_type=pl.DeviceIdType.MESH,
        )
        copy.start()
        copies.append(copy)
    slots[me] = parts_ref[...]
    for shift in range(1, count):
        source = lax.rem(me + count - shift, count)
        pltpu.make_async_remote_copy(
            src_ref=parts_ref,
            dst_ref=slots.at[source],
            send_sem=send_sems.at[shift],
            recv_sem=recv_sems.at[source],
            device_id=(row, source),
            device_id_type=pl.DeviceIdType.MESH,
        ).wait_recv()
    total = slots[0]
    for index in range(1, count):
        total = total + slots[index]
    out_ref[...] = total
    for copy in copies:
        copy.wait_send()


def head_sum(square_sum, cross_sum):
    count = lax.axis_size("head")
    rows = square_sum.shape[0]
    parts = jnp.concatenate(
        [square_sum[None], cross_sum[None], jnp.zeros((6, rows), jnp.float32)], axis=0
    )
    total = pl.pallas_call(
        functools.partial(head_sum_kernel, count),
        out_shape=jax.ShapeDtypeStruct(parts.shape, jnp.float32),
        in_specs=[pl.BlockSpec(memory_space=pltpu.VMEM)],
        out_specs=pl.BlockSpec(memory_space=pltpu.VMEM),
        scratch_shapes=[
            pltpu.VMEM((count,) + parts.shape, jnp.float32),
            pltpu.SemaphoreType.DMA((count,)),
            pltpu.SemaphoreType.DMA((count,)),
        ],
        compiler_params=pltpu.CompilerParams(collective_id=2, has_side_effects=True),
    )(parts)
    return total[0], total[1]


def gradient_kernel(scale, query_ref, key_ref, value_ref, grad_ref, before_ref, after_ref,
                    carried_ref, returned_ref, query_local, key_local, value_local,
                    query_out, key_out, value_out):
    rows = query_ref.shape[0]
    begin = lax.axis_index("seq") * rows
    before = (jnp.broadcast_to(before_ref[...], (rows, rows)).T < begin).astype(jnp.float32)
    after = (jnp.broadcast_to(after_ref[...], (rows, rows)).T > begin + rows).astype(jnp.float32)
    contract_last = (((1,), (1,)), ((), ()))

    def halves(state):
        upper = state.astype(jnp.bfloat16)
        return upper, (state - upper.astype(jnp.float32)).astype(jnp.bfloat16)

    def across(rows, state, form):
        upper, lower = halves(state)
        if form == "nt":
            first = lax.dot_general(rows, upper, contract_last, preferred_element_type=jnp.float32)
            return first + lax.dot_general(rows, lower, contract_last, preferred_element_type=jnp.float32)
        first = jnp.dot(rows, upper, preferred_element_type=jnp.float32)
        return first + jnp.dot(rows, lower, preferred_element_type=jnp.float32)

    for part in range(query_ref.shape[1] // HD):
        cols = pl.ds(part * HD, HD)
        carried = carried_ref[part]
        returned = returned_ref[part]
        query_out[:, cols] = (
            query_local[:, cols] + before * scale * across(grad_ref[:, cols], carried, "nt")
        ).astype(jnp.bfloat16)
        key_out[:, cols] = (
            key_local[:, cols] + after * scale * across(value_ref[:, cols], returned, "nt")
        ).astype(jnp.bfloat16)
        value_out[:, cols] = (
            value_local[:, cols] + after * scale * across(key_ref[:, cols], returned, "nn")
        ).astype(jnp.bfloat16)


def gradients(scale, queries, key_rows, value_rows, grad_flat, before, after, carried, returned, local):
    flat = jax.ShapeDtypeStruct(queries.shape, jnp.bfloat16)
    vmem = pl.BlockSpec(memory_space=pltpu.VMEM)
    rows = queries.shape[0]
    wide = lambda bounds: bounds.reshape(1, rows)
    return pl.pallas_call(
        functools.partial(gradient_kernel, scale),
        out_shape=(flat, flat, flat),
        in_specs=[vmem] * 11,
        out_specs=(vmem, vmem, vmem),
    )(queries, key_rows, value_rows, grad_flat, wide(before), wide(after), carried, returned, *local)

def join_states(earlier_part, later_part):
    return (
        later_part[0] + (1.0 - later_part[1]) * earlier_part[0],
        jnp.maximum(earlier_part[1], later_part[1]),
    )


def split_state(state):
    upper = state.astype(jnp.bfloat16)
    lower = (state - upper.astype(jnp.float32)).astype(jnp.bfloat16)
    return (upper, lower)


def state_product(form, rows, state):
    upper, lower = split_state(state)
    first = jnp.einsum(form, rows, upper, preferred_element_type=jnp.float32)
    return first + jnp.einsum(form, rows, lower, preferred_element_type=jnp.float32)


def shards(queries, key_rows, value_rows, out_grad, norm_gain, dial_start, dial_end):
    token_count = queries.shape[0]
    head_count = queries.shape[1] // HD
    score_scale = HD ** (-0.5)
    width_all = HEADS * HD
    block_begin = lax.axis_index("seq") * token_count
    local_pos = jnp.arange(token_count, dtype=jnp.int32)
    position = block_begin + local_pos
    query_h = queries.reshape(token_count, head_count, HD)
    key_h = key_rows.reshape(token_count, head_count, HD)
    value_h = value_rows.reshape(token_count, head_count, HD)
    last_start = dial_start[token_count - 1]
    keep_last = position >= last_start
    element = jnp.einsum(
        "shd,she->hde",
        jnp.where(keep_last[:, None, None], key_h, jnp.zeros((), jnp.bfloat16)),
        value_h,
        preferred_element_type=jnp.float32,
    )
    carried = scan_window(element, last_start < block_begin, 1, 0)[0]
    carried, query_h, key_h, value_h = lax.optimization_barrier((carried, query_h, key_h, value_h))
    inside = (position[None, :] >= dial_start[:, None]) & (local_pos[None, :] <= local_pos[:, None])
    scores = jnp.einsum("thd,shd->hts", query_h, key_h, preferred_element_type=jnp.float32)
    weights = jnp.where(inside[None], score_scale * scores, 0.0).astype(jnp.bfloat16)
    local_mix = jnp.einsum("hts,she->the", weights, value_h, preferred_element_type=jnp.float32)
    across = score_scale * state_product("thd,hde->the", query_h, carried)
    from_before = (dial_start < block_begin).astype(jnp.float32)[:, None, None]
    attended = (local_mix + from_before * across).reshape(token_count, head_count * HD)
    grad_wide = out_grad.astype(jnp.float32)
    square_sum, cross_sum = head_sum(
        jnp.sum(attended * attended, axis=1), jnp.sum(norm_gain * grad_wide * attended, axis=1)
    )
    inv_rms = lax.rsqrt(square_sum / width_all + EPSILON)
    normed = (attended * inv_rms[:, None] * norm_gain).astype(jnp.bfloat16)
    grad_attn = (
        inv_rms[:, None] * norm_gain * grad_wide
        - attended * (inv_rms * inv_rms * inv_rms * cross_sum / width_all)[:, None]
    )
    grad_weight = grad_attn.astype(jnp.bfloat16).reshape(token_count, head_count, HD)
    first_end = dial_end[0]
    keep_first = position < first_end
    back_element = jnp.einsum(
        "thd,the->hde",
        jnp.where(keep_first[:, None, None], query_h, jnp.zeros((), jnp.bfloat16)),
        grad_weight,
        preferred_element_type=jnp.float32,
    )
    wide_shape = jax.ShapeDtypeStruct(queries.shape, jnp.float32)
    grad_flat = grad_weight.reshape(queries.shape)
    returned, *local = scan_window(
        back_element, first_end > block_begin + token_count, -1, 1,
        functools.partial(backward_local, score_scale),
        (queries, key_rows, value_rows, grad_flat, dial_start.reshape(1, token_count)),
        (wide_shape,) * 3,
    )
    query_grad, key_grad, value_grad = gradients(
        score_scale, queries, key_rows, value_rows, grad_flat,
        dial_start, dial_end, carried, returned, local,
    )
    return (normed, query_grad, key_grad, value_grad)


def solution(mesh):
    placed = (
        P("seq", "head"),
        P("seq", "head"),
        P("seq", "head"),
        P("seq", "head"),
        P("head"),
        P("seq"),
        P("seq"),
    )
    return jax.shard_map(
        shards,
        mesh=mesh,
        in_specs=placed,
        out_specs=(P("seq", "head"), P("seq", "head"), P("seq", "head"), P("seq", "head")),
        check_vma=False,
    )
```

```python
import functools

import jax
import jax.numpy as jnp
from jax import lax
from jax.experimental import pallas as pl
from jax.experimental.pallas import tpu as pltpu
from jax.sharding import PartitionSpec as P

HEADS = 64
HD = 128
SPAN = 4
PIECES = 4


EPSILON = 1e-06


def from_behind(x, axis, by):
    count = lax.axis_size(axis)
    pairs = [(i, i + by) for i in range(count) if 0 <= i + by < count]
    return lax.ppermute(x, axis, pairs)


def scan_window_permutes(element, reach, step):
    nearest = from_behind(element, "seq", step)
    second = from_behind(nearest, "seq", step)
    pair = nearest + (reach >= 2).astype(jnp.float32) * second
    far_pair = from_behind(pair, "seq", 2 * step)
    total = pair + (reach >= 3).astype(jnp.float32) * far_pair
    return (reach >= 1).astype(jnp.float32) * total


def chain_kernel(count, step, side_work, extra_in, prologue, pro_in, flag_ref, *refs):
    if prologue is None:
        element_ref, refs = refs[0], refs[1:]
    pro_refs = refs[:pro_in]
    refs = refs[pro_in:]
    side_in = refs[:extra_in]
    out_ref = refs[extra_in]
    if prologue is None:
        link_slot, state_slot, sent_slot, send_sems, recv_sems = refs[-5:]
        side_out = refs[extra_in + 1:-5]
    else:
        link_slot, state_slot, sent_slot, send_sems, recv_sems, element_ref = refs[-6:]
        side_out = refs[extra_in + 1:-6]
    me = lax.axis_index("seq")
    head = lax.axis_index("head")
    heads = element_ref.shape[0]
    pos = lax.rem(me, 4) if step == 1 else 3 - lax.rem(me + 2, 4)
    ahead_exists = (me + step >= 0) & (me + step < count)
    behind_exists = (me - step >= 0) & (me - step < count)

    barrier = pltpu.get_barrier_semaphore()
    for offset in (1, -1):
        ring_peer = (lax.rem(me + offset + count, count), head)
        pl.semaphore_signal(barrier, inc=1, device_id=ring_peer, device_id_type=pl.DeviceIdType.MESH)
    pl.semaphore_wait(barrier, 2)
    if prologue is not None:
        prologue(pro_refs, element_ref)

    def describe(kind, part, source, landing):
        return pltpu.make_async_remote_copy(
            src_ref=source,
            dst_ref=landing.at[part],
            send_sem=send_sems.at[kind, part],
            recv_sem=recv_sems.at[kind, part],
            device_id=(me + step, head),
            device_id_type=pl.DeviceIdType.MESH,
        )

    flag = flag_ref[0]
    sends = []
    for part in range(heads):
        @pl.when((pos >= 1) & behind_exists)
        def _():
            describe(0, part, link_slot.at[part], link_slot).wait_recv()
            link_slot[part] = element_ref[part] + flag * link_slot[part]

        @pl.when((pos == 0) | jnp.logical_not(behind_exists))
        def _():
            link_slot[part] = element_ref[part]

        into_link = describe(0, part, link_slot.at[part], link_slot)
        into_state = pltpu.make_async_remote_copy(
            src_ref=link_slot.at[part],
            dst_ref=state_slot.at[part],
            send_sem=send_sems.at[0, part],
            recv_sem=recv_sems.at[1, part],
            device_id=(me + step, head),
            device_id_type=pl.DeviceIdType.MESH,
        )

        @pl.when((pos <= 2) & ahead_exists)
        def _():
            into_link.start()

        @pl.when((pos == 3) & ahead_exists)
        def _():
            into_state.start()

        sends.append((into_link, into_state))
    side_work(side_in, side_out)
    state_sends = []
    for part in range(heads):
        @pl.when(behind_exists)
        def _():
            describe(1, part, state_slot.at[part], state_slot).wait_recv()

        @pl.when(jnp.logical_not(behind_exists))
        def _():
            state_slot[part] = jnp.zeros(state_slot.shape[1:], jnp.float32)

        out_ref[part] = state_slot[part]
        copy = describe(1, part, sent_slot.at[part], state_slot)

        @pl.when((pos <= 2) & ahead_exists)
        def _():
            sent_slot[part] = element_ref[part] + flag * state_slot[part]
            copy.start()

        state_sends.append(copy)
    for part in range(heads):
        into_link, into_state = sends[part]

        @pl.when((pos <= 2) & ahead_exists)
        def _():
            into_link.wait_send()

        @pl.when((pos == 3) & ahead_exists)
        def _():
            into_state.wait_send()

        @pl.when((pos <= 2) & ahead_exists)
        def _():
            state_sends[part].wait_send()


def no_side_work(side_in, side_out):
    del side_in, side_out


def backward_local(scale, side_in, side_out):
    query_ref, key_ref, value_ref, grad_ref, starts_ref = side_in
    query_out, key_out, value_out = side_out
    rows = query_ref.shape[0]
    row = lax.broadcasted_iota(jnp.int32, (rows, rows), 0)
    col = lax.broadcasted_iota(jnp.int32, (rows, rows), 1)
    begin = lax.axis_index("seq") * rows
    starts = jnp.broadcast_to(starts_ref[...], (rows, rows)).T
    inside = (begin + col >= starts) & (col <= row)
    contract_last = (((1,), (1,)), ((), ()))
    for part in range(query_ref.shape[1] // HD):
        cols = pl.ds(part * HD, HD)
        query_h = query_ref[:, cols]
        key_h = key_ref[:, cols]
        grad_h = grad_ref[:, cols]
        scores = lax.dot_general(query_h, key_h, contract_last, preferred_element_type=jnp.float32)
        scaled = jnp.where(inside, scale * scores, 0.0)
        grad_scores = lax.dot_general(
            grad_h, value_ref[:, cols], contract_last, preferred_element_type=jnp.float32
        )
        mixed = jnp.where(inside, scale * grad_scores, 0.0)
        query_out[:, cols] = jnp.dot(mixed.astype(jnp.bfloat16), key_h, preferred_element_type=jnp.float32)
        key_out[:, cols] = jnp.dot(mixed.T.astype(jnp.bfloat16), query_h, preferred_element_type=jnp.float32)
        value_out[:, cols] = jnp.dot(scaled.T.astype(jnp.bfloat16), grad_h, preferred_element_type=jnp.float32)


def forward_element(cut_ref, key_ref, value_ref, element_ref):
    rows = key_ref.shape[0]
    keep = lax.broadcasted_iota(jnp.int32, (rows, HD), 0) >= cut_ref[0]
    size = HD // PIECES
    for part in range(key_ref.shape[1] // HD):
        cols = pl.ds(part * HD, HD)
        kept = jnp.where(keep, key_ref[:, cols].astype(jnp.float32), 0.0).T.astype(jnp.bfloat16)
        block = jnp.dot(kept, value_ref[:, cols], preferred_element_type=jnp.float32)
        for piece in range(PIECES):
            element_ref[part * PIECES + piece] = block[piece * size:(piece + 1) * size, :]


def scan_window(element, flag, step, ident, side_work=no_side_work, side_inputs=(), side_shapes=(),
                prologue=None, prologue_inputs=(), shape=None):
    count = lax.axis_size("seq")
    shape = element.shape if element is not None else shape
    chunked = (shape[0] * PIECES, shape[1] // PIECES, shape[2])
    heads = chunked[0]
    vmem = pl.BlockSpec(memory_space=pltpu.VMEM)
    smem = pl.BlockSpec(memory_space=pltpu.SMEM)
    scratch = [
        pltpu.VMEM(chunked, jnp.float32),
        pltpu.VMEM(chunked, jnp.float32),
        pltpu.VMEM(chunked, jnp.float32),
        pltpu.SemaphoreType.DMA((2, heads)),
        pltpu.SemaphoreType.DMA((2, heads)),
    ]
    if prologue is None:
        leading = (element.reshape(chunked),)
        leading_specs = [vmem]
    else:
        leading = ()
        leading_specs = []
        scratch.append(pltpu.VMEM(chunked, jnp.float32))
    pro_specs = [smem] + [vmem] * (len(prologue_inputs) - 1) if prologue_inputs else []
    outs = pl.pallas_call(
        functools.partial(chain_kernel, count, step, side_work, len(side_inputs), prologue, len(prologue_inputs)),
        out_shape=(jax.ShapeDtypeStruct(chunked, jnp.float32),) + tuple(side_shapes),
        in_specs=[smem] + leading_specs + pro_specs + [vmem] * len(side_inputs),
        out_specs=(vmem,) * (1 + len(side_shapes)),
        scratch_shapes=scratch,
        compiler_params=pltpu.CompilerParams(collective_id=ident, has_side_effects=True),
    )(flag.astype(jnp.float32).reshape(1), *leading, *prologue_inputs, *side_inputs)
    return (outs[0].reshape(shape),) + tuple(outs[1:])

def head_sum_kernel(count, parts_ref, out_ref, slots, send_sems, recv_sems):
    me = lax.axis_index("head")
    row = lax.axis_index("seq")
    barrier = pltpu.get_barrier_semaphore()
    for shift in range(1, count):
        peer = (row, lax.rem(me + shift, count))
        pl.semaphore_signal(barrier, inc=1, device_id=peer, device_id_type=pl.DeviceIdType.MESH)
    pl.semaphore_wait(barrier, count - 1)
    copies = []
    for shift in range(1, count):
        copy = pltpu.make_async_remote_copy(
            src_ref=parts_ref,
            dst_ref=slots.at[me],
            send_sem=send_sems.at[shift],
            recv_sem=recv_sems.at[me],
            device_id=(row, lax.rem(me + shift, count)),
            device_id_type=pl.DeviceIdType.MESH,
        )
        copy.start()
        copies.append(copy)
    slots[me] = parts_ref[...]
    for shift in range(1, count):
        source = lax.rem(me + count - shift, count)
        pltpu.make_async_remote_copy(
            src_ref=parts_ref,
            dst_ref=slots.at[source],
            send_sem=send_sems.at[shift],
            recv_sem=recv_sems.at[source],
            device_id=(row, source),
            device_id_type=pl.DeviceIdType.MESH,
        ).wait_recv()
    total = slots[0]
    for index in range(1, count):
        total = total + slots[index]
    out_ref[...] = total
    for copy in copies:
        copy.wait_send()


def head_sum(square_sum, cross_sum):
    count = lax.axis_size("head")
    rows = square_sum.shape[0]
    parts = jnp.concatenate(
        [square_sum[None], cross_sum[None], jnp.zeros((6, rows), jnp.float32)], axis=0
    )
    total = pl.pallas_call(
        functools.partial(head_sum_kernel, count),
        out_shape=jax.ShapeDtypeStruct(parts.shape, jnp.float32),
        in_specs=[pl.BlockSpec(memory_space=pltpu.VMEM)],
        out_specs=pl.BlockSpec(memory_space=pltpu.VMEM),
        scratch_shapes=[
            pltpu.VMEM((count,) + parts.shape, jnp.float32),
            pltpu.SemaphoreType.DMA((count,)),
            pltpu.SemaphoreType.DMA((count,)),
        ],
        compiler_params=pltpu.CompilerParams(collective_id=2, has_side_effects=True),
    )(parts)
    return total[0], total[1]


def gradient_kernel(scale, query_ref, key_ref, value_ref, grad_ref, before_ref, after_ref,
                    carried_ref, returned_ref, query_local, key_local, value_local,
                    query_out, key_out, value_out):
    rows = query_ref.shape[0]
    begin = lax.axis_index("seq") * rows
    before = (jnp.broadcast_to(before_ref[...], (rows, rows)).T < begin).astype(jnp.float32)
    after = (jnp.broadcast_to(after_ref[...], (rows, rows)).T > begin + rows).astype(jnp.float32)
    contract_last = (((1,), (1,)), ((), ()))

    def halves(state):
        upper = state.astype(jnp.bfloat16)
        return upper, (state - upper.astype(jnp.float32)).astype(jnp.bfloat16)

    def across(rows, state, form):
        upper, lower = halves(state)
        if form == "nt":
            first = lax.dot_general(rows, upper, contract_last, preferred_element_type=jnp.float32)
            return first + lax.dot_general(rows, lower, contract_last, preferred_element_type=jnp.float32)
        first = jnp.dot(rows, upper, preferred_element_type=jnp.float32)
        return first + jnp.dot(rows, lower, preferred_element_type=jnp.float32)

    for part in range(query_ref.shape[1] // HD):
        cols = pl.ds(part * HD, HD)
        carried = carried_ref[part]
        returned = returned_ref[part]
        query_out[:, cols] = (
            query_local[:, cols] + before * scale * across(grad_ref[:, cols], carried, "nt")
        ).astype(jnp.bfloat16)
        key_out[:, cols] = (
            key_local[:, cols] + after * scale * across(value_ref[:, cols], returned, "nt")
        ).astype(jnp.bfloat16)
        value_out[:, cols] = (
            value_local[:, cols] + after * scale * across(key_ref[:, cols], returned, "nn")
        ).astype(jnp.bfloat16)


def gradients(scale, queries, key_rows, value_rows, grad_flat, before, after, carried, returned, local):
    flat = jax.ShapeDtypeStruct(queries.shape, jnp.bfloat16)
    vmem = pl.BlockSpec(memory_space=pltpu.VMEM)
    rows = queries.shape[0]
    wide = lambda bounds: bounds.reshape(1, rows)
    return pl.pallas_call(
        functools.partial(gradient_kernel, scale),
        out_shape=(flat, flat, flat),
        in_specs=[vmem] * 11,
        out_specs=(vmem, vmem, vmem),
    )(queries, key_rows, value_rows, grad_flat, wide(before), wide(after), carried, returned, *local)

def join_states(earlier_part, later_part):
    return (
        later_part[0] + (1.0 - later_part[1]) * earlier_part[0],
        jnp.maximum(earlier_part[1], later_part[1]),
    )


def split_state(state):
    upper = state.astype(jnp.bfloat16)
    lower = (state - upper.astype(jnp.float32)).astype(jnp.bfloat16)
    return (upper, lower)


def state_product(form, rows, state):
    upper, lower = split_state(state)
    first = jnp.einsum(form, rows, upper, preferred_element_type=jnp.float32)
    return first + jnp.einsum(form, rows, lower, preferred_element_type=jnp.float32)


def shards(queries, key_rows, value_rows, out_grad, norm_gain, dial_start, dial_end):
    token_count = queries.shape[0]
    head_count = queries.shape[1] // HD
    score_scale = HD ** (-0.5)
    width_all = HEADS * HD
    block_begin = lax.axis_index("seq") * token_count
    local_pos = jnp.arange(token_count, dtype=jnp.int32)
    position = block_begin + local_pos
    query_h = queries.reshape(token_count, head_count, HD)
    key_h = key_rows.reshape(token_count, head_count, HD)
    value_h = value_rows.reshape(token_count, head_count, HD)
    last_start = dial_start[token_count - 1]
    carried = scan_window(
        None, last_start < block_begin, 1, 0,
        prologue=lambda refs, out: forward_element(*refs, out),
        prologue_inputs=((last_start - block_begin).reshape(1), key_rows, value_rows),
        shape=(head_count, HD, HD),
    )[0]
    carried, query_h, key_h, value_h = lax.optimization_barrier((carried, query_h, key_h, value_h))
    inside = (position[None, :] >= dial_start[:, None]) & (local_pos[None, :] <= local_pos[:, None])
    scores = jnp.einsum("thd,shd->hts", query_h, key_h, preferred_element_type=jnp.float32)
    weights = jnp.where(inside[None], score_scale * scores, 0.0).astype(jnp.bfloat16)
    local_mix = jnp.einsum("hts,she->the", weights, value_h, preferred_element_type=jnp.float32)
    across = score_scale * state_product("thd,hde->the", query_h, carried)
    from_before = (dial_start < block_begin).astype(jnp.float32)[:, None, None]
    attended = (local_mix + from_before * across).reshape(token_count, head_count * HD)
    grad_wide = out_grad.astype(jnp.float32)
    square_sum, cross_sum = head_sum(
        jnp.sum(attended * attended, axis=1), jnp.sum(norm_gain * grad_wide * attended, axis=1)
    )
    inv_rms = lax.rsqrt(square_sum / width_all + EPSILON)
    normed = (attended * inv_rms[:, None] * norm_gain).astype(jnp.bfloat16)
    grad_attn = (
        inv_rms[:, None] * norm_gain * grad_wide
        - attended * (inv_rms * inv_rms * inv_rms * cross_sum / width_all)[:, None]
    )
    grad_weight = grad_attn.astype(jnp.bfloat16).reshape(token_count, head_count, HD)
    first_end = dial_end[0]
    keep_first = position < first_end
    back_element = jnp.einsum(
        "thd,the->hde",
        jnp.where(keep_first[:, None, None], query_h, jnp.zeros((), jnp.bfloat16)),
        grad_weight,
        preferred_element_type=jnp.float32,
    )
    wide_shape = jax.ShapeDtypeStruct(queries.shape, jnp.float32)
    grad_flat = grad_weight.reshape(queries.shape)
    returned, *local = scan_window(
        back_element, first_end > block_begin + token_count, -1, 1,
        functools.partial(backward_local, score_scale),
        (queries, key_rows, value_rows, grad_flat, dial_start.reshape(1, token_count)),
        (wide_shape,) * 3,
    )
    query_grad, key_grad, value_grad = gradients(
        score_scale, queries, key_rows, value_rows, grad_flat,
        dial_start, dial_end, carried, returned, local,
    )
    return (normed, query_grad, key_grad, value_grad)


def solution(mesh):
    placed = (
        P("seq", "head"),
        P("seq", "head"),
        P("seq", "head"),
        P("seq", "head"),
        P("head"),
        P("seq"),
        P("seq"),
    )
    return jax.shard_map(
        shards,
        mesh=mesh,
        in_specs=placed,
        out_specs=(P("seq", "head"), P("seq", "head"), P("seq", "head"), P("seq", "head")),
        check_vma=False,
    )
```

```python
import functools

import jax
import jax.numpy as jnp
from jax import lax
from jax.experimental import pallas as pl
from jax.experimental.pallas import tpu as pltpu
from jax.sharding import PartitionSpec as P

HEADS = 64
HD = 128
SPAN = 4
PIECES = 4


EPSILON = 1e-06


def from_behind(x, axis, by):
    count = lax.axis_size(axis)
    pairs = [(i, i + by) for i in range(count) if 0 <= i + by < count]
    return lax.ppermute(x, axis, pairs)


def scan_window_permutes(element, reach, step):
    nearest = from_behind(element, "seq", step)
    second = from_behind(nearest, "seq", step)
    pair = nearest + (reach >= 2).astype(jnp.float32) * second
    far_pair = from_behind(pair, "seq", 2 * step)
    total = pair + (reach >= 3).astype(jnp.float32) * far_pair
    return (reach >= 1).astype(jnp.float32) * total


def chain_kernel(count, step, side_work, extra_in, prologue, pro_in, flag_ref, *refs):
    if prologue is None:
        element_ref, refs = refs[0], refs[1:]
    pro_refs = refs[:pro_in]
    refs = refs[pro_in:]
    side_in = refs[:extra_in]
    out_ref = refs[extra_in]
    if prologue is None:
        link_slot, state_slot, sent_slot, send_sems, recv_sems = refs[-5:]
        side_out = refs[extra_in + 1:-5]
    else:
        link_slot, state_slot, sent_slot, send_sems, recv_sems, element_ref = refs[-6:]
        side_out = refs[extra_in + 1:-6]
    me = lax.axis_index("seq")
    head = lax.axis_index("head")
    heads = element_ref.shape[0]
    pos = lax.rem(me, 4) if step == 1 else 3 - lax.rem(me + 2, 4)
    ahead_exists = (me + step >= 0) & (me + step < count)
    behind_exists = (me - step >= 0) & (me - step < count)

    barrier = pltpu.get_barrier_semaphore()
    for offset in (1, -1):
        ring_peer = (lax.rem(me + offset + count, count), head)
        pl.semaphore_signal(barrier, inc=1, device_id=ring_peer, device_id_type=pl.DeviceIdType.MESH)
    pl.semaphore_wait(barrier, 2)
    if prologue is not None:
        prologue(pro_refs, element_ref)

    def describe(kind, part, source, landing):
        return pltpu.make_async_remote_copy(
            src_ref=source,
            dst_ref=landing.at[part],
            send_sem=send_sems.at[kind, part],
            recv_sem=recv_sems.at[kind, part],
            device_id=(me + step, head),
            device_id_type=pl.DeviceIdType.MESH,
        )

    flag = flag_ref[0]
    sends = []
    for part in range(heads):
        @pl.when((pos >= 1) & behind_exists)
        def _():
            describe(0, part, link_slot.at[part], link_slot).wait_recv()
            link_slot[part] = element_ref[part] + flag * link_slot[part]

        @pl.when((pos == 0) | jnp.logical_not(behind_exists))
        def _():
            link_slot[part] = element_ref[part]

        into_link = describe(0, part, link_slot.at[part], link_slot)
        into_state = pltpu.make_async_remote_copy(
            src_ref=link_slot.at[part],
            dst_ref=state_slot.at[part],
            send_sem=send_sems.at[0, part],
            recv_sem=recv_sems.at[1, part],
            device_id=(me + step, head),
            device_id_type=pl.DeviceIdType.MESH,
        )

        @pl.when((pos <= 2) & ahead_exists)
        def _():
            into_link.start()

        @pl.when((pos == 3) & ahead_exists)
        def _():
            into_state.start()

        sends.append((into_link, into_state))
    side_work(side_in, side_out)
    state_sends = []
    for part in range(heads):
        @pl.when(behind_exists)
        def _():
            describe(1, part, state_slot.at[part], state_slot).wait_recv()

        @pl.when(jnp.logical_not(behind_exists))
        def _():
            state_slot[part] = jnp.zeros(state_slot.shape[1:], jnp.float32)

        out_ref[part] = state_slot[part]
        copy = describe(1, part, sent_slot.at[part], state_slot)

        @pl.when((pos <= 2) & ahead_exists)
        def _():
            sent_slot[part] = element_ref[part] + flag * state_slot[part]
            copy.start()

        state_sends.append(copy)
    for part in range(heads):
        into_link, into_state = sends[part]

        @pl.when((pos <= 2) & ahead_exists)
        def _():
            into_link.wait_send()

        @pl.when((pos == 3) & ahead_exists)
        def _():
            into_state.wait_send()

        @pl.when((pos <= 2) & ahead_exists)
        def _():
            state_sends[part].wait_send()


def no_side_work(side_in, side_out):
    del side_in, side_out


def backward_local(scale, side_in, side_out):
    query_ref, key_ref, value_ref, grad_ref, starts_ref = side_in
    query_out, key_out, value_out = side_out
    rows = query_ref.shape[0]
    row = lax.broadcasted_iota(jnp.int32, (rows, rows), 0)
    col = lax.broadcasted_iota(jnp.int32, (rows, rows), 1)
    begin = lax.axis_index("seq") * rows
    starts = jnp.broadcast_to(starts_ref[...], (rows, rows)).T
    inside = (begin + col >= starts) & (col <= row)
    contract_last = (((1,), (1,)), ((), ()))
    for part in range(query_ref.shape[1] // HD):
        cols = pl.ds(part * HD, HD)
        query_h = query_ref[:, cols]
        key_h = key_ref[:, cols]
        grad_h = grad_ref[:, cols]
        scores = lax.dot_general(query_h, key_h, contract_last, preferred_element_type=jnp.float32)
        scaled = jnp.where(inside, scale * scores, 0.0)
        grad_scores = lax.dot_general(
            grad_h, value_ref[:, cols], contract_last, preferred_element_type=jnp.float32
        )
        mixed = jnp.where(inside, scale * grad_scores, 0.0)
        query_out[:, cols] = jnp.dot(mixed.astype(jnp.bfloat16), key_h, preferred_element_type=jnp.float32)
        key_out[:, cols] = jnp.dot(mixed.T.astype(jnp.bfloat16), query_h, preferred_element_type=jnp.float32)
        value_out[:, cols] = jnp.dot(scaled.T.astype(jnp.bfloat16), grad_h, preferred_element_type=jnp.float32)


def forward_element(cut_ref, key_ref, value_ref, element_ref, below=False):
    rows = key_ref.shape[0]
    index = lax.broadcasted_iota(jnp.int32, (rows, HD), 0)
    keep = index < cut_ref[0] if below else index >= cut_ref[0]
    size = HD // PIECES
    for part in range(key_ref.shape[1] // HD):
        cols = pl.ds(part * HD, HD)
        kept = jnp.where(keep, key_ref[:, cols].astype(jnp.float32), 0.0).T.astype(jnp.bfloat16)
        block = jnp.dot(kept, value_ref[:, cols], preferred_element_type=jnp.float32)
        for piece in range(PIECES):
            element_ref[part * PIECES + piece] = block[piece * size:(piece + 1) * size, :]


def scan_window(element, flag, step, ident, side_work=no_side_work, side_inputs=(), side_shapes=(),
                prologue=None, prologue_inputs=(), shape=None):
    count = lax.axis_size("seq")
    shape = element.shape if element is not None else shape
    chunked = (shape[0] * PIECES, shape[1] // PIECES, shape[2])
    heads = chunked[0]
    vmem = pl.BlockSpec(memory_space=pltpu.VMEM)
    smem = pl.BlockSpec(memory_space=pltpu.SMEM)
    scratch = [
        pltpu.VMEM(chunked, jnp.float32),
        pltpu.VMEM(chunked, jnp.float32),
        pltpu.VMEM(chunked, jnp.float32),
        pltpu.SemaphoreType.DMA((2, heads)),
        pltpu.SemaphoreType.DMA((2, heads)),
    ]
    if prologue is None:
        leading = (element.reshape(chunked),)
        leading_specs = [vmem]
    else:
        leading = ()
        leading_specs = []
        scratch.append(pltpu.VMEM(chunked, jnp.float32))
    pro_specs = [smem] + [vmem] * (len(prologue_inputs) - 1) if prologue_inputs else []
    outs = pl.pallas_call(
        functools.partial(chain_kernel, count, step, side_work, len(side_inputs), prologue, len(prologue_inputs)),
        out_shape=(jax.ShapeDtypeStruct(chunked, jnp.float32),) + tuple(side_shapes),
        in_specs=[smem] + leading_specs + pro_specs + [vmem] * len(side_inputs),
        out_specs=(vmem,) * (1 + len(side_shapes)),
        scratch_shapes=scratch,
        compiler_params=pltpu.CompilerParams(collective_id=ident, has_side_effects=True),
    )(flag.astype(jnp.float32).reshape(1), *leading, *prologue_inputs, *side_inputs)
    return (outs[0].reshape(shape),) + tuple(outs[1:])

def head_sum_kernel(count, parts_ref, out_ref, slots, send_sems, recv_sems):
    me = lax.axis_index("head")
    row = lax.axis_index("seq")
    barrier = pltpu.get_barrier_semaphore()
    for shift in range(1, count):
        peer = (row, lax.rem(me + shift, count))
        pl.semaphore_signal(barrier, inc=1, device_id=peer, device_id_type=pl.DeviceIdType.MESH)
    pl.semaphore_wait(barrier, count - 1)
    copies = []
    for shift in range(1, count):
        copy = pltpu.make_async_remote_copy(
            src_ref=parts_ref,
            dst_ref=slots.at[me],
            send_sem=send_sems.at[shift],
            recv_sem=recv_sems.at[me],
            device_id=(row, lax.rem(me + shift, count)),
            device_id_type=pl.DeviceIdType.MESH,
        )
        copy.start()
        copies.append(copy)
    slots[me] = parts_ref[...]
    for shift in range(1, count):
        source = lax.rem(me + count - shift, count)
        pltpu.make_async_remote_copy(
            src_ref=parts_ref,
            dst_ref=slots.at[source],
            send_sem=send_sems.at[shift],
            recv_sem=recv_sems.at[source],
            device_id=(row, source),
            device_id_type=pl.DeviceIdType.MESH,
        ).wait_recv()
    total = slots[0]
    for index in range(1, count):
        total = total + slots[index]
    out_ref[...] = total
    for copy in copies:
        copy.wait_send()


def head_sum(square_sum, cross_sum):
    count = lax.axis_size("head")
    rows = square_sum.shape[0]
    parts = jnp.concatenate(
        [square_sum[None], cross_sum[None], jnp.zeros((6, rows), jnp.float32)], axis=0
    )
    total = pl.pallas_call(
        functools.partial(head_sum_kernel, count),
        out_shape=jax.ShapeDtypeStruct(parts.shape, jnp.float32),
        in_specs=[pl.BlockSpec(memory_space=pltpu.VMEM)],
        out_specs=pl.BlockSpec(memory_space=pltpu.VMEM),
        scratch_shapes=[
            pltpu.VMEM((count,) + parts.shape, jnp.float32),
            pltpu.SemaphoreType.DMA((count,)),
            pltpu.SemaphoreType.DMA((count,)),
        ],
        compiler_params=pltpu.CompilerParams(collective_id=2, has_side_effects=True),
    )(parts)
    return total[0], total[1]


def gradient_kernel(scale, query_ref, key_ref, value_ref, grad_ref, before_ref, after_ref,
                    carried_ref, returned_ref, query_local, key_local, value_local,
                    query_out, key_out, value_out):
    rows = query_ref.shape[0]
    begin = lax.axis_index("seq") * rows
    before = (jnp.broadcast_to(before_ref[...], (rows, rows)).T < begin).astype(jnp.float32)
    after = (jnp.broadcast_to(after_ref[...], (rows, rows)).T > begin + rows).astype(jnp.float32)
    contract_last = (((1,), (1,)), ((), ()))

    def halves(state):
        upper = state.astype(jnp.bfloat16)
        return upper, (state - upper.astype(jnp.float32)).astype(jnp.bfloat16)

    def across(rows, state, form):
        upper, lower = halves(state)
        if form == "nt":
            first = lax.dot_general(rows, upper, contract_last, preferred_element_type=jnp.float32)
            return first + lax.dot_general(rows, lower, contract_last, preferred_element_type=jnp.float32)
        first = jnp.dot(rows, upper, preferred_element_type=jnp.float32)
        return first + jnp.dot(rows, lower, preferred_element_type=jnp.float32)

    for part in range(query_ref.shape[1] // HD):
        cols = pl.ds(part * HD, HD)
        carried = carried_ref[part]
        returned = returned_ref[part]
        query_out[:, cols] = (
            query_local[:, cols] + before * scale * across(grad_ref[:, cols], carried, "nt")
        ).astype(jnp.bfloat16)
        key_out[:, cols] = (
            key_local[:, cols] + after * scale * across(value_ref[:, cols], returned, "nt")
        ).astype(jnp.bfloat16)
        value_out[:, cols] = (
            value_local[:, cols] + after * scale * across(key_ref[:, cols], returned, "nn")
        ).astype(jnp.bfloat16)


def gradients(scale, queries, key_rows, value_rows, grad_flat, before, after, carried, returned, local):
    flat = jax.ShapeDtypeStruct(queries.shape, jnp.bfloat16)
    vmem = pl.BlockSpec(memory_space=pltpu.VMEM)
    rows = queries.shape[0]
    wide = lambda bounds: bounds.reshape(1, rows)
    return pl.pallas_call(
        functools.partial(gradient_kernel, scale),
        out_shape=(flat, flat, flat),
        in_specs=[vmem] * 11,
        out_specs=(vmem, vmem, vmem),
    )(queries, key_rows, value_rows, grad_flat, wide(before), wide(after), carried, returned, *local)

def join_states(earlier_part, later_part):
    return (
        later_part[0] + (1.0 - later_part[1]) * earlier_part[0],
        jnp.maximum(earlier_part[1], later_part[1]),
    )


def split_state(state):
    upper = state.astype(jnp.bfloat16)
    lower = (state - upper.astype(jnp.float32)).astype(jnp.bfloat16)
    return (upper, lower)


def state_product(form, rows, state):
    upper, lower = split_state(state)
    first = jnp.einsum(form, rows, upper, preferred_element_type=jnp.float32)
    return first + jnp.einsum(form, rows, lower, preferred_element_type=jnp.float32)


def shards(queries, key_rows, value_rows, out_grad, norm_gain, dial_start, dial_end):
    token_count = queries.shape[0]
    head_count = queries.shape[1] // HD
    score_scale = HD ** (-0.5)
    width_all = HEADS * HD
    block_begin = lax.axis_index("seq") * token_count
    local_pos = jnp.arange(token_count, dtype=jnp.int32)
    position = block_begin + local_pos
    query_h = queries.reshape(token_count, head_count, HD)
    key_h = key_rows.reshape(token_count, head_count, HD)
    value_h = value_rows.reshape(token_count, head_count, HD)
    last_start = dial_start[token_count - 1]
    carried = scan_window(
        None, last_start < block_begin, 1, 0,
        prologue=lambda refs, out: forward_element(*refs, out),
        prologue_inputs=((last_start - block_begin).reshape(1), key_rows, value_rows),
        shape=(head_count, HD, HD),
    )[0]
    carried, query_h, key_h, value_h = lax.optimization_barrier((carried, query_h, key_h, value_h))
    inside = (position[None, :] >= dial_start[:, None]) & (local_pos[None, :] <= local_pos[:, None])
    scores = jnp.einsum("thd,shd->hts", query_h, key_h, preferred_element_type=jnp.float32)
    weights = jnp.where(inside[None], score_scale * scores, 0.0).astype(jnp.bfloat16)
    local_mix = jnp.einsum("hts,she->the", weights, value_h, preferred_element_type=jnp.float32)
    across = score_scale * state_product("thd,hde->the", query_h, carried)
    from_before = (dial_start < block_begin).astype(jnp.float32)[:, None, None]
    attended = (local_mix + from_before * across).reshape(token_count, head_count * HD)
    grad_wide = out_grad.astype(jnp.float32)
    square_sum, cross_sum = head_sum(
        jnp.sum(attended * attended, axis=1), jnp.sum(norm_gain * grad_wide * attended, axis=1)
    )
    inv_rms = lax.rsqrt(square_sum / width_all + EPSILON)
    normed = (attended * inv_rms[:, None] * norm_gain).astype(jnp.bfloat16)
    grad_attn = (
        inv_rms[:, None] * norm_gain * grad_wide
        - attended * (inv_rms * inv_rms * inv_rms * cross_sum / width_all)[:, None]
    )
    grad_weight = grad_attn.astype(jnp.bfloat16).reshape(token_count, head_count, HD)
    first_end = dial_end[0]
    keep_first = position < first_end
    wide_shape = jax.ShapeDtypeStruct(queries.shape, jnp.float32)
    grad_flat = grad_weight.reshape(queries.shape)
    returned, *local = scan_window(
        None, first_end > block_begin + token_count, -1, 1,
        functools.partial(backward_local, score_scale),
        (queries, key_rows, value_rows, grad_flat, dial_start.reshape(1, token_count)),
        (wide_shape,) * 3,
        prologue=lambda refs, out: forward_element(*refs, out, below=True),
        prologue_inputs=((first_end - block_begin).reshape(1), queries, grad_flat),
        shape=(head_count, HD, HD),
    )
    query_grad, key_grad, value_grad = gradients(
        score_scale, queries, key_rows, value_rows, grad_flat,
        dial_start, dial_end, carried, returned, local,
    )
    return (normed, query_grad, key_grad, value_grad)


def solution(mesh):
    placed = (
        P("seq", "head"),
        P("seq", "head"),
        P("seq", "head"),
        P("seq", "head"),
        P("head"),
        P("seq"),
        P("seq"),
    )
    return jax.shard_map(
        shards,
        mesh=mesh,
        in_specs=placed,
        out_specs=(P("seq", "head"), P("seq", "head"), P("seq", "head"), P("seq", "head")),
        check_vma=False,
    )
```

```python
import functools

import jax
import jax.numpy as jnp
from jax import lax
from jax.experimental import pallas as pl
from jax.experimental.pallas import tpu as pltpu
from jax.sharding import PartitionSpec as P

HEADS = 64
HD = 128
SPAN = 4
PIECES = 4


EPSILON = 1e-06


def from_behind(x, axis, by):
    count = lax.axis_size(axis)
    pairs = [(i, i + by) for i in range(count) if 0 <= i + by < count]
    return lax.ppermute(x, axis, pairs)


def scan_window_permutes(element, reach, step):
    nearest = from_behind(element, "seq", step)
    second = from_behind(nearest, "seq", step)
    pair = nearest + (reach >= 2).astype(jnp.float32) * second
    far_pair = from_behind(pair, "seq", 2 * step)
    total = pair + (reach >= 3).astype(jnp.float32) * far_pair
    return (reach >= 1).astype(jnp.float32) * total


def chain_kernel(count, step, side_work, extra_in, prologue, pro_in, flag_ref, *refs):
    if prologue is None:
        element_ref, refs = refs[0], refs[1:]
    pro_refs = refs[:pro_in]
    refs = refs[pro_in:]
    side_in = refs[:extra_in]
    out_ref = refs[extra_in]
    if prologue is None:
        link_slot, state_slot, sent_slot, send_sems, recv_sems = refs[-5:]
        side_out = refs[extra_in + 1:-5]
    else:
        link_slot, state_slot, sent_slot, send_sems, recv_sems, element_ref = refs[-6:]
        side_out = refs[extra_in + 1:-6]
    me = lax.axis_index("seq")
    head = lax.axis_index("head")
    heads = element_ref.shape[0]
    pos = lax.rem(me, 4) if step == 1 else 3 - lax.rem(me + 2, 4)
    ahead_exists = (me + step >= 0) & (me + step < count)
    behind_exists = (me - step >= 0) & (me - step < count)

    barrier = pltpu.get_barrier_semaphore()
    for offset in (1, -1):
        ring_peer = (lax.rem(me + offset + count, count), head)
        pl.semaphore_signal(barrier, inc=1, device_id=ring_peer, device_id_type=pl.DeviceIdType.MESH)
    pl.semaphore_wait(barrier, 2)
    if prologue is not None:
        prologue(pro_refs, element_ref)

    def describe(kind, part, source, landing):
        return pltpu.make_async_remote_copy(
            src_ref=source,
            dst_ref=landing.at[part],
            send_sem=send_sems.at[kind, part],
            recv_sem=recv_sems.at[kind, part],
            device_id=(me + step, head),
            device_id_type=pl.DeviceIdType.MESH,
        )

    flag = flag_ref[0]
    sends = []
    for part in range(heads):
        @pl.when((pos >= 1) & behind_exists)
        def _():
            describe(0, part, link_slot.at[part], link_slot).wait_recv()
            link_slot[part] = element_ref[part] + flag * link_slot[part]

        @pl.when((pos == 0) | jnp.logical_not(behind_exists))
        def _():
            link_slot[part] = element_ref[part]

        into_link = describe(0, part, link_slot.at[part], link_slot)
        into_state = pltpu.make_async_remote_copy(
            src_ref=link_slot.at[part],
            dst_ref=state_slot.at[part],
            send_sem=send_sems.at[0, part],
            recv_sem=recv_sems.at[1, part],
            device_id=(me + step, head),
            device_id_type=pl.DeviceIdType.MESH,
        )

        @pl.when((pos <= 2) & ahead_exists)
        def _():
            into_link.start()

        @pl.when((pos == 3) & ahead_exists)
        def _():
            into_state.start()

        sends.append((into_link, into_state))
    side_work(side_in, side_out)
    state_sends = []
    for part in range(heads):
        @pl.when(behind_exists)
        def _():
            describe(1, part, state_slot.at[part], state_slot).wait_recv()

        @pl.when(jnp.logical_not(behind_exists))
        def _():
            state_slot[part] = jnp.zeros(state_slot.shape[1:], jnp.float32)

        out_ref[part] = state_slot[part]
        copy = describe(1, part, sent_slot.at[part], state_slot)

        @pl.when((pos <= 2) & ahead_exists)
        def _():
            sent_slot[part] = element_ref[part] + flag * state_slot[part]
            copy.start()

        state_sends.append(copy)
    for part in range(heads):
        into_link, into_state = sends[part]

        @pl.when((pos <= 2) & ahead_exists)
        def _():
            into_link.wait_send()

        @pl.when((pos == 3) & ahead_exists)
        def _():
            into_state.wait_send()

        @pl.when((pos <= 2) & ahead_exists)
        def _():
            state_sends[part].wait_send()


def no_side_work(side_in, side_out):
    del side_in, side_out


def backward_local(scale, side_in, side_out):
    query_ref, key_ref, value_ref, grad_ref, starts_ref, carried_ref = side_in
    query_out, key_out, value_out = side_out
    rows = query_ref.shape[0]
    row = lax.broadcasted_iota(jnp.int32, (rows, rows), 0)
    col = lax.broadcasted_iota(jnp.int32, (rows, rows), 1)
    begin = lax.axis_index("seq") * rows
    starts = jnp.broadcast_to(starts_ref[...], (rows, rows)).T
    before = (starts < begin).astype(jnp.float32)
    inside = (begin + col >= starts) & (col <= row)
    contract_last = (((1,), (1,)), ((), ()))
    for part in range(query_ref.shape[1] // HD):
        cols = pl.ds(part * HD, HD)
        query_h = query_ref[:, cols]
        key_h = key_ref[:, cols]
        grad_h = grad_ref[:, cols]
        scores = lax.dot_general(query_h, key_h, contract_last, preferred_element_type=jnp.float32)
        scaled = jnp.where(inside, scale * scores, 0.0)
        grad_scores = lax.dot_general(
            grad_h, value_ref[:, cols], contract_last, preferred_element_type=jnp.float32
        )
        mixed = jnp.where(inside, scale * grad_scores, 0.0)
        upper = carried_ref[part].astype(jnp.bfloat16)
        lower = (carried_ref[part] - upper.astype(jnp.float32)).astype(jnp.bfloat16)
        across = lax.dot_general(grad_h, upper, contract_last, preferred_element_type=jnp.float32)
        across = across + lax.dot_general(grad_h, lower, contract_last, preferred_element_type=jnp.float32)
        query_out[:, cols] = jnp.dot(
            mixed.astype(jnp.bfloat16), key_h, preferred_element_type=jnp.float32
        ) + before * scale * across
        key_out[:, cols] = jnp.dot(mixed.T.astype(jnp.bfloat16), query_h, preferred_element_type=jnp.float32)
        value_out[:, cols] = jnp.dot(scaled.T.astype(jnp.bfloat16), grad_h, preferred_element_type=jnp.float32)


def forward_element(cut_ref, key_ref, value_ref, element_ref, below=False):
    rows = key_ref.shape[0]
    index = lax.broadcasted_iota(jnp.int32, (rows, HD), 0)
    keep = index < cut_ref[0] if below else index >= cut_ref[0]
    size = HD // PIECES
    for part in range(key_ref.shape[1] // HD):
        cols = pl.ds(part * HD, HD)
        kept = jnp.where(keep, key_ref[:, cols].astype(jnp.float32), 0.0).T.astype(jnp.bfloat16)
        block = jnp.dot(kept, value_ref[:, cols], preferred_element_type=jnp.float32)
        for piece in range(PIECES):
            element_ref[part * PIECES + piece] = block[piece * size:(piece + 1) * size, :]


def scan_window(element, flag, step, ident, side_work=no_side_work, side_inputs=(), side_shapes=(),
                prologue=None, prologue_inputs=(), shape=None):
    count = lax.axis_size("seq")
    shape = element.shape if element is not None else shape
    chunked = (shape[0] * PIECES, shape[1] // PIECES, shape[2])
    heads = chunked[0]
    vmem = pl.BlockSpec(memory_space=pltpu.VMEM)
    smem = pl.BlockSpec(memory_space=pltpu.SMEM)
    scratch = [
        pltpu.VMEM(chunked, jnp.float32),
        pltpu.VMEM(chunked, jnp.float32),
        pltpu.VMEM(chunked, jnp.float32),
        pltpu.SemaphoreType.DMA((2, heads)),
        pltpu.SemaphoreType.DMA((2, heads)),
    ]
    if prologue is None:
        leading = (element.reshape(chunked),)
        leading_specs = [vmem]
    else:
        leading = ()
        leading_specs = []
        scratch.append(pltpu.VMEM(chunked, jnp.float32))
    pro_specs = [smem] + [vmem] * (len(prologue_inputs) - 1) if prologue_inputs else []
    outs = pl.pallas_call(
        functools.partial(chain_kernel, count, step, side_work, len(side_inputs), prologue, len(prologue_inputs)),
        out_shape=(jax.ShapeDtypeStruct(chunked, jnp.float32),) + tuple(side_shapes),
        in_specs=[smem] + leading_specs + pro_specs + [vmem] * len(side_inputs),
        out_specs=(vmem,) * (1 + len(side_shapes)),
        scratch_shapes=scratch,
        compiler_params=pltpu.CompilerParams(collective_id=ident, has_side_effects=True),
    )(flag.astype(jnp.float32).reshape(1), *leading, *prologue_inputs, *side_inputs)
    return (outs[0].reshape(shape),) + tuple(outs[1:])

def head_sum_kernel(count, parts_ref, out_ref, slots, send_sems, recv_sems):
    me = lax.axis_index("head")
    row = lax.axis_index("seq")
    barrier = pltpu.get_barrier_semaphore()
    for shift in range(1, count):
        peer = (row, lax.rem(me + shift, count))
        pl.semaphore_signal(barrier, inc=1, device_id=peer, device_id_type=pl.DeviceIdType.MESH)
    pl.semaphore_wait(barrier, count - 1)
    copies = []
    for shift in range(1, count):
        copy = pltpu.make_async_remote_copy(
            src_ref=parts_ref,
            dst_ref=slots.at[me],
            send_sem=send_sems.at[shift],
            recv_sem=recv_sems.at[me],
            device_id=(row, lax.rem(me + shift, count)),
            device_id_type=pl.DeviceIdType.MESH,
        )
        copy.start()
        copies.append(copy)
    slots[me] = parts_ref[...]
    for shift in range(1, count):
        source = lax.rem(me + count - shift, count)
        pltpu.make_async_remote_copy(
            src_ref=parts_ref,
            dst_ref=slots.at[source],
            send_sem=send_sems.at[shift],
            recv_sem=recv_sems.at[source],
            device_id=(row, source),
            device_id_type=pl.DeviceIdType.MESH,
        ).wait_recv()
    total = slots[0]
    for index in range(1, count):
        total = total + slots[index]
    out_ref[...] = total
    for copy in copies:
        copy.wait_send()


def head_sum(square_sum, cross_sum):
    count = lax.axis_size("head")
    rows = square_sum.shape[0]
    parts = jnp.concatenate(
        [square_sum[None], cross_sum[None], jnp.zeros((6, rows), jnp.float32)], axis=0
    )
    total = pl.pallas_call(
        functools.partial(head_sum_kernel, count),
        out_shape=jax.ShapeDtypeStruct(parts.shape, jnp.float32),
        in_specs=[pl.BlockSpec(memory_space=pltpu.VMEM)],
        out_specs=pl.BlockSpec(memory_space=pltpu.VMEM),
        scratch_shapes=[
            pltpu.VMEM((count,) + parts.shape, jnp.float32),
            pltpu.SemaphoreType.DMA((count,)),
            pltpu.SemaphoreType.DMA((count,)),
        ],
        compiler_params=pltpu.CompilerParams(collective_id=2, has_side_effects=True),
    )(parts)
    return total[0], total[1]


def gradient_kernel(scale, query_ref, key_ref, value_ref, grad_ref, before_ref, after_ref,
                    carried_ref, returned_ref, query_local, key_local, value_local,
                    query_out, key_out, value_out):
    rows = query_ref.shape[0]
    begin = lax.axis_index("seq") * rows
    before = (jnp.broadcast_to(before_ref[...], (rows, rows)).T < begin).astype(jnp.float32)
    after = (jnp.broadcast_to(after_ref[...], (rows, rows)).T > begin + rows).astype(jnp.float32)
    contract_last = (((1,), (1,)), ((), ()))

    def halves(state):
        upper = state.astype(jnp.bfloat16)
        return upper, (state - upper.astype(jnp.float32)).astype(jnp.bfloat16)

    def across(rows, state, form):
        upper, lower = halves(state)
        if form == "nt":
            first = lax.dot_general(rows, upper, contract_last, preferred_element_type=jnp.float32)
            return first + lax.dot_general(rows, lower, contract_last, preferred_element_type=jnp.float32)
        first = jnp.dot(rows, upper, preferred_element_type=jnp.float32)
        return first + jnp.dot(rows, lower, preferred_element_type=jnp.float32)

    for part in range(query_ref.shape[1] // HD):
        cols = pl.ds(part * HD, HD)
        carried = carried_ref[part]
        returned = returned_ref[part]
        query_out[:, cols] = query_local[:, cols].astype(jnp.bfloat16)
        key_out[:, cols] = (
            key_local[:, cols] + after * scale * across(value_ref[:, cols], returned, "nt")
        ).astype(jnp.bfloat16)
        value_out[:, cols] = (
            value_local[:, cols] + after * scale * across(key_ref[:, cols], returned, "nn")
        ).astype(jnp.bfloat16)


def gradients(scale, queries, key_rows, value_rows, grad_flat, before, after, carried, returned, local):
    flat = jax.ShapeDtypeStruct(queries.shape, jnp.bfloat16)
    vmem = pl.BlockSpec(memory_space=pltpu.VMEM)
    rows = queries.shape[0]
    wide = lambda bounds: bounds.reshape(1, rows)
    return pl.pallas_call(
        functools.partial(gradient_kernel, scale),
        out_shape=(flat, flat, flat),
        in_specs=[vmem] * 11,
        out_specs=(vmem, vmem, vmem),
    )(queries, key_rows, value_rows, grad_flat, wide(before), wide(after), carried, returned, *local)

def join_states(earlier_part, later_part):
    return (
        later_part[0] + (1.0 - later_part[1]) * earlier_part[0],
        jnp.maximum(earlier_part[1], later_part[1]),
    )


def split_state(state):
    upper = state.astype(jnp.bfloat16)
    lower = (state - upper.astype(jnp.float32)).astype(jnp.bfloat16)
    return (upper, lower)


def state_product(form, rows, state):
    upper, lower = split_state(state)
    first = jnp.einsum(form, rows, upper, preferred_element_type=jnp.float32)
    return first + jnp.einsum(form, rows, lower, preferred_element_type=jnp.float32)


def shards(queries, key_rows, value_rows, out_grad, norm_gain, dial_start, dial_end):
    token_count = queries.shape[0]
    head_count = queries.shape[1] // HD
    score_scale = HD ** (-0.5)
    width_all = HEADS * HD
    block_begin = lax.axis_index("seq") * token_count
    local_pos = jnp.arange(token_count, dtype=jnp.int32)
    position = block_begin + local_pos
    query_h = queries.reshape(token_count, head_count, HD)
    key_h = key_rows.reshape(token_count, head_count, HD)
    value_h = value_rows.reshape(token_count, head_count, HD)
    last_start = dial_start[token_count - 1]
    carried = scan_window(
        None, last_start < block_begin, 1, 0,
        prologue=lambda refs, out: forward_element(*refs, out),
        prologue_inputs=((last_start - block_begin).reshape(1), key_rows, value_rows),
        shape=(head_count, HD, HD),
    )[0]
    carried, query_h, key_h, value_h = lax.optimization_barrier((carried, query_h, key_h, value_h))
    inside = (position[None, :] >= dial_start[:, None]) & (local_pos[None, :] <= local_pos[:, None])
    scores = jnp.einsum("thd,shd->hts", query_h, key_h, preferred_element_type=jnp.float32)
    weights = jnp.where(inside[None], score_scale * scores, 0.0).astype(jnp.bfloat16)
    local_mix = jnp.einsum("hts,she->the", weights, value_h, preferred_element_type=jnp.float32)
    across = score_scale * state_product("thd,hde->the", query_h, carried)
    from_before = (dial_start < block_begin).astype(jnp.float32)[:, None, None]
    attended = (local_mix + from_before * across).reshape(token_count, head_count * HD)
    grad_wide = out_grad.astype(jnp.float32)
    square_sum, cross_sum = head_sum(
        jnp.sum(attended * attended, axis=1), jnp.sum(norm_gain * grad_wide * attended, axis=1)
    )
    inv_rms = lax.rsqrt(square_sum / width_all + EPSILON)
    normed = (attended * inv_rms[:, None] * norm_gain).astype(jnp.bfloat16)
    grad_attn = (
        inv_rms[:, None] * norm_gain * grad_wide
        - attended * (inv_rms * inv_rms * inv_rms * cross_sum / width_all)[:, None]
    )
    grad_weight = grad_attn.astype(jnp.bfloat16).reshape(token_count, head_count, HD)
    first_end = dial_end[0]
    keep_first = position < first_end
    wide_shape = jax.ShapeDtypeStruct(queries.shape, jnp.float32)
    grad_flat = grad_weight.reshape(queries.shape)
    returned, *local = scan_window(
        None, first_end > block_begin + token_count, -1, 1,
        functools.partial(backward_local, score_scale),
        (queries, key_rows, value_rows, grad_flat, dial_start.reshape(1, token_count), carried),
        (wide_shape,) * 3,
        prologue=lambda refs, out: forward_element(*refs, out, below=True),
        prologue_inputs=((first_end - block_begin).reshape(1), queries, grad_flat),
        shape=(head_count, HD, HD),
    )
    query_grad, key_grad, value_grad = gradients(
        score_scale, queries, key_rows, value_rows, grad_flat,
        dial_start, dial_end, carried, returned, local,
    )
    return (normed, query_grad, key_grad, value_grad)


def solution(mesh):
    placed = (
        P("seq", "head"),
        P("seq", "head"),
        P("seq", "head"),
        P("seq", "head"),
        P("head"),
        P("seq"),
        P("seq"),
    )
    return jax.shard_map(
        shards,
        mesh=mesh,
        in_specs=placed,
        out_specs=(P("seq", "head"), P("seq", "head"), P("seq", "head"), P("seq", "head")),
        check_vma=False,
    )
```
